128 devices in a mesh: gx: 16 (over z_lo, x, core), gy: 8 (over y, z_hi).
Axes of the slice: x: 4, y: 4, z: 4 (z_hi: 2, z_lo: 2; z = z_hi * 2 + z_lo), core: 2. Of those that a mesh axis runs over, the one named last changes fastest.
Arguments:
- disp_prev: float32 [3, 256, 128, 384], P(None, 'gx', 'gy'), may hold values from -6 to 6
- disp_now: float32 [3, 256, 128, 384], P(None, 'gx', 'gy'), may hold values from -6 to 6
- buoyancy: float32 [256, 128, 384], P('gx', 'gy'), may hold values from 0.4 to 1
- shear_mod: float32 [256, 128, 384], P('gx', 'gy'), may hold values from 0.3 to 1
- lame_first: float32 [256, 128, 384], P('gx', 'gy'), may hold values from 0.3 to 1
- foot_offset: int32 [16384, 2], P(('gx', 'gy')), may hold values from 0 to 8
- owner_source: int32 [16384], P(('gx', 'gy')), may hold values from 0 to 16383, as said below
- owner_count: int32 [128], P(('gx', 'gy')), may hold values from 96 to 128, as said below
- force_history: float32 [31, 64, 16384], P(None, None, ('gx', 'gy')), may hold values from -6 to 6
- participation: float32 [192, 64], replicated, may hold values from -0.4375 to 0.4375
- kernels: float32 [64, 32], replicated, may hold values from -1 to 1
Outputs:
- disp_mid: float32 [3, 256, 128, 384], P(None, 'gx', 'gy')
- disp_next: float32 [3, 256, 128, 384], P(None, 'gx', 'gy')
- responses: float32 [2, 64, 16384], P(None, None, ('gx', 'gy'))
The draws below stay inside these ranges and needn't reach their ends.
Inputs may be any that keep to these rules, and one draw needn't show every extreme that they name: `owner_source`: building slot s belongs to owner device s // 128; its first owner_count slots are live. Among the live slots of one owner at most 2 name footprints on one tile, and every owner reaches 2. Footprints cluster on a few tiles. `owner_count`: some owner holds 128.
All inputs are finite; a program needn't handle non-finite values.
Results may differ from the reference program's by a relative error of at most 0.00012.
Values sent between devices are 32-bit elements; how exact they have to be, the bound alone decides.
No kernel may reach another device: no remote copies, remote signals or barrier semaphores. Data moves between devices by JAX's collectives and lax.ppermute only.
A program may use at most 128 MiB of HBM per device.

```python
import math
import jax
import jax.numpy as jnp
from jax import lax

TILE = 16
CZ = 384
PX = 8
MODES = 64
KTAPS = 32
TILE_CAP = 128
OWN_CAP = 128
PAIR_CAP = 2
NX = 256
NY = 128
FOOT_SLOTS = 16384
BUILD_SLOTS = 16384
N_GY = 8
DEVICES = 128


def owner_plan(key):
    counts = jax.random.randint(jax.random.fold_in(key, 11), (DEVICES,), 3 * OWN_CAP // 4, OWN_CAP + 1)
    fullest = jax.random.randint(jax.random.fold_in(key, 12), (), 0, DEVICES)
    counts = jnp.where(jnp.arange(DEVICES) == fullest, OWN_CAP, counts).astype(jnp.int32)
    downtown = (jax.random.permutation(jax.random.fold_in(key, 13), DEVICES) < max(1, DEVICES // 16)).astype(jnp.int32)
    scores = jax.random.randint(jax.random.fold_in(key, 14), (DEVICES, DEVICES), 0, 1024) + 1024 * downtown[None, :]
    scores = scores * DEVICES + jnp.arange(DEVICES, dtype=jnp.int32)[None, :]
    chosen_tiles = lax.top_k(scores, OWN_CAP // PAIR_CAP)[1]
    slot_tiles = jnp.repeat(chosen_tiles, PAIR_CAP, axis=1)
    local_slot = jax.random.randint(jax.random.fold_in(key, 15), (DEVICES, OWN_CAP), 0, TILE_CAP)
    source = (slot_tiles * TILE_CAP + local_slot).reshape(-1).astype(jnp.int32)
    return (source, counts)


def draw_owner_source(key, part):
    return owner_plan(key)[0]


def draw_owner_count(key, part):
    return owner_plan(key)[1]


def place_ends(result, stream_key, smallest, top_value):
    shape = result.shape
    place = [jax.random.randint(jax.random.fold_in(stream_key, axis), (), 0, shape[axis]) for axis in range(len(shape))]
    result = result.at[tuple(place)].set(smallest)
    longest = shape.index(max(shape))
    place[longest] = (place[longest] + 1) % shape[longest]
    return result.at[tuple(place)].set(top_value)


def steps_of(own_key, dims, cuts, smallest, top_value):
    factor_of, own = 1.0, jax.random.fold_in(own_key, 6)
    for dim, shards_of in cuts:
        draws = jnp.exp(jax.random.uniform(jax.random.fold_in(own, dim), (shards_of,), jnp.float32, smallest / len(cuts), top_value / len(cuts)))
        factor_of = factor_of * jnp.repeat(draws, dims[dim] // shards_of).reshape([-1 if axis == dim else 1 for axis in range(len(dims))])
    return factor_of


def normal_values(key, shape, scale, reach, pieces=(), kind=jnp.bfloat16):
    factor_of = steps_of(key, shape, pieces, -0.22, 0.18) if pieces else 1.0
    entries = jax.random.normal(key, shape, jnp.float32) * scale * factor_of
    return jnp.minimum(jnp.maximum(entries, -reach), reach).astype(kind)


def setup_inputs(seed: int = 0) -> dict:
    seeds = jax.random.split(jax.random.key(seed), 12)
    return {
        "disp_prev": normal_values(seeds[0], (3, NX, NY, CZ), 1.0, 6.0, ((1, 16), (2, 8)), jnp.float32),
        "disp_now": normal_values(seeds[1], (3, NX, NY, CZ), 1.0, 6.0, ((1, 16), (2, 8)), jnp.float32),
        "buoyancy": jnp.clip(jnp.exp(math.log(1.0) - 0.9162907 * jax.random.uniform(seeds[2], (NX, NY, CZ), jnp.float32) ** steps_of(seeds[2], (NX, NY, CZ), ((0, 16), (1, 8)), -0.2, 0.2)), 0.4, 1.0),
        "shear_mod": jnp.clip(jnp.exp(math.log(1.0) - 1.2039728 * jax.random.uniform(seeds[3], (NX, NY, CZ), jnp.float32) ** steps_of(seeds[3], (NX, NY, CZ), ((0, 16), (1, 8)), -0.2, 0.2)), 0.3, 1.0),
        "lame_first": jnp.clip(jnp.exp(math.log(1.0) - 1.2039728 * jax.random.uniform(seeds[4], (NX, NY, CZ), jnp.float32) ** steps_of(seeds[4], (NX, NY, CZ), ((0, 16), (1, 8)), -0.2, 0.2)), 0.3, 1.0),
        "foot_offset": place_ends(jax.random.randint(seeds[5], (FOOT_SLOTS, 2), 0, TILE - PX + 1), jax.random.fold_in(seeds[5], 1), 0, TILE - PX).astype(jnp.int32),
        "owner_source": draw_owner_source(jax.random.fold_in(seeds[11], 71), 0),
        "owner_count": draw_owner_count(jax.random.fold_in(seeds[11], 71), 0),
        "force_history": normal_values(seeds[8], (KTAPS - 1, MODES, BUILD_SLOTS), 1.0, 6.0, ((2, 128),), jnp.float32),
        "participation": normal_values(seeds[9], (3 * PX * PX, MODES), (3 * PX * PX) ** -0.5, 0.4375, (), jnp.float32),
        "kernels": normal_values(seeds[10], (MODES, KTAPS), KTAPS ** -0.5, 1.0, (), jnp.float32),
    }


second_terms = ((0, -1.0 / 12.0), (1, 16.0 / 12.0), (2, -30.0 / 12.0), (3, 16.0 / 12.0), (4, -1.0 / 12.0))
first_terms = ((0, 1.0 / 12.0), (1, -8.0 / 12.0), (3, 8.0 / 12.0), (4, -1.0 / 12.0))
time_scale = 0.09


def stencil_along(padded, which_axis, terms):
    length = padded.shape[which_axis] - 4
    summed = jnp.zeros_like(lax.slice_in_dim(padded, 0, length, axis=which_axis))
    for offset_index, weight in terms:
        summed = summed + weight * lax.slice_in_dim(padded, offset_index, offset_index + length, axis=which_axis)
    return summed


def strip_rim(padded, which_axis):
    return lax.slice_in_dim(padded, 2, padded.shape[which_axis] - 2, axis=which_axis)


def inner_part(array, keep_axes):
    for which_axis in range(3):
        if which_axis not in keep_axes:
            array = strip_rim(array, which_axis)
    return array


def acceleration(padded, coefficients):
    shear = coefficients[1]
    lame = coefficients[2]
    outputs = []
    for component in range(3):
        second_parts = [inner_part(stencil_along(padded[component], which_axis, second_terms), (which_axis,)) for which_axis in range(3)]
        laplace = second_parts[0] + second_parts[1] + second_parts[2]
        mixed = second_parts[component]
        for other_axis in range(3):
            if other_axis != component:
                inner_diff = stencil_along(padded[other_axis], other_axis, first_terms)
                outer_diff = stencil_along(inner_diff, component, first_terms)
                mixed = mixed + inner_part(outer_diff, (component, other_axis))
        outputs.append(shear * laplace + (lame + shear) * mixed)
    return jnp.stack(outputs)


def advance(padded, previous, coefficients):
    current = padded[:, 2:-2, 2:-2, 2:-2]
    return 2.0 * current - previous + time_scale * coefficients[0] * acceleration(padded, coefficients)


def convolve(history, forces, kernels):
    sequence = jnp.concatenate([history, forces], axis=0)
    flipped = kernels[:, ::-1]
    results = [jnp.einsum('mk,kms->ms', flipped, sequence[new_step:new_step + KTAPS], precision=lax.Precision.HIGHEST) for new_step in range(2)]
    return jnp.stack(results)


def reference(disp_prev, disp_now, buoyancy, shear_mod, lame_first, foot_offset, owner_source, owner_count, force_history, participation, kernels):
    coefficients = jnp.stack([buoyancy, shear_mod, lame_first])
    margins = ((0, 0), (2, 2), (2, 2), (2, 2))
    disp_mid = advance(jnp.pad(disp_now, margins), disp_prev, coefficients)
    disp_next = advance(jnp.pad(disp_mid, margins), disp_now, coefficients)
    surface = jnp.stack([disp_mid[:, :, :, 0], disp_next[:, :, :, 0]])
    tile_of = owner_source // TILE_CAP
    offsets = foot_offset[owner_source]
    start_east = ((tile_of // N_GY) * TILE + offsets[:, 0]).astype(jnp.int32)
    start_north = ((tile_of % N_GY) * TILE + offsets[:, 1]).astype(jnp.int32)
    zero_index = jnp.zeros((), jnp.int32)

    def cut_patch(east, north):
        return lax.dynamic_slice(surface, (zero_index, zero_index, east, north), (2, 3, PX, PX))

    patches = jax.vmap(cut_patch)(start_east, start_north).reshape(owner_source.shape[0], 2, 3 * PX * PX)
    forces = jnp.einsum('snj,jm->nms', patches, participation, precision=lax.Precision.HIGHEST)
    responses = convolve(force_history, forces, kernels)
    slot_ids = jnp.arange(owner_source.shape[0], dtype=jnp.int32) % OWN_CAP
    is_live = slot_ids < jnp.repeat(owner_count, OWN_CAP)
    responses = jnp.where(is_live[None, None, :], responses, jnp.zeros((), jnp.float32))
    return disp_mid, disp_next, responses
```

```python
import jax
import jax.numpy as jnp
from jax import lax
from jax.experimental import pallas as pl
from jax.experimental.pallas import tpu as pltpu
from jax.sharding import PartitionSpec as P

PX = 8
SIDE = 16
LANES = 128
HIGHEST = lax.Precision.HIGHEST
F32 = jnp.float32

VMEM_SPEC = pl.BlockSpec(memory_space=pltpu.VMEM)
SMEM_SPEC = pl.BlockSpec(memory_space=pltpu.SMEM)


def iota(shape, axis):
    return lax.broadcasted_iota(jnp.int32, shape, axis)


def z_shifts(block):
    columns = [block[:, k * LANES : (k + 1) * LANES] for k in range(block.shape[1] // LANES)]
    count = len(columns)
    lane = iota(columns[0].shape, 1)
    zero = jnp.zeros_like(columns[0])
    shifted = {}
    for s in (1, -1, 2, -2):
        rolled = [pltpu.roll(c, (-s) % LANES, axis=1) for c in columns]
        picked = []
        for k in range(count):
            if s > 0:
                other = rolled[k + 1] if k + 1 < count else zero
                picked.append(jnp.where(lane < LANES - s, rolled[k], other))
            else:
                other = rolled[k - 1] if k > 0 else zero
                picked.append(jnp.where(lane >= -s, rolled[k], other))
        shifted[s] = jnp.concatenate(picked, axis=1)
    return shifted


def first_of(a1, b1, a2, b2):
    return (a1 - b1) - (a2 - b2) * 0.125


def second_of(a1, b1, a2, b2):
    return (a1 + b1) - (a2 + b2) * 0.0625


def z_first(block):
    t = z_shifts(block)
    return first_of(t[1], t[-1], t[2], t[-2])


def stencil_kernel(v, xlo, xhi, ylo, yhi, prev, buoy, mu, lam, out, vp, byx, syz):
    rows = v.shape[1]
    vp[:, 2 : rows + 2, 8:24, :] = v[...]
    vp[:, 0:2, 8:24, :] = xlo[...]
    vp[:, rows + 2 : rows + 4, 8:24, :] = xhi[...]
    vp[:, :, 6:8, :] = ylo[...]
    vp[:, :, 24:26, :] = yhi[...]

    def y_four(c, r, h):
        return [vp[c, r, pl.ds(8 + 8 * h + d, 8), :] for d in (1, -1, 2, -2)]

    def inner(r, carry):
        for h in range(2):
            here = pl.ds(8 * h, 8)
            byx[r, here, :] = first_of(*y_four(0, r, h))
            syz[r, here, :] = first_of(*y_four(1, r, h)) + z_first(vp[2, r, pl.ds(8 + 8 * h, 8), :])
        return carry

    lax.fori_loop(0, rows + 4, inner, 0)

    def outer(i, carry):
        r = i + 2
        for h in range(2):
            here = pl.ds(8 * h, 8)
            core = pl.ds(8 + 8 * h, 8)

            def x_four(ref):
                return [ref[r + d, here, :] for d in (1, -1, 2, -2)]

            def vx_four(c):
                return [vp[c, r + d, core, :] for d in (1, -1, 2, -2)]

            shear = mu[i, here, :]
            both = lam[i, here, :] + shear
            scale = buoy[i, here, :] * 0.12
            x0 = vx_four(0)
            dxx = first_of(*x0)
            y1 = y_four(1, r, h)
            y2 = y_four(2, r, h)
            mixed = [
                first_of(*x_four(syz)),
                first_of(*x_four(byx)) + z_first(first_of(*y2)),
                z_first(dxx + first_of(*y1)),
            ]
            for c in range(3):
                centre = vp[c, r, core, :]
                t = z_shifts(centre)
                q = [
                    second_of(*(x0 if c == 0 else vx_four(c))),
                    second_of(*(y1 if c == 1 else y2 if c == 2 else y_four(c, r, h))),
                    second_of(t[1], t[-1], t[2], t[-2]),
                ]
                laplace = (q[0] + q[1]) + (q[2] - centre * 5.625)
                along = (q[c] - centre * 1.875) + mixed[c] * (1.0 / 3.0)
                total = shear * laplace + both * along
                out[c, i, here, :] = (2.0 * centre - prev[c, i, here, :]) + scale * total
        return carry

    lax.fori_loop(0, rows, outer, 0)


def stencil(v, halos, prev, buoy, mu, lam):
    three, rows, cols, depth = v.shape
    return pl.pallas_call(
        stencil_kernel,
        out_shape=jax.ShapeDtypeStruct(v.shape, F32),
        in_specs=[VMEM_SPEC] * 9,
        out_specs=VMEM_SPEC,
        scratch_shapes=[
            pltpu.VMEM((3, rows + 4, 32, depth), F32),
            pltpu.VMEM((rows + 4, cols, depth), F32),
            pltpu.VMEM((rows + 4, cols, depth), F32),
        ],
        name="stencil",
    )(v, *halos, prev, buoy, mu, lam)


def request_kernel(source, count, req, pos):
    shape = (LANES, LANES)
    src = source[...]
    slot = iota((1, LANES), 1)
    live = slot < count[0]
    tile = src // LANES
    local = (src % LANES).astype(F32)
    mine = jnp.where((iota(shape, 0) == tile) & live, 1.0, 0.0)
    earlier = jnp.where(iota(shape, 0) < iota(shape, 1), 1.0, 0.0)
    before = jnp.dot(mine, earlier, preferred_element_type=F32)
    rank = jnp.sum(before * mine, axis=0, keepdims=True)
    wanted = mine * local
    lane = iota(shape, 1)
    first = jnp.sum(jnp.where(rank < 0.5, wanted, 0.0), axis=1, keepdims=True)
    second = jnp.sum(jnp.where(rank > 0.5, wanted, 0.0), axis=1, keepdims=True)
    req[...] = jnp.where(lane == 0, first, jnp.where(lane == 1, second, 0.0)).astype(jnp.int32)
    pos[...] = jnp.where(live, tile * 2 + rank.astype(jnp.int32), -1)


def make_requests(source, count):
    return pl.pallas_call(
        request_kernel,
        out_shape=(
            jax.ShapeDtypeStruct((LANES, LANES), jnp.int32),
            jax.ShapeDtypeStruct((1, LANES), jnp.int32),
        ),
        in_specs=[VMEM_SPEC, SMEM_SPEC],
        out_specs=(VMEM_SPEC, VMEM_SPEC),
        name="requests",
    )(source.reshape(1, LANES), count)


def history_kernel(hist, ker, out):
    k = ker[...]
    steps = hist.shape[0]
    half = hist.shape[1] // 2
    for part in range(2):
        rows = pl.ds(part * half, half)
        kp = k[part * half : (part + 1) * half]
        first = jnp.zeros((half, LANES), F32)
        second = jnp.zeros((half, LANES), F32)
        for h in range(steps):
            past = hist[h, rows, :]
            first = first + kp[:, steps - h : steps - h + 1] * past
            if h > 0:
                second = second + kp[:, steps + 1 - h : steps + 2 - h] * past
        out[0, rows, :] = first
        out[1, rows, :] = second


def history_part(hist, ker):
    return pl.pallas_call(
        history_kernel,
        out_shape=jax.ShapeDtypeStruct((2,) + hist.shape[1:], F32),
        in_specs=[VMEM_SPEC, VMEM_SPEC],
        out_specs=VMEM_SPEC,
        name="history",
    )(hist, ker)


def answer_kernel(mid, nxt, asked, offset, part, out, weights, windows):
    cells = SIDE * SIDE
    flat = jnp.zeros((8, cells), F32)
    for n, field in enumerate((mid, nxt)):
        for c in range(3):
            pick = jnp.where((iota((8, LANES), 0) == n * 3 + c) & (iota((8, LANES), 1) == 0), 1.0, 0.0)
            flat = flat + lax.dot_general(
                pick,
                field[c].reshape(cells, LANES),
                (((1,), (1,)), ((), ())),
                precision=HIGHEST,
                preferred_element_type=F32,
            )
    windows[...] = jnp.zeros_like(windows)
    span = SIDE - PX + 1
    for ox in range(span):
        for oy in range(span):
            shift = ox * SIDE + oy
            moved = pltpu.roll(flat, (cells - shift) % cells, axis=1) if shift else flat
            windows[pl.ds((ox * span + oy) * 8, 8), :] = moved[:, :LANES]
    weights[...] = jnp.zeros_like(weights)
    modes = part.shape[1]
    for c in range(3):
        for i in range(PX):
            block = part[pl.ds((c * PX + i) * PX, PX), :]
            block = jnp.concatenate([block, block], axis=1)
            low = iota(block.shape, 1) < modes
            weights[c, pl.ds(i * SIDE, PX), :] = jnp.where(low, block, 0.0)
            weights[3 + c, pl.ds(i * SIDE, PX), :] = jnp.where(low, 0.0, block)
    table = jnp.zeros((LANES, LANES), F32)
    for nc in range(6):
        table = table + jnp.dot(
            windows[pl.ds(nc, LANES, stride=8), :], weights[nc], precision=HIGHEST, preferred_element_type=F32
        )
    lane = iota((LANES, LANES), 1)
    where = offset[:, 0:1] * span + offset[:, 1:2]
    by_slot = jnp.dot(
        jnp.where(lane == where, 1.0, 0.0), table, precision=HIGHEST, preferred_element_type=F32
    )
    for r in range(2):
        chosen = jnp.where(lane == asked[:, r : r + 1], 1.0, 0.0)
        out[pl.ds(r, LANES, stride=2), :] = jnp.dot(
            chosen, by_slot, precision=HIGHEST, preferred_element_type=F32
        )


def make_answers(mid, nxt, asked, offset, part):
    surface_spec = pl.BlockSpec((3, SIDE, SIDE, LANES), lambda i: (0, 0, 0, 0))
    whole = lambda a: pl.BlockSpec(a.shape, lambda i: (0,) * a.ndim)
    return pl.pallas_call(
        answer_kernel,
        grid=(1,),
        out_shape=jax.ShapeDtypeStruct((2 * LANES, LANES), F32),
        in_specs=[surface_spec, surface_spec, whole(asked), whole(offset), whole(part)],
        out_specs=pl.BlockSpec((2 * LANES, LANES), lambda i: (0, 0)),
        scratch_shapes=[pltpu.VMEM((6, LANES, LANES), F32), pltpu.VMEM((8 * LANES, LANES), F32)],
        name="answers",
    )(mid, nxt, asked, offset, part)


def response_kernel(ans, pos, base, ker, out):
    at = pos[...]
    chosen = jnp.where(iota((2 * LANES, LANES), 0) == at, 1.0, 0.0)
    forces = lax.dot_general(
        ans[...], chosen, (((0,), (0,)), ((), ())), precision=HIGHEST, preferred_element_type=F32
    )
    k = ker[...]
    modes = k.shape[0]
    early, late = forces[:modes], forces[modes:]
    live = at >= 0
    out[0] = jnp.where(live, base[0] + k[:, 0:1] * early, 0.0)
    out[1] = jnp.where(live, base[1] + k[:, 0:1] * late + k[:, 1:2] * early, 0.0)


def make_responses(ans, pos, base, ker):
    return pl.pallas_call(
        response_kernel,
        out_shape=jax.ShapeDtypeStruct(base.shape, F32),
        in_specs=[VMEM_SPEC] * 4,
        out_specs=VMEM_SPEC,
        name="responses",
    )(ans, pos, base, ker)


def neighbours(axis, low, high):
    size = lax.axis_size(axis)
    up = [(i, i + 1) for i in range(size - 1)]
    down = [(j, i) for i, j in up]
    return lax.ppermute(high, axis, up), lax.ppermute(low, axis, down)


def rims(field):
    xlo, xhi = neighbours("gx", field[:, :2], field[:, -2:])
    low = jnp.concatenate([xlo[:, :, :2], field[:, :, :2], xhi[:, :, :2]], axis=1)
    high = jnp.concatenate([xlo[:, :, -2:], field[:, :, -2:], xhi[:, :, -2:]], axis=1)
    ylo, yhi = neighbours("gy", low, high)
    return xlo, xhi, ylo, yhi


def per_device(
    disp_prev,
    disp_now,
    buoyancy,
    shear_mod,
    lame_first,
    foot_offset,
    owner_source,
    owner_count,
    force_history,
    participation,
    kernels,
):
    axes = ("gx", "gy")
    req, pos = make_requests(owner_source, owner_count)
    asked = lax.all_to_all(req.reshape(LANES, 1, LANES), axes, split_axis=0, concat_axis=0, tiled=True)
    base = history_part(force_history, kernels)
    disp_mid = stencil(disp_now, rims(disp_now), disp_prev, buoyancy, shear_mod, lame_first)
    disp_next = stencil(disp_mid, rims(disp_mid), disp_now, buoyancy, shear_mod, lame_first)
    ans = make_answers(disp_mid, disp_next, asked.reshape(LANES, LANES), foot_offset, participation)
    back = lax.all_to_all(ans.reshape(LANES, 2, LANES), axes, split_axis=0, concat_axis=0, tiled=True)
    responses = make_responses(back.reshape(2 * LANES, LANES), pos, base, kernels)
    return disp_mid, disp_next, responses


def solution(mesh):
    return jax.shard_map(
        per_device,
        mesh=mesh,
        in_specs=(
            P(None, "gx", "gy", None),
            P(None, "gx", "gy", None),
            P("gx", "gy", None),
            P("gx", "gy", None),
            P("gx", "gy", None),
            P(("gx", "gy"), None),
            P(("gx", "gy")),
            P(("gx", "gy")),
            P(None, None, ("gx", "gy")),
            P(),
            P(),
        ),
        out_specs=(
            P(None, "gx", "gy", None),
            P(None, "gx", "gy", None),
            P(None, None, ("gx", "gy")),
        ),
        check_vma=False,
    )
```

```python
import jax
import jax.numpy as jnp
from jax import lax
from jax.experimental import pallas as pl
from jax.experimental.pallas import tpu as pltpu
from jax.sharding import PartitionSpec as P

PX = 8
SIDE = 16
LANES = 128
HIGHEST = lax.Precision.HIGHEST
F32 = jnp.float32
VMEM_BYTES = 16 << 20

VMEM_SPEC = pl.BlockSpec(memory_space=pltpu.VMEM)
HBM_SPEC = pl.BlockSpec(memory_space=pltpu.HBM)
SMEM_SPEC = pl.BlockSpec(memory_space=pltpu.SMEM)


def iota(shape, axis):
    return lax.broadcasted_iota(jnp.int32, shape, axis)


def in_vmem(array):
    return pltpu.with_memory_space_constraint(array, pltpu.VMEM)


def in_hbm(array):
    return pltpu.with_memory_space_constraint(array, pltpu.HBM)


def parity(axis):
    return lax.axis_index(axis) % 2


def first_of(a1, b1, a2, b2):
    return (a1 - b1) - (a2 - b2) * 0.125


def second_of(a1, b1, a2, b2):
    return (a1 + b1) - (a2 + b2) * 0.0625


def z_four(below, columns, above):
    lane = iota(columns[0].shape, 1)
    zero = jnp.zeros_like(columns[0])
    count = len(columns)
    out = [[] for _ in columns]
    for s in (1, -1, 2, -2):
        turned = [pltpu.roll(c, (-s) % LANES, axis=1) for c in columns]
        if s > 0:
            turned.append(zero if above is None else pltpu.roll(above, LANES - s, axis=1))
        else:
            turned.insert(0, zero if below is None else pltpu.roll(below, -s, axis=1))
        for k in range(count):
            if s > 0:
                out[k].append(jnp.where(lane < LANES - s, turned[k], turned[k + 1]))
            else:
                out[k].append(jnp.where(lane >= -s, turned[k + 1], turned[k]))
    return out


def z_first(below, columns, above):
    return [first_of(*four) for four in z_four(below, columns, above)]


def fill_rims(vp, xa, xb, ya, yb):
    rows = vp.shape[1] - 4
    odd_x, odd_y = parity("gx"), parity("gy")
    vp[:, pl.ds((rows + 2) * (1 - odd_x), 2), 8:24, :] = xa[...]
    vp[:, pl.ds((rows + 2) * odd_x, 2), 8:24, :] = xb[...]

    @pl.when(odd_y == 0)
    def _():
        vp[:, :, 6:8, :] = yb[...]
        vp[:, :, 24:26, :] = ya[...]

    @pl.when(odd_y == 1)
    def _():
        vp[:, :, 6:8, :] = ya[...]
        vp[:, :, 24:26, :] = yb[...]


def step_columns(vp, prev, buoy, mu, lam, out, byx, syz, first, last, ready, done):
    rows = vp.shape[1] - 4
    total = vp.shape[3] // LANES
    span = range(first, last)
    lanes = lambda k: pl.ds(k * LANES, LANES)

    def y_four(c, r, h, k):
        return [vp[c, r, pl.ds(8 + 8 * h + d, 8), lanes(k)] for d in (1, -1, 2, -2)]

    def ends(get):
        below = get(first - 1) if first > 0 else None
        above = get(last) if last < total else None
        return below, [get(k) for k in span], above

    def inner(r, carry):
        for h in range(2):
            here = pl.ds(8 * h, 8)
            core = pl.ds(8 + 8 * h, 8)
            dz = z_first(*ends(lambda k: vp[2, r, core, lanes(k)]))
            for n, k in enumerate(span):
                byx[r, here, lanes(k - first)] = first_of(*y_four(0, r, h, k))
                syz[r, here, lanes(k - first)] = first_of(*y_four(1, r, h, k)) + dz[n]
        return carry

    lax.fori_loop(0, rows + 4, inner, 0)

    def outer(i, carry):
        r = i + 2
        for h in range(2):
            here = pl.ds(8 * h, 8)
            core = pl.ds(8 + 8 * h, 8)

            def x_four(c, k):
                return [vp[c, r + d, core, lanes(k)] for d in (1, -1, 2, -2)]

            def derived(ref, k):
                return first_of(*[ref[r + d, here, lanes(k - first)] for d in (1, -1, 2, -2)])

            yz = z_first(*ends(lambda k: first_of(*y_four(2, r, h, k))))
            xy = z_first(*ends(lambda k: first_of(*x_four(0, k)) + first_of(*y_four(1, r, h, k))))
            along_z = [z_four(*ends(lambda k: vp[c, r, core, lanes(k)])) for c in range(3)]
            for n, k in enumerate(span):
                shear = mu[i, here, lanes(k - first)]
                both = lam[i, here, lanes(k - first)] + shear
                scale = buoy[i, here, lanes(k - first)] * 0.12
                mixed = [derived(syz, k), derived(byx, k) + yz[n], xy[n]]
                for c in range(3):
                    centre = vp[c, r, core, lanes(k)]
                    q = [second_of(*x_four(c, k)), second_of(*y_four(c, r, h, k)), second_of(*along_z[c][n])]
                    laplace = (q[0] + q[1]) + (q[2] - centre * 5.625)
                    along = (q[c] - centre * 1.875) + mixed[c] * (1.0 / 3.0)
                    update = shear * laplace + both * along
                    out[c, i, here, lanes(k - first)] = (
                        2.0 * centre - prev[c, i, here, lanes(k - first)]
                    ) + scale * update
        return carry

    ready()
    for start in range(0, rows, rows // 4):
        lax.fori_loop(start, start + rows // 4, outer, 0)
        done(start, rows // 4)


def surface_rows(field, first):
    cells = SIDE * SIDE
    flat = jnp.zeros((8, cells), F32)
    for c in range(3):
        pick = jnp.where((iota((8, LANES), 0) == first + c) & (iota((8, LANES), 1) == 0), 1.0, 0.0)
        flat = flat + lax.dot_general(
            pick,
            field[c, :, :, 0:LANES].reshape(cells, LANES),
            (((1,), (1,)), ((), ())),
            precision=HIGHEST,
            preferred_element_type=F32,
        )
    return flat


def started(pairs, sems):
    copies = [pltpu.make_async_copy(src, dst, sems.at[n]) for n, (src, dst) in enumerate(pairs)]
    for copy in copies:
        copy.start()
    return copies


def wait_all(copies):
    for copy in copies:
        copy.wait()


def first_step_kernel(
    v, prev, buoy, mu, lam, xa, xb, ya, yb, mid, out, nxa, nxb, nlo, nhi, top, vp, pv, bv, mv, lv, byx, syz, sems
):
    rows = v.shape[1]
    copies = started(
        [(v, vp.at[:, 2 : rows + 2, 8:24, :]), (prev, pv), (buoy, bv), (mu, mv), (lam, lv)], sems
    )
    fill_rims(vp, xa, xb, ya, yb)
    copies[0].wait()
    stores = []

    def done(row, count):
        part = (slice(None), pl.ds(row, count))
        stores.extend(started([(out.at[part], mid.at[part])], sems.at[pl.ds(5 + len(stores), 1)]))

    step_columns(
        vp, pv, bv, mv, lv, out, byx, syz, 0, v.shape[3] // LANES, lambda: wait_all(copies[1:]), done
    )
    odd_x = parity("gx")
    nxa[...] = out[:, pl.ds((rows - 2) * (1 - odd_x), 2), :, :]
    nxb[...] = out[:, pl.ds((rows - 2) * odd_x, 2), :, :]
    nlo[...] = out[:, :, 0:2, :]
    nhi[...] = out[:, :, 14:16, :]
    top[...] = surface_rows(out, 0)
    wait_all(stores)


def first_step(v, halos, prev, buoy, mu, lam):
    three, rows, cols, depth = v.shape
    whole = pltpu.VMEM(v.shape, F32)
    one = pltpu.VMEM((rows, cols, depth), F32)
    return pl.pallas_call(
        first_step_kernel,
        out_shape=(
            pltpu.HBM(v.shape, F32),
            whole,
            pltpu.VMEM((3, 2, cols, depth), F32),
            pltpu.VMEM((3, 2, cols, depth), F32),
            pltpu.VMEM((3, rows, 2, depth), F32),
            pltpu.VMEM((3, rows, 2, depth), F32),
            pltpu.VMEM((8, SIDE * SIDE), F32),
        ),
        in_specs=[VMEM_SPEC] + [HBM_SPEC] * 4 + [VMEM_SPEC] * 4,
        out_specs=(HBM_SPEC,) + (VMEM_SPEC,) * 6,
        scratch_shapes=[
            pltpu.VMEM((3, rows + 4, 32, depth), F32),
            whole,
            one,
            one,
            one,
            pltpu.VMEM((rows + 4, cols, depth), F32),
            pltpu.VMEM((rows + 4, cols, depth), F32),
            pltpu.SemaphoreType.DMA((9,)),
        ],
        compiler_params=pltpu.CompilerParams(vmem_limit_bytes=VMEM_BYTES),
        name="first_step",
    )(v, prev, buoy, mu, lam, *halos)


def near_step_kernel(
    prev, buoy, mu, lam, v, xa, xb, ya, yb, top, asked, offset, part,
    nxt, padded, ans, vp, pv, bv, mv, lv, near, byx, syz, windows, sems,
):
    rows = v.shape[1]
    column = pl.ds(0, LANES)
    copies = started(
        [(prev.at[:, :, :, column], pv)]
        + [(full.at[:, :, column], own) for full, own in ((buoy, bv), (mu, mv), (lam, lv))],
        sems,
    )
    fill_rims(vp, xa, xb, ya, yb)
    vp[:, 2 : rows + 2, 8:24, :] = v[...]
    stores = started([(vp, padded)], sems.at[pl.ds(4, 1)])
    step_columns(
        vp, pv, bv, mv, lv, near, byx, syz, 0, 1, lambda: wait_all(copies), lambda row, count: None
    )
    stores += started([(near, nxt.at[:, :, :, column])], sems.at[pl.ds(5, 1)])
    cells = SIDE * SIDE
    span = SIDE - PX + 1
    modes = part.shape[0]
    flat = top[...] + surface_rows(near, 3)
    windows[...] = jnp.zeros_like(windows)
    for ox in range(span):
        for oy in range(span):
            shift = ox * SIDE + oy
            moved = pltpu.roll(flat, (cells - shift) % cells, axis=1) if shift else flat
            windows[pl.ds((ox * span + oy) * 8, 8), :] = moved[:, :LANES]
    table = []
    for n in range(2):
        total = jnp.zeros((LANES, modes), F32)
        for c in range(3):
            total = total + jnp.dot(
                windows[pl.ds(n * 3 + c, LANES, stride=8), :],
                spread(part, c),
                precision=HIGHEST,
                preferred_element_type=F32,
            )
        table.append(total)
    table = jnp.concatenate(table, axis=1)
    where = offset[0:1, :] * span + offset[1:2, :]
    by_slot = lax.dot_general(
        jnp.where(iota((LANES, LANES), 0) == where, 1.0, 0.0),
        table,
        (((0,), (0,)), ((), ())),
        precision=HIGHEST,
        preferred_element_type=F32,
    )
    lane = iota((LANES, LANES), 1)
    for r in range(2):
        chosen = jnp.where(lane == asked[:, r : r + 1], 1.0, 0.0)
        ans[pl.ds(r, LANES, stride=2), :] = jnp.dot(
            chosen, by_slot, precision=HIGHEST, preferred_element_type=F32
        )
    wait_all(stores)


def spread(part, c):
    shape = (LANES, part.shape[1])
    cell = iota(shape, 0)
    row = c * PX * PX + (cell // SIDE) * PX + cell % SIDE
    place = jnp.where((iota(shape, 1) == row) & (cell % SIDE < PX), 1.0, 0.0)
    return lax.dot_general(
        place, part[...], (((1,), (1,)), ((), ())), precision=HIGHEST, preferred_element_type=F32
    )


def near_step(v, halos, prev, buoy, mu, lam, top, asked, offset, part):
    three, rows, cols, depth = v.shape
    padded = (3, rows + 4, 32, depth)
    one = pltpu.VMEM((rows, cols, LANES), F32)
    return pl.pallas_call(
        near_step_kernel,
        out_shape=(
            pltpu.HBM(v.shape, F32),
            pltpu.HBM(padded, F32),
            jax.ShapeDtypeStruct((2 * LANES, LANES), F32),
        ),
        in_specs=[HBM_SPEC] * 4 + [VMEM_SPEC] * 9,
        out_specs=(HBM_SPEC, HBM_SPEC, VMEM_SPEC),
        scratch_shapes=[
            pltpu.VMEM(padded, F32),
            pltpu.VMEM((3, rows, cols, LANES), F32),
            one,
            one,
            one,
            pltpu.VMEM((3, rows, cols, LANES), F32),
            pltpu.VMEM((rows + 4, cols, LANES), F32),
            pltpu.VMEM((rows + 4, cols, LANES), F32),
            pltpu.VMEM((8 * LANES, LANES), F32),
            pltpu.SemaphoreType.DMA((6,)),
        ],
        compiler_params=pltpu.CompilerParams(vmem_limit_bytes=VMEM_BYTES),
        name="near_step",
    )(prev, buoy, mu, lam, v, *halos, top, asked, offset, part)


def far_step_kernel(padded, prev, buoy, mu, lam, before, nxt, vp, pv, bv, mv, lv, out, byx, syz, sems):
    count = out.shape[3]
    columns = pl.ds(LANES, count)
    copies = started(
        [(padded, vp), (prev.at[:, :, :, columns], pv)]
        + [(full.at[:, :, columns], own) for full, own in ((buoy, bv), (mu, mv), (lam, lv))],
        sems,
    )
    copies[0].wait()
    stores = []

    def done(row, number):
        src = out.at[:, pl.ds(row, number)]
        dst = nxt.at[:, pl.ds(row, number), :, columns]
        stores.extend(started([(src, dst)], sems.at[pl.ds(5 + len(stores), 1)]))

    step_columns(
        vp, pv, bv, mv, lv, out, byx, syz, 1, 1 + count // LANES, lambda: wait_all(copies[1:]), done
    )
    wait_all(stores)


def far_step(padded, nxt, prev, buoy, mu, lam):
    three, rows, cols, depth = prev.shape
    rest = depth - LANES
    one = pltpu.VMEM((rows, cols, rest), F32)
    return pl.pallas_call(
        far_step_kernel,
        out_shape=jax.ShapeDtypeStruct(prev.shape, F32),
        in_specs=[HBM_SPEC] * 6,
        out_specs=HBM_SPEC,
        input_output_aliases={5: 0},
        scratch_shapes=[
            pltpu.VMEM(padded.shape, F32),
            pltpu.VMEM((3, rows, cols, rest), F32),
            one,
            one,
            one,
            pltpu.VMEM((3, rows, cols, rest), F32),
            pltpu.VMEM((rows + 4, cols, rest), F32),
            pltpu.VMEM((rows + 4, cols, rest), F32),
            pltpu.SemaphoreType.DMA((9,)),
        ],
        compiler_params=pltpu.CompilerParams(vmem_limit_bytes=VMEM_BYTES),
        name="far_step",
    )(padded, prev, buoy, mu, lam, nxt)


def north_kernel(low, high, xa, xb, ya, yb):
    rows = low.shape[1]
    odd_x, odd_y = parity("gx"), parity("gy")
    after = pl.ds((rows + 2) * (1 - odd_x), 2)
    before = pl.ds((rows + 2) * odd_x, 2)

    def gather(out, own, edge):
        out[:, 2 : rows + 2] = own[...]
        out[:, after] = xa[:, :, edge : edge + 2, :]
        out[:, before] = xb[:, :, edge : edge + 2, :]

    top = SIDE - 2

    @pl.when(odd_y == 0)
    def _():
        gather(ya, high, top)
        gather(yb, low, 0)

    @pl.when(odd_y == 1)
    def _():
        gather(ya, low, 0)
        gather(yb, high, top)


def north_edges(low, high, xa, xb):
    three, rows, two, depth = low.shape
    out = pltpu.VMEM((3, rows + 4, 2, depth), F32)
    return pl.pallas_call(
        north_kernel,
        out_shape=(out, out),
        in_specs=[VMEM_SPEC] * 4,
        out_specs=(VMEM_SPEC, VMEM_SPEC),
        compiler_params=pltpu.CompilerParams(vmem_limit_bytes=VMEM_BYTES),
        name="north_edges",
    )(low, high, xa, xb)

def request_kernel(source, count, req, pos):
    shape = (LANES, LANES)
    src = source[...]
    slot = iota((1, LANES), 1)
    live = slot < count[0]
    tile = src // LANES
    local = (src % LANES).astype(F32)
    mine = jnp.where((iota(shape, 0) == tile) & live, 1.0, 0.0)
    earlier = jnp.where(iota(shape, 0) < iota(shape, 1), 1.0, 0.0)
    before = jnp.dot(mine, earlier, preferred_element_type=F32)
    rank = jnp.sum(before * mine, axis=0, keepdims=True)
    wanted = mine * local
    lane = iota(shape, 1)
    first = jnp.sum(jnp.where(rank < 0.5, wanted, 0.0), axis=1, keepdims=True)
    second = jnp.sum(jnp.where(rank > 0.5, wanted, 0.0), axis=1, keepdims=True)
    req[...] = jnp.where(lane == 0, first, jnp.where(lane == 1, second, 0.0)).astype(jnp.int32)
    pos[...] = jnp.where(live, tile * 2 + rank.astype(jnp.int32), -1)


def make_requests(source, count):
    return pl.pallas_call(
        request_kernel,
        out_shape=(
            jax.ShapeDtypeStruct((LANES, LANES), jnp.int32),
            jax.ShapeDtypeStruct((1, LANES), jnp.int32),
        ),
        in_specs=[VMEM_SPEC, SMEM_SPEC],
        out_specs=(VMEM_SPEC, VMEM_SPEC),
        compiler_params=pltpu.CompilerParams(vmem_limit_bytes=VMEM_BYTES),
        name="requests",
    )(source.reshape(1, LANES), count)


def columns_of(ker):
    taps = ker.shape[0]
    same = jnp.where(iota((taps, taps), 0) == iota((taps, taps), 1), 1.0, 0.0)
    return lax.dot_general(
        ker[...], same, (((0,), (0,)), ((), ())), precision=HIGHEST, preferred_element_type=F32
    )


def history_kernel(hist, ker, out):
    k = columns_of(ker)
    steps = hist.shape[0]
    half = hist.shape[1] // 2
    for part in range(2):
        rows = pl.ds(part * half, half)
        kp = k[part * half : (part + 1) * half]
        first = jnp.zeros((half, LANES), F32)
        second = jnp.zeros((half, LANES), F32)
        for h in range(steps):
            past = hist[h, rows, :]
            first = first + kp[:, steps - h : steps - h + 1] * past
            if h > 0:
                second = second + kp[:, steps + 1 - h : steps + 2 - h] * past
        out[0, rows, :] = first
        out[1, rows, :] = second


def history_part(hist, ker):
    return pl.pallas_call(
        history_kernel,
        out_shape=jax.ShapeDtypeStruct((2,) + hist.shape[1:], F32),
        in_specs=[VMEM_SPEC, VMEM_SPEC],
        out_specs=VMEM_SPEC,
        compiler_params=pltpu.CompilerParams(vmem_limit_bytes=VMEM_BYTES),
        name="history",
    )(hist, ker)


def response_kernel(ans, pos, base, ker, out):
    at = pos[...]
    chosen = jnp.where(iota((2 * LANES, LANES), 0) == at, 1.0, 0.0)
    forces = lax.dot_general(
        ans[...], chosen, (((0,), (0,)), ((), ())), precision=HIGHEST, preferred_element_type=F32
    )
    k = columns_of(ker)
    modes = k.shape[0]
    early, late = forces[:modes], forces[modes:]
    live = at >= 0
    out[0] = jnp.where(live, base[0] + k[:, 0:1] * early, 0.0)
    out[1] = jnp.where(live, base[1] + k[:, 0:1] * late + k[:, 1:2] * early, 0.0)


def make_responses(ans, pos, base, ker):
    return pl.pallas_call(
        response_kernel,
        out_shape=jax.ShapeDtypeStruct(base.shape, F32),
        in_specs=[VMEM_SPEC] * 4,
        out_specs=VMEM_SPEC,
        compiler_params=pltpu.CompilerParams(vmem_limit_bytes=VMEM_BYTES),
        name="responses",
    )(ans, pos, base, ker)


def swap(array, axis, first):
    pairs = []
    for low in range(first, lax.axis_size(axis) - 1, 2):
        pairs += [(low, low + 1), (low + 1, low)]
    return in_vmem(lax.ppermute(array, axis, pairs))


def east_swaps(xa, xb):
    return swap(xa, "gx", 0), swap(xb, "gx", 1)


def north_swaps(low, high, xa, xb):
    ya, yb = north_edges(low, high, xa, xb)
    return swap(ya, "gy", 0), swap(yb, "gy", 1)


def per_device(
    disp_prev,
    disp_now,
    buoyancy,
    shear_mod,
    lame_first,
    foot_offset,
    owner_source,
    owner_count,
    force_history,
    participation,
    kernels,
):
    axes = ("gx", "gy")
    edge = SIDE - 2
    odd_x = parity("gx")
    halo = east_swaps(
        lax.dynamic_slice_in_dim(disp_now, edge * (1 - odd_x), 2, axis=1),
        lax.dynamic_slice_in_dim(disp_now, edge * odd_x, 2, axis=1),
    )
    low, high = in_vmem(disp_now[:, :, :2]), in_vmem(disp_now[:, :, edge:])
    req, pos = make_requests(owner_source, owner_count)
    halo, low, high, req = lax.optimization_barrier((halo, low, high, req))
    halo = halo + north_swaps(low, high, *halo)
    asked = lax.all_to_all(req.reshape(LANES, 1, LANES), axes, split_axis=0, concat_axis=0, tiled=True)
    halo, asked = lax.optimization_barrier((halo, asked))
    medium = tuple(in_hbm(a) for a in (buoyancy, shear_mod, lame_first))
    disp_mid, mid, xa, xb, low, high, top = first_step(in_vmem(disp_now), halo, in_hbm(disp_prev), *medium)
    halo = east_swaps(xa, xb)
    base = history_part(force_history, kernels.T)
    halo, base = lax.optimization_barrier((halo, base))
    halo = halo + north_swaps(low, high, *halo)
    disp_next, padded, ans = near_step(
        mid, halo, in_hbm(disp_now), *medium, top, in_vmem(asked.reshape(LANES, LANES)), foot_offset.T, participation.T
    )
    back = lax.all_to_all(ans.reshape(LANES, 2, LANES), axes, split_axis=0, concat_axis=0, tiled=True)
    disp_next = far_step(in_hbm(padded), in_hbm(disp_next), in_hbm(disp_now), *medium)
    responses = make_responses(back.reshape(2 * LANES, LANES), pos, base, kernels.T)
    return disp_mid, disp_next, responses


def solution(mesh):
    return jax.shard_map(
        per_device,
        mesh=mesh,
        in_specs=(
            P(None, "gx", "gy", None),
            P(None, "gx", "gy", None),
            P("gx", "gy", None),
            P("gx", "gy", None),
            P("gx", "gy", None),
            P(("gx", "gy"), None),
            P(("gx", "gy")),
            P(("gx", "gy")),
            P(None, None, ("gx", "gy")),
            P(),
            P(),
        ),
        out_specs=(
            P(None, "gx", "gy", None),
            P(None, "gx", "gy", None),
            P(None, None, ("gx", "gy")),
        ),
        check_vma=False,
    )
```

```python
import jax
import jax.numpy as jnp
from jax import lax
from jax.experimental import pallas as pl
from jax.experimental.pallas import tpu as pltpu
from jax.sharding import PartitionSpec as P


PX = 8
SIDE = 16
LANES = 128
HIGHEST = lax.Precision.HIGHEST
F32 = jnp.float32
VMEM_BYTES = 16 << 20

VMEM_SPEC = pl.BlockSpec(memory_space=pltpu.VMEM)
HBM_SPEC = pl.BlockSpec(memory_space=pltpu.HBM)
SMEM_SPEC = pl.BlockSpec(memory_space=pltpu.SMEM)


def iota(shape, axis):
    return lax.broadcasted_iota(jnp.int32, shape, axis)


def in_vmem(array):
    return pltpu.with_memory_space_constraint(array, pltpu.VMEM)


def in_hbm(array):
    return pltpu.with_memory_space_constraint(array, pltpu.HBM)


def parity(axis):
    return lax.axis_index(axis) % 2


def first_of(a1, b1, a2, b2):
    return (a1 - b1) - (a2 - b2) * 0.125


def second_of(a1, b1, a2, b2):
    return (a1 + b1) - (a2 + b2) * 0.0625


def z_four(below, columns, above):
    lane = iota(columns[0].shape, 1)
    zero = jnp.zeros_like(columns[0])
    count = len(columns)
    out = [[] for _ in columns]
    for s in (1, -1, 2, -2):
        turned = [pltpu.roll(c, (-s) % LANES, axis=1) for c in columns]
        if s > 0:
            turned.append(zero if above is None else pltpu.roll(above, LANES - s, axis=1))
        else:
            turned.insert(0, zero if below is None else pltpu.roll(below, -s, axis=1))
        for k in range(count):
            if s > 0:
                out[k].append(jnp.where(lane < LANES - s, turned[k], turned[k + 1]))
            else:
                out[k].append(jnp.where(lane >= -s, turned[k + 1], turned[k]))
    return out


def z_first(below, columns, above):
    return [first_of(*four) for four in z_four(below, columns, above)]


def fill_rims(vp, xa, xb, ya, yb):
    rows = vp.shape[1] - 4
    odd_x, odd_y = parity("gx"), parity("gy")
    vp[:, pl.ds((rows + 2) * (1 - odd_x), 2), 8:24, :] = xa[...]
    vp[:, pl.ds((rows + 2) * odd_x, 2), 8:24, :] = xb[...]

    @pl.when(odd_y == 0)
    def _():
        vp[:, :, 6:8, :] = yb[...]
        vp[:, :, 24:26, :] = ya[...]

    @pl.when(odd_y == 1)
    def _():
        vp[:, :, 6:8, :] = ya[...]
        vp[:, :, 24:26, :] = yb[...]


def step_columns(vp, prev, buoy, mu, lam, out, byx, syz, first, last, ready, done):
    rows = vp.shape[1] - 4
    total = vp.shape[3] // LANES
    span = range(first, last)
    lanes = lambda k: pl.ds(k * LANES, LANES)

    def y_four(c, r, h, k):
        return [vp[c, r, pl.ds(8 + 8 * h + d, 8), lanes(k)] for d in (1, -1, 2, -2)]

    def ends(get):
        below = get(first - 1) if first > 0 else None
        above = get(last) if last < total else None
        return below, [get(k) for k in span], above

    def inner(r, carry):
        for h in range(2):
            here = pl.ds(8 * h, 8)
            core = pl.ds(8 + 8 * h, 8)
            dz = z_first(*ends(lambda k: vp[2, r, core, lanes(k)]))
            for n, k in enumerate(span):
                byx[r, here, lanes(k - first)] = first_of(*y_four(0, r, h, k))
                syz[r, here, lanes(k - first)] = first_of(*y_four(1, r, h, k)) + dz[n]
        return carry

    lax.fori_loop(0, rows + 4, inner, 0)

    def outer(i, carry):
        r = i + 2
        for h in range(2):
            here = pl.ds(8 * h, 8)
            core = pl.ds(8 + 8 * h, 8)

            def x_four(c, k):
                return [vp[c, r + d, core, lanes(k)] for d in (1, -1, 2, -2)]

            def derived(ref, k):
                return first_of(*[ref[r + d, here, lanes(k - first)] for d in (1, -1, 2, -2)])

            yz = z_first(*ends(lambda k: first_of(*y_four(2, r, h, k))))
            xy = z_first(*ends(lambda k: first_of(*x_four(0, k)) + first_of(*y_four(1, r, h, k))))
            along_z = [z_four(*ends(lambda k: vp[c, r, core, lanes(k)])) for c in range(3)]
            for n, k in enumerate(span):
                shear = mu[i, here, lanes(k - first)]
                both = lam[i, here, lanes(k - first)] + shear
                scale = buoy[i, here, lanes(k - first)] * 0.12
                mixed = [derived(syz, k), derived(byx, k) + yz[n], xy[n]]
                for c in range(3):
                    centre = vp[c, r, core, lanes(k)]
                    q = [second_of(*x_four(c, k)), second_of(*y_four(c, r, h, k)), second_of(*along_z[c][n])]
                    laplace = (q[0] + q[1]) + (q[2] - centre * 5.625)
                    along = (q[c] - centre * 1.875) + mixed[c] * (1.0 / 3.0)
                    update = shear * laplace + both * along
                    out[c, i, here, lanes(k - first)] = (
                        2.0 * centre - prev[c, i, here, lanes(k - first)]
                    ) + scale * update
        return carry

    ready()
    for start in range(0, rows, rows // 4):
        lax.fori_loop(start, start + rows // 4, outer, 0)
        done(start, rows // 4)


def surface_rows(field, first):
    cells = SIDE * SIDE
    flat = jnp.zeros((8, cells), F32)
    for c in range(3):
        pick = jnp.where((iota((8, LANES), 0) == first + c) & (iota((8, LANES), 1) == 0), 1.0, 0.0)
        flat = flat + lax.dot_general(
            pick,
            field[c, :, :, 0:LANES].reshape(cells, LANES),
            (((1,), (1,)), ((), ())),
            precision=HIGHEST,
            preferred_element_type=F32,
        )
    return flat


def started(pairs, sems):
    copies = [pltpu.make_async_copy(src, dst, sems.at[n]) for n, (src, dst) in enumerate(pairs)]
    for copy in copies:
        copy.start()
    return copies


def wait_all(copies):
    for copy in copies:
        copy.wait()


def first_step_kernel(
    v, prev, buoy, mu, lam, xa, xb, ya, yb, mid, out, nxa, nxb, nlo, nhi, top, vp, pv, bv, mv, lv, byx, syz, sems
):
    rows = v.shape[1]
    copies = started(
        [(v, vp.at[:, 2 : rows + 2, 8:24, :]), (prev, pv), (buoy, bv), (mu, mv), (lam, lv)], sems
    )
    fill_rims(vp, xa, xb, ya, yb)
    copies[0].wait()
    stores = []

    def done(row, count):
        part = (slice(None), pl.ds(row, count))
        stores.extend(started([(out.at[part], mid.at[part])], sems.at[pl.ds(5 + len(stores), 1)]))

    step_columns(
        vp, pv, bv, mv, lv, out, byx, syz, 0, v.shape[3] // LANES, lambda: wait_all(copies[1:]), done
    )
    odd_x = parity("gx")
    nxa[...] = out[:, pl.ds((rows - 2) * (1 - odd_x), 2), :, :]
    nxb[...] = out[:, pl.ds((rows - 2) * odd_x, 2), :, :]
    nlo[...] = out[:, :, 0:2, :]
    nhi[...] = out[:, :, 14:16, :]
    top[...] = surface_rows(out, 0)
    wait_all(stores)


def first_step(v, halos, prev, buoy, mu, lam):
    _, rows, cols, depth = v.shape
    whole = pltpu.VMEM(v.shape, F32)
    one = pltpu.VMEM((rows, cols, depth), F32)
    return pl.pallas_call(
        first_step_kernel,
        out_shape=(
            pltpu.HBM(v.shape, F32),
            whole,
            pltpu.VMEM((3, 2, cols, depth), F32),
            pltpu.VMEM((3, 2, cols, depth), F32),
            pltpu.VMEM((3, rows, 2, depth), F32),
            pltpu.VMEM((3, rows, 2, depth), F32),
            pltpu.VMEM((8, SIDE * SIDE), F32),
        ),
        in_specs=[VMEM_SPEC] + [HBM_SPEC] * 4 + [VMEM_SPEC] * 4,
        out_specs=(HBM_SPEC,) + (VMEM_SPEC,) * 6,
        scratch_shapes=[
            pltpu.VMEM((3, rows + 4, 32, depth), F32),
            whole,
            one,
            one,
            one,
            pltpu.VMEM((rows + 4, cols, depth), F32),
            pltpu.VMEM((rows + 4, cols, depth), F32),
            pltpu.SemaphoreType.DMA((9,)),
        ],
        compiler_params=pltpu.CompilerParams(vmem_limit_bytes=VMEM_BYTES),
        name="first_step",
    )(v, prev, buoy, mu, lam, *halos)


def main_step_kernel(prev, buoy, mu, lam, v, xa, xb, nxt, near, vp, pv, bv, mv, lv, out, byx, syz, sems):
    rows = v.shape[1]
    copies = started([(prev, pv), (buoy, bv), (mu, mv), (lam, lv)], sems)
    odd_x = parity("gx")
    vp[:, 2 : rows + 2, 8:24, :] = v[...]
    vp[:, pl.ds((rows + 2) * (1 - odd_x), 2), 8:24, :] = xa[...]
    vp[:, pl.ds((rows + 2) * odd_x, 2), 8:24, :] = xb[...]
    none = jnp.zeros((vp.shape[0], vp.shape[1], 2, vp.shape[3]), F32)
    vp[:, :, 6:8, :] = none
    vp[:, :, 24:26, :] = none
    stores = []
    rest = pl.ds(LANES, v.shape[3] - LANES)

    def done(row, count):
        part = pl.ds(row, count)
        near[:, part] = out[:, part, :, 0:LANES]
        stores.extend(
            started([(out.at[:, part, :, rest], nxt.at[:, part, :, rest])], sems.at[pl.ds(4 + len(stores), 1)])
        )

    step_columns(
        vp, pv, bv, mv, lv, out, byx, syz, 0, v.shape[3] // LANES, lambda: wait_all(copies), done
    )
    wait_all(stores)


def main_step(v, xa, xb, prev, buoy, mu, lam):
    _, rows, cols, depth = v.shape
    whole = pltpu.VMEM(v.shape, F32)
    one = pltpu.VMEM((rows, cols, depth), F32)
    return pl.pallas_call(
        main_step_kernel,
        out_shape=(pltpu.HBM(v.shape, F32), pltpu.VMEM((3, rows, cols, LANES), F32)),
        in_specs=[HBM_SPEC] * 4 + [VMEM_SPEC] * 3,
        out_specs=(HBM_SPEC, VMEM_SPEC),
        scratch_shapes=[
            pltpu.VMEM((3, rows + 4, 32, depth), F32),
            whole,
            one,
            one,
            one,
            whole,
            pltpu.VMEM((rows + 4, cols, depth), F32),
            pltpu.VMEM((rows + 4, cols, depth), F32),
            pltpu.SemaphoreType.DMA((8,)),
        ],
        compiler_params=pltpu.CompilerParams(vmem_limit_bytes=VMEM_BYTES),
        name="main_step",
    )(prev, buoy, mu, lam, v, xa, xb)


def fill_north(rim, ya, yb):
    odd_y = parity("gy")
    rim[:, :, 8:16, :] = jnp.zeros((rim.shape[0], rim.shape[1], 8, rim.shape[3]), F32)

    @pl.when(odd_y == 0)
    def _():
        rim[:, :, 6:8, :] = yb[...]
        rim[:, :, 16:18, :] = ya[...]

    @pl.when(odd_y == 1)
    def _():
        rim[:, :, 6:8, :] = ya[...]
        rim[:, :, 16:18, :] = yb[...]


def add_north(rim, buoy, mu, lam, out, ex, ey, first, last, ready):
    rows = rim.shape[1] - 4
    total = rim.shape[3] // LANES
    span = range(first, last)
    lanes = lambda k: pl.ds(k * LANES, LANES)
    local = lambda k: pl.ds((k - first) * LANES, LANES)
    below, above = max(first - 1, 0), min(last + 1, total)

    def y_four(c, r, k):
        return [rim[c, r, pl.ds(8 + d, 8), lanes(k)] for d in (1, -1, 2, -2)]

    def ends(get):
        return (
            get(first - 1) if first > 0 else None,
            [get(k) for k in span],
            get(last) if last < total else None,
        )

    def inner(r, carry):
        for k in range(below, above):
            ey[r, :, lanes(k)] = first_of(*y_four(1, r, k))
        for k in span:
            ex[r, :, lanes(k)] = first_of(*y_four(0, r, k))
        return carry

    lax.fori_loop(0, rows + 4, inner, 0)
    ready()

    def outer(i, carry):
        r = i + 2
        yz = z_first(*ends(lambda k: first_of(*y_four(2, r, k))))
        xy = z_first(*ends(lambda k: ey[r, :, lanes(k)]))
        low = iota((8, LANES), 0) < 4
        for n, k in enumerate(span):

            def packed(ref):
                return jnp.where(low, ref[i, 0:8, local(k)], ref[i, 8:16, local(k)])

            def derived(ref):
                return first_of(*[ref[r + d, :, lanes(k)] for d in (1, -1, 2, -2)])

            shear = packed(mu)
            both = packed(lam) + shear
            scale = packed(buoy) * 0.12
            mixed = [derived(ey), derived(ex) + yz[n], xy[n]]
            for c in range(3):
                q = second_of(*y_four(c, r, k))
                along = mixed[c] * (1.0 / 3.0)
                if c == 1:
                    along = along + q
                update = scale * (shear * q + both * along)
                out[c, i, 0:8, local(k)] = out[c, i, 0:8, local(k)] + jnp.where(low, update, 0.0)
                out[c, i, 8:16, local(k)] = out[c, i, 8:16, local(k)] + jnp.where(low, 0.0, update)
        return carry

    lax.fori_loop(0, rows, outer, 0)


def window_tables(flat, windows):
    span = SIDE - PX + 1
    halves = [flat[:, :LANES], flat[:, LANES:]]
    lane = iota((8, LANES), 1)
    windows[span * span * 8 :, :] = jnp.zeros((windows.shape[0] - span * span * 8, LANES), F32)
    for ox in range(span):
        for oy in range(span):
            half, shift = divmod(ox * SIDE + oy, LANES)
            moved = halves[half]
            if shift:
                other = pltpu.roll(halves[1], LANES - shift, axis=1) if half == 0 else jnp.zeros_like(moved)
                moved = jnp.where(lane < LANES - shift, pltpu.roll(moved, LANES - shift, axis=1), other)
            windows[pl.ds((ox * span + oy) * 8, 8), :] = moved


def corner_forces(flat, weights, windows):
    window_tables(flat, windows)
    total = jnp.zeros((LANES, weights.shape[2]), F32)
    for c in range(3):
        total = total + jnp.dot(
            windows[pl.ds(c, LANES, stride=8), :], weights[c], precision=HIGHEST, preferred_element_type=F32
        )
    return total


def spread(part, c):
    shape = (LANES, part.shape[1])
    cell = iota(shape, 0)
    row = c * PX * PX + (cell // SIDE) * PX + cell % SIDE
    place = jnp.where((iota(shape, 1) == row) & (cell % SIDE < PX), 1.0, 0.0)
    return lax.dot_general(
        place, part[...], (((1,), (1,)), ((), ())), precision=HIGHEST, preferred_element_type=F32
    )


def prepare_kernel(top, asked, offset, part, chosen, weights, early, windows):
    span = SIDE - PX + 1
    shape = (LANES, LANES)
    where = offset[0:1, :] * span + offset[1:2, :]
    corner = jnp.where(iota(shape, 0) == where, 1.0, 0.0)
    lane = iota(shape, 1)
    for r in range(2):
        slot = jnp.where(lane == asked[:, r : r + 1], 1.0, 0.0)
        chosen[pl.ds(r, LANES, stride=2), :] = lax.dot_general(
            slot, corner, (((1,), (1,)), ((), ())), preferred_element_type=F32
        )
    for c in range(3):
        weights[c] = spread(part, c)
    forces = corner_forces(top[...], weights, windows)
    early[...] = jnp.dot(chosen[...], forces, precision=HIGHEST, preferred_element_type=F32)


def prepare(top, asked, offset, part):
    modes = part.shape[0]
    return pl.pallas_call(
        prepare_kernel,
        out_shape=(
            pltpu.VMEM((2 * LANES, LANES), F32),
            pltpu.VMEM((3, LANES, modes), F32),
            pltpu.VMEM((2 * LANES, modes), F32),
        ),
        in_specs=[VMEM_SPEC] * 4,
        out_specs=(VMEM_SPEC,) * 3,
        scratch_shapes=[pltpu.VMEM((8 * LANES, LANES), F32)],
        compiler_params=pltpu.CompilerParams(vmem_limit_bytes=VMEM_BYTES),
        name="prepare",
    )(top, asked, offset, part)


def near_north_kernel(
    buoy, mu, lam, before, near, ya, yb, chosen, weights, early,
    nxt, yao, ybo, ans, rim, bv, mv, lv, out, ex, ey, windows, sems,
):
    column = pl.ds(0, LANES)
    copies = started([(full.at[:, :, column], own) for full, own in ((buoy, bv), (mu, mv), (lam, lv))], sems)
    stores = started([(ya, yao), (yb, ybo)], sems.at[pl.ds(3, 2)])
    fill_north(rim, ya, yb)
    out[...] = near[...]
    add_north(rim, bv, mv, lv, out, ex, ey, 0, 1, lambda: wait_all(copies))
    stores += started([(out, nxt.at[:, :, :, column])], sems.at[pl.ds(5, 1)])
    forces = corner_forces(surface_rows(out, 0), weights, windows)
    late = jnp.dot(chosen[...], forces, precision=HIGHEST, preferred_element_type=F32)
    ans[...] = jnp.concatenate([early[...], late], axis=1)
    wait_all(stores)


def near_north(nxt, near, ya, yb, prepared, buoy, mu, lam):
    _, rows, cols, depth = nxt.shape
    one = pltpu.VMEM((rows, cols, LANES), F32)
    rim = pltpu.HBM(ya.shape, F32)
    return pl.pallas_call(
        near_north_kernel,
        out_shape=(pltpu.HBM(nxt.shape, F32), rim, rim, jax.ShapeDtypeStruct((2 * LANES, LANES), F32)),
        in_specs=[HBM_SPEC] * 4 + [VMEM_SPEC] * 6,
        out_specs=(HBM_SPEC,) * 3 + (VMEM_SPEC,),
        input_output_aliases={3: 0},
        scratch_shapes=[
            pltpu.VMEM((3, rows + 4, 24, depth), F32),
            one,
            one,
            one,
            pltpu.VMEM((3, rows, cols, LANES), F32),
            pltpu.VMEM((rows + 4, 8, depth), F32),
            pltpu.VMEM((rows + 4, 8, depth), F32),
            pltpu.VMEM((8 * LANES, LANES), F32),
            pltpu.SemaphoreType.DMA((6,)),
        ],
        compiler_params=pltpu.CompilerParams(vmem_limit_bytes=VMEM_BYTES),
        name="near_north",
    )(buoy, mu, lam, nxt, near, ya, yb, *prepared)


def far_north_kernel(buoy, mu, lam, before, ya, yb, nxt, rim, yav, ybv, bv, mv, lv, out, ex, ey, sems):
    count = out.shape[3]
    columns = pl.ds(LANES, count)
    copies = started(
        [(ya, yav), (yb, ybv), (before.at[:, :, :, columns], out)]
        + [(full.at[:, :, columns], own) for full, own in ((buoy, bv), (mu, mv), (lam, lv))],
        sems,
    )
    wait_all(copies[:2])
    fill_north(rim, yav, ybv)
    add_north(rim, bv, mv, lv, out, ex, ey, 1, 1 + count // LANES, lambda: wait_all(copies[2:]))
    wait_all(started([(out, nxt.at[:, :, :, columns])], sems.at[pl.ds(6, 1)]))


def far_north(nxt, ya, yb, buoy, mu, lam):
    _, rows, cols, depth = nxt.shape
    rest = depth - LANES
    one = pltpu.VMEM((rows, cols, rest), F32)
    return pl.pallas_call(
        far_north_kernel,
        out_shape=jax.ShapeDtypeStruct(nxt.shape, F32),
        in_specs=[HBM_SPEC] * 6,
        out_specs=HBM_SPEC,
        input_output_aliases={3: 0},
        scratch_shapes=[
            pltpu.VMEM((3, rows + 4, 24, depth), F32),
            pltpu.VMEM(ya.shape, F32),
            pltpu.VMEM(ya.shape, F32),
            one,
            one,
            one,
            pltpu.VMEM((3, rows, cols, rest), F32),
            pltpu.VMEM((rows + 4, 8, depth), F32),
            pltpu.VMEM((rows + 4, 8, depth), F32),
            pltpu.SemaphoreType.DMA((7,)),
        ],
        compiler_params=pltpu.CompilerParams(vmem_limit_bytes=VMEM_BYTES),
        name="far_north",
    )(buoy, mu, lam, nxt, ya, yb)


def north_kernel(low, high, xa, xb, ya, yb):
    rows = low.shape[1]
    odd_x, odd_y = parity("gx"), parity("gy")
    after = pl.ds((rows + 2) * (1 - odd_x), 2)
    before = pl.ds((rows + 2) * odd_x, 2)

    def gather(out, own, edge):
        out[:, 2 : rows + 2] = own[...]
        out[:, after] = xa[:, :, edge : edge + 2, :]
        out[:, before] = xb[:, :, edge : edge + 2, :]

    top = SIDE - 2

    @pl.when(odd_y == 0)
    def _():
        gather(ya, high, top)
        gather(yb, low, 0)

    @pl.when(odd_y == 1)
    def _():
        gather(ya, low, 0)
        gather(yb, high, top)


def north_edges(low, high, xa, xb):
    _, rows, _, depth = low.shape
    out = pltpu.VMEM((3, rows + 4, 2, depth), F32)
    return pl.pallas_call(
        north_kernel,
        out_shape=(out, out),
        in_specs=[VMEM_SPEC] * 4,
        out_specs=(VMEM_SPEC, VMEM_SPEC),
        compiler_params=pltpu.CompilerParams(vmem_limit_bytes=VMEM_BYTES),
        name="north_edges",
    )(low, high, xa, xb)


def request_kernel(source, count, req, pos):
    shape = (LANES, LANES)
    src = source[...]
    slot = iota((1, LANES), 1)
    live = slot < count[0]
    tile = src // LANES
    local = (src % LANES).astype(F32)
    mine = jnp.where((iota(shape, 0) == tile) & live, 1.0, 0.0)
    earlier = jnp.where(iota(shape, 0) < iota(shape, 1), 1.0, 0.0)
    before = jnp.dot(mine, earlier, preferred_element_type=F32)
    rank = jnp.sum(before * mine, axis=0, keepdims=True)
    wanted = mine * local
    lane = iota(shape, 1)
    first = jnp.sum(jnp.where(rank < 0.5, wanted, 0.0), axis=1, keepdims=True)
    second = jnp.sum(jnp.where(rank > 0.5, wanted, 0.0), axis=1, keepdims=True)
    req[...] = jnp.where(lane == 0, first, jnp.where(lane == 1, second, 0.0)).astype(jnp.int32)
    pos[...] = jnp.where(live, tile * 2 + rank.astype(jnp.int32), -1)


def make_requests(source, count):
    return pl.pallas_call(
        request_kernel,
        out_shape=(
            jax.ShapeDtypeStruct((LANES, LANES), jnp.int32),
            jax.ShapeDtypeStruct((1, LANES), jnp.int32),
        ),
        in_specs=[VMEM_SPEC, SMEM_SPEC],
        out_specs=(VMEM_SPEC, VMEM_SPEC),
        compiler_params=pltpu.CompilerParams(vmem_limit_bytes=VMEM_BYTES),
        name="requests",
    )(source.reshape(1, LANES), count)


def columns_of(ker):
    taps = ker.shape[0]
    same = jnp.where(iota((taps, taps), 0) == iota((taps, taps), 1), 1.0, 0.0)
    return lax.dot_general(
        ker[...], same, (((0,), (0,)), ((), ())), precision=HIGHEST, preferred_element_type=F32
    )


def history_kernel(hist, ker, out):
    k = columns_of(ker)
    steps = hist.shape[0]
    half = hist.shape[1] // 2
    for part in range(2):
        rows = pl.ds(part * half, half)
        kp = k[part * half : (part + 1) * half]
        first = jnp.zeros((half, LANES), F32)
        second = jnp.zeros((half, LANES), F32)
        for h in range(steps):
            past = hist[h, rows, :]
            first = first + kp[:, steps - h : steps - h + 1] * past
            if h > 0:
                second = second + kp[:, steps + 1 - h : steps + 2 - h] * past
        out[0, rows, :] = first
        out[1, rows, :] = second


def history_part(hist, ker):
    return pl.pallas_call(
        history_kernel,
        out_shape=jax.ShapeDtypeStruct((2,) + hist.shape[1:], F32),
        in_specs=[VMEM_SPEC, VMEM_SPEC],
        out_specs=VMEM_SPEC,
        compiler_params=pltpu.CompilerParams(vmem_limit_bytes=VMEM_BYTES),
        name="history",
    )(hist, ker)


def response_kernel(ans, pos, base, ker, out):
    at = pos[...]
    chosen = jnp.where(iota((2 * LANES, LANES), 0) == at, 1.0, 0.0)
    forces = lax.dot_general(
        ans[...], chosen, (((0,), (0,)), ((), ())), precision=HIGHEST, preferred_element_type=F32
    )
    k = columns_of(ker)
    modes = k.shape[0]
    early, late = forces[:modes], forces[modes:]
    live = at >= 0
    out[0] = jnp.where(live, base[0] + k[:, 0:1] * early, 0.0)
    out[1] = jnp.where(live, base[1] + k[:, 0:1] * late + k[:, 1:2] * early, 0.0)


def make_responses(ans, pos, base, ker):
    return pl.pallas_call(
        response_kernel,
        out_shape=jax.ShapeDtypeStruct(base.shape, F32),
        in_specs=[VMEM_SPEC] * 4,
        out_specs=VMEM_SPEC,
        compiler_params=pltpu.CompilerParams(vmem_limit_bytes=VMEM_BYTES),
        name="responses",
    )(ans, pos, base, ker)


def swap(array, axis, first):
    pairs = []
    for low in range(first, lax.axis_size(axis) - 1, 2):
        pairs += [(low, low + 1), (low + 1, low)]
    return in_vmem(lax.ppermute(array, axis, pairs))


def east_swaps(xa, xb):
    return swap(xa, "gx", 0), swap(xb, "gx", 1)


def north_swaps(ya, yb):
    return swap(ya, "gy", 0), swap(yb, "gy", 1)


def per_device(
    disp_prev,
    disp_now,
    buoyancy,
    shear_mod,
    lame_first,
    foot_offset,
    owner_source,
    owner_count,
    force_history,
    participation,
    kernels,
):
    return steps(
        disp_prev,
        disp_now,
        tuple(in_hbm(a) for a in (buoyancy, shear_mod, lame_first)),
        foot_offset.T,
        owner_source,
        owner_count,
        force_history,
        participation.T,
        kernels.T,
    )


def exchange(array):
    rows = array.reshape(LANES, -1, LANES)
    out = lax.all_to_all(rows, ("gx", "gy"), split_axis=0, concat_axis=0, tiled=True)
    return out.reshape(array.shape)


def steps(prev, now, medium, offset, source, count, history, part, kernels):
    edge = SIDE - 2
    odd_x = parity("gx")
    east = east_swaps(
        lax.dynamic_slice_in_dim(now, edge * (1 - odd_x), 2, axis=1),
        lax.dynamic_slice_in_dim(now, edge * odd_x, 2, axis=1),
    )
    low, high = in_vmem(now[:, :, :2]), in_vmem(now[:, :, edge:])
    req, pos = make_requests(source, count)
    east, low, high, req = lax.optimization_barrier((east, low, high, req))
    north = north_edges(low, high, *east)
    north = north_swaps(*north)
    asked = exchange(req)
    disp_mid, mid, xa, xb, low, high, top = first_step(in_vmem(now), east + north, in_hbm(prev), *medium)
    east = east_swaps(xa, xb)
    base = history_part(history, kernels)
    prepared = prepare(top, in_vmem(asked), offset, part)
    east, base, prepared = lax.optimization_barrier((east, base, prepared))
    north = north_edges(low, high, *east)
    north = north_swaps(*north)
    rest, near = main_step(mid, *east, in_hbm(now), *medium)
    north, rest, near = lax.optimization_barrier((north, rest, near))
    disp_next, ya, yb, ans = near_north(in_hbm(rest), near, *north, prepared, *medium)
    back = exchange(ans)
    disp_next = far_north(in_hbm(disp_next), in_hbm(ya), in_hbm(yb), *medium)
    responses = make_responses(back, pos, base, kernels)
    return disp_mid, disp_next, responses


def solution(mesh):
    return jax.shard_map(
        per_device,
        mesh=mesh,
        in_specs=(
            P(None, "gx", "gy", None),
            P(None, "gx", "gy", None),
            P("gx", "gy", None),
            P("gx", "gy", None),
            P("gx", "gy", None),
            P(("gx", "gy"), None),
            P(("gx", "gy")),
            P(("gx", "gy")),
            P(None, None, ("gx", "gy")),
            P(),
            P(),
        ),
        out_specs=(
            P(None, "gx", "gy", None),
            P(None, "gx", "gy", None),
            P(None, None, ("gx", "gy")),
        ),
        check_vma=False,
    )
```

```python
import jax
import jax.numpy as jnp
from jax import lax
from jax.experimental import pallas as pl
from jax.experimental.pallas import tpu as pltpu
from jax.sharding import PartitionSpec as P


PX = 8
SIDE = 16
LANES = 128
HIGHEST = lax.Precision.HIGHEST
F32 = jnp.float32
VMEM_BYTES = 16 << 20

VMEM_SPEC = pl.BlockSpec(memory_space=pltpu.VMEM)
HBM_SPEC = pl.BlockSpec(memory_space=pltpu.HBM)
SMEM_SPEC = pl.BlockSpec(memory_space=pltpu.SMEM)


def iota(shape, axis):
    return lax.broadcasted_iota(jnp.int32, shape, axis)


def in_vmem(array):
    return pltpu.with_memory_space_constraint(array, pltpu.VMEM)


def in_hbm(array):
    return pltpu.with_memory_space_constraint(array, pltpu.HBM)


def parity(axis):
    return lax.axis_index(axis) % 2


def first_of(a1, b1, a2, b2):
    return (a1 - b1) - (a2 - b2) * 0.125


def second_of(a1, b1, a2, b2):
    return (a1 + b1) - (a2 + b2) * 0.0625


def z_four(below, columns, above):
    lane = iota(columns[0].shape, 1)
    zero = jnp.zeros_like(columns[0])
    count = len(columns)
    out = [[] for _ in columns]
    for s in (1, -1, 2, -2):
        turned = [pltpu.roll(c, (-s) % LANES, axis=1) for c in columns]
        if s > 0:
            turned.append(zero if above is None else pltpu.roll(above, LANES - s, axis=1))
        else:
            turned.insert(0, zero if below is None else pltpu.roll(below, -s, axis=1))
        for k in range(count):
            if s > 0:
                out[k].append(jnp.where(lane < LANES - s, turned[k], turned[k + 1]))
            else:
                out[k].append(jnp.where(lane >= -s, turned[k + 1], turned[k]))
    return out


def z_first(below, columns, above):
    return [first_of(*four) for four in z_four(below, columns, above)]


def step_columns(vp, prev, buoy, mu, lam, out, pack, byx, syz, first, last, ready, done):
    rows = vp.shape[1] - 4
    total = vp.shape[3] // LANES
    span = range(first, last)
    lanes = lambda k: pl.ds(k * LANES, LANES)

    def y_four(c, r, h, k):
        return [vp[c, r, pl.ds(8 + 8 * h + d, 8), lanes(k)] for d in (1, -1, 2, -2)]

    def ends(get):
        below = get(first - 1) if first > 0 else None
        above = get(last) if last < total else None
        return below, [get(k) for k in span], above

    def inner(r, carry):
        for h in range(2):
            here = pl.ds(8 * h, 8)
            core = pl.ds(8 + 8 * h, 8)
            dz = z_first(*ends(lambda k: vp[2, r, core, lanes(k)]))
            for n, k in enumerate(span):
                byx[r, here, lanes(k - first)] = first_of(*y_four(0, r, h, k))
                syz[r, here, lanes(k - first)] = first_of(*y_four(1, r, h, k)) + dz[n]
        return carry

    lax.fori_loop(0, rows + 4, inner, 0)

    def outer(i, carry):
        r = i + 2
        low = iota((8, LANES), 0) < 4
        lower = {}
        for h in range(2):
            here = pl.ds(8 * h, 8)
            core = pl.ds(8 + 8 * h, 8)

            def x_four(c, k):
                return [vp[c, r + d, core, lanes(k)] for d in (1, -1, 2, -2)]

            def derived(ref, k):
                return first_of(*[ref[r + d, here, lanes(k - first)] for d in (1, -1, 2, -2)])

            yz = z_first(*ends(lambda k: first_of(*y_four(2, r, h, k))))
            xy = z_first(*ends(lambda k: first_of(*x_four(0, k)) + first_of(*y_four(1, r, h, k))))
            along_z = [z_four(*ends(lambda k: vp[c, r, core, lanes(k)])) for c in range(3)]
            for n, k in enumerate(span):
                shear = mu[i, here, lanes(k - first)]
                both = lam[i, here, lanes(k - first)] + shear
                scale = buoy[i, here, lanes(k - first)] * 0.12
                for which, factor in enumerate((shear, both, scale)):
                    if h == 0:
                        lower[which, k] = factor
                    else:
                        pack[which, i, :, lanes(k - first)] = jnp.where(low, lower[which, k], factor)
                mixed = [derived(syz, k), derived(byx, k) + yz[n], xy[n]]
                for c in range(3):
                    centre = vp[c, r, core, lanes(k)]
                    q = [second_of(*x_four(c, k)), second_of(*y_four(c, r, h, k)), second_of(*along_z[c][n])]
                    laplace = (q[0] + q[1]) + (q[2] - centre * 5.625)
                    along = (q[c] - centre * 1.875) + mixed[c] * (1.0 / 3.0)
                    update = shear * laplace + both * along
                    out[c, i, here, lanes(k - first)] = (
                        2.0 * centre - prev[c, i, here, lanes(k - first)]
                    ) + scale * update
        return carry

    ready()
    for start in range(0, rows, rows // 4):
        lax.fori_loop(start, start + rows // 4, outer, 0)
        done(start, rows // 4)


def surface_rows(field, first):
    cells = SIDE * SIDE
    flat = jnp.zeros((8, cells), F32)
    for c in range(3):
        pick = jnp.where((iota((8, LANES), 0) == first + c) & (iota((8, LANES), 1) == 0), 1.0, 0.0)
        flat = flat + lax.dot_general(
            pick,
            field[c, :, :, 0:LANES].reshape(cells, LANES),
            (((1,), (1,)), ((), ())),
            precision=HIGHEST,
            preferred_element_type=F32,
        )
    return flat


def started(pairs, sems):
    copies = [pltpu.make_async_copy(src, dst, sems.at[n]) for n, (src, dst) in enumerate(pairs)]
    for copy in copies:
        copy.start()
    return copies


def wait_all(copies):
    for copy in copies:
        copy.wait()


def east_pack_kernel(now, prev, buoy, mu, lam, pa, pb, sems):
    rows = now.shape[1]
    odd = parity("gx")
    pairs = []
    for out, side in ((pa, 1 - odd), (pb, odd)):
        four = pl.ds((rows - 4) * side, 4)
        two = pl.ds((rows - 2) * side, 2)
        for c in range(3):
            pairs.append((now.at[c, four], out.at[pl.ds(4 * c, 4)]))
            pairs.append((prev.at[c, two], out.at[pl.ds(12 + 2 * c, 2)]))
        for n, field in enumerate((buoy, mu, lam)):
            pairs.append((field.at[two], out.at[pl.ds(18 + 2 * n, 2)]))
    wait_all(started(pairs, sems))


def east_pack(now, prev, buoy, mu, lam):
    _, _, cols, depth = now.shape
    out = pltpu.VMEM((24, cols, depth), F32)
    return pl.pallas_call(
        east_pack_kernel,
        out_shape=(out, out),
        in_specs=[HBM_SPEC] * 5,
        out_specs=(VMEM_SPEC,) * 2,
        scratch_shapes=[pltpu.SemaphoreType.DMA((18,))],
        compiler_params=pltpu.CompilerParams(vmem_limit_bytes=VMEM_BYTES),
        name="east_pack",
    )(now, prev, buoy, mu, lam)


def clear_north(vp):
    none = jnp.zeros((vp.shape[0], vp.shape[1], 2, vp.shape[3]), F32)
    vp[:, :, 6:8, :] = none
    vp[:, :, 24:26, :] = none


def first_main_kernel(prev, buoy, mu, lam, now, xa, xb, out, pack, vp, pv, bv, mv, lv, byx, syz, sems):
    rows = now.shape[1]
    own = pl.ds(2, rows)
    copies = started(
        [(prev, pv.at[:, own])] + [(src, dst.at[own]) for src, dst in ((buoy, bv), (mu, mv), (lam, lv))], sems
    )
    odd = parity("gx")
    vp[:, 4 : rows + 4, 8:24, :] = now[...]
    for edge, side in ((xa, 1 - odd), (xb, odd)):
        four = pl.ds((rows + 4) * side, 4)
        two = pl.ds((rows + 2) * side, 2)
        for c in range(3):
            vp[c, four, 8:24, :] = edge[4 * c : 4 * c + 4]
            pv[c, two] = edge[12 + 2 * c : 14 + 2 * c]
        for n, field in enumerate((bv, mv, lv)):
            field[two] = edge[18 + 2 * n : 20 + 2 * n]
    clear_north(vp)
    step_columns(
        vp, pv, bv, mv, lv, out, pack, byx, syz, 0, now.shape[3] // LANES,
        lambda: wait_all(copies), lambda row, count: None,
    )


def first_main(now, xa, xb, prev, buoy, mu, lam):
    _, rows, cols, depth = now.shape
    wide = rows + 4
    one = pltpu.VMEM((wide, cols, depth), F32)
    return pl.pallas_call(
        first_main_kernel,
        out_shape=(pltpu.VMEM((3, wide, cols, depth), F32), pltpu.VMEM((3, wide, 8, depth), F32)),
        in_specs=[HBM_SPEC] * 4 + [VMEM_SPEC] * 3,
        out_specs=(VMEM_SPEC,) * 2,
        scratch_shapes=[
            pltpu.VMEM((3, wide + 4, 32, depth), F32),
            pltpu.VMEM((3, wide, cols, depth), F32),
            one,
            one,
            one,
            pltpu.VMEM((wide + 4, cols, depth), F32),
            pltpu.VMEM((wide + 4, cols, depth), F32),
            pltpu.SemaphoreType.DMA((4,)),
        ],
        compiler_params=pltpu.CompilerParams(vmem_limit_bytes=VMEM_BYTES),
        name="first_main",
    )(prev, buoy, mu, lam, now, xa, xb)


def first_north_kernel(main, pack, ya, yb, mid, ma, mb, top, rim, ex, ey):
    rows = main.shape[1] - 4
    fill_north(rim, ya, yb)
    add_north(rim, pack, main, mid, ex, ey, 0, main.shape[3] // LANES)
    odd = parity("gy")

    @pl.when(odd == 0)
    def _():
        ma[...] = mid[:, :, 14:16, :]
        mb[...] = mid[:, :, 0:2, :]

    @pl.when(odd == 1)
    def _():
        ma[...] = mid[:, :, 0:2, :]
        mb[...] = mid[:, :, 14:16, :]

    top[...] = surface_rows(mid.at[:, pl.ds(2, rows)], 0)


def first_north(main, pack, ya, yb):
    _, wide, _, depth = main.shape
    edge = pltpu.VMEM((3, wide, 2, depth), F32)
    return pl.pallas_call(
        first_north_kernel,
        out_shape=(pltpu.VMEM(main.shape, F32), edge, edge, pltpu.VMEM((8, SIDE * SIDE), F32)),
        in_specs=[VMEM_SPEC] * 4,
        out_specs=(VMEM_SPEC,) * 4,
        scratch_shapes=[
            pltpu.VMEM((3, wide + 4, 24, depth), F32),
            pltpu.VMEM((wide + 4, 8, depth), F32),
            pltpu.VMEM((wide + 4, 8, depth), F32),
        ],
        compiler_params=pltpu.CompilerParams(vmem_limit_bytes=VMEM_BYTES),
        name="first_north",
    )(main, pack, ya, yb)


def second_main_kernel(
    prev, buoy, mu, lam, v, mid, nxt, far, near, close, vp, pv, bv, mv, lv, out, pack, byx, syz, sems
):
    rows = prev.shape[1]
    total = prev.shape[3] // LANES
    copies = started([(prev, pv), (buoy, bv), (mu, mv), (lam, lv)], sems)
    stores = started([(v.at[:, pl.ds(2, rows)], mid)], sems.at[pl.ds(4, 1)])
    vp[:, :, 8:24, :] = v[...]
    clear_north(vp)
    rest = pl.ds(LANES, prev.shape[3] - LANES)

    def done(row, count):
        part = pl.ds(row, count)
        near[:, part] = out[:, part, :, 0:LANES]
        stores.extend(
            started([(out.at[:, part, :, rest], nxt.at[:, part, :, rest])], sems.at[pl.ds(4 + len(stores), 1)])
        )

    step_columns(
        vp, pv, bv, mv, lv, out, pack, byx, syz, 0, total, lambda: wait_all(copies), done
    )
    stores += started([(pack.at[:, :, :, rest], far)], sems.at[pl.ds(9, 1)])
    close[...] = pack[:, :, :, 0:LANES]
    wait_all(stores)


def second_main(v, prev, buoy, mu, lam):
    _, rows, cols, depth = prev.shape
    whole = pltpu.VMEM(prev.shape, F32)
    one = pltpu.VMEM((rows, cols, depth), F32)
    return pl.pallas_call(
        second_main_kernel,
        out_shape=(
            pltpu.HBM(prev.shape, F32),
            pltpu.HBM(prev.shape, F32),
            pltpu.HBM((3, rows, 8, depth - LANES), F32),
            pltpu.VMEM((3, rows, cols, LANES), F32),
            pltpu.VMEM((3, rows, 8, LANES), F32),
        ),
        in_specs=[HBM_SPEC] * 4 + [VMEM_SPEC],
        out_specs=(HBM_SPEC,) * 3 + (VMEM_SPEC,) * 2,
        scratch_shapes=[
            pltpu.VMEM((3, rows + 4, 32, depth), F32),
            whole,
            one,
            one,
            one,
            whole,
            pltpu.VMEM((3, rows, 8, depth), F32),
            pltpu.VMEM((rows + 4, cols, depth), F32),
            pltpu.VMEM((rows + 4, cols, depth), F32),
            pltpu.SemaphoreType.DMA((10,)),
        ],
        compiler_params=pltpu.CompilerParams(vmem_limit_bytes=VMEM_BYTES),
        name="second_main",
    )(prev, buoy, mu, lam, v)


def fill_north(rim, ya, yb):
    odd_y = parity("gy")
    rim[:, :, 8:16, :] = jnp.zeros((rim.shape[0], rim.shape[1], 8, rim.shape[3]), F32)

    wide = rim.shape[3]

    @pl.when(odd_y == 0)
    def _():
        rim[:, :, 6:8, :] = yb[:, :, :, :wide]
        rim[:, :, 16:18, :] = ya[:, :, :, :wide]

    @pl.when(odd_y == 1)
    def _():
        rim[:, :, 6:8, :] = ya[:, :, :, :wide]
        rim[:, :, 16:18, :] = yb[:, :, :, :wide]


def add_north(rim, pack, main, out, ex, ey, first, last, ready=None, total=3):
    rows = rim.shape[1] - 4
    span = range(first, last)
    lanes = lambda k: pl.ds(k * LANES, LANES)
    local = lambda k: pl.ds((k - first) * LANES, LANES)
    below, above = max(first - 1, 0), min(last + 1, total)

    def y_four(c, r, k):
        return [rim[c, r, pl.ds(8 + d, 8), lanes(k)] for d in (1, -1, 2, -2)]

    def ends(get):
        return (
            get(first - 1) if first > 0 else None,
            [get(k) for k in span],
            get(last) if last < total else None,
        )

    def inner(r, carry):
        for k in range(below, above):
            ey[r, :, lanes(k)] = first_of(*y_four(1, r, k))
        for k in span:
            ex[r, :, lanes(k)] = first_of(*y_four(0, r, k))
        return carry

    lax.fori_loop(0, rows + 4, inner, 0)
    if ready is not None:
        ready()

    def outer(i, carry):
        r = i + 2
        yz = z_first(*ends(lambda k: first_of(*y_four(2, r, k))))
        xy = z_first(*ends(lambda k: ey[r, :, lanes(k)]))
        low = iota((8, LANES), 0) < 4
        for n, k in enumerate(span):

            def derived(ref):
                return first_of(*[ref[r + d, :, lanes(k)] for d in (1, -1, 2, -2)])

            shear, both, scale = [pack[which, i, :, local(k)] for which in range(3)]
            mixed = [derived(ey), derived(ex) + yz[n], xy[n]]
            for c in range(3):
                q = second_of(*y_four(c, r, k))
                along = mixed[c] * (1.0 / 3.0)
                if c == 1:
                    along = along + q
                update = scale * (shear * q + both * along)
                out[c, i, 0:8, local(k)] = main[c, i, 0:8, local(k)] + jnp.where(low, update, 0.0)
                out[c, i, 8:16, local(k)] = main[c, i, 8:16, local(k)] + jnp.where(low, 0.0, update)
        return carry

    lax.fori_loop(0, rows, outer, 0)


def window_tables(flat, windows):
    span = SIDE - PX + 1
    halves = [flat[:, :LANES], flat[:, LANES:]]
    lane = iota((8, LANES), 1)
    windows[span * span * 8 :, :] = jnp.zeros((windows.shape[0] - span * span * 8, LANES), F32)
    for ox in range(span):
        for oy in range(span):
            half, shift = divmod(ox * SIDE + oy, LANES)
            moved = halves[half]
            if shift:
                other = pltpu.roll(halves[1], LANES - shift, axis=1) if half == 0 else jnp.zeros_like(moved)
                moved = jnp.where(lane < LANES - shift, pltpu.roll(moved, LANES - shift, axis=1), other)
            windows[pl.ds((ox * span + oy) * 8, 8), :] = moved


def corner_forces(flat, weights, windows):
    window_tables(flat, windows)
    total = jnp.zeros((LANES, weights.shape[2]), F32)
    for c in range(3):
        total = total + jnp.dot(
            windows[pl.ds(c, LANES, stride=8), :], weights[c], precision=HIGHEST, preferred_element_type=F32
        )
    return total


def spread(part, c):
    shape = (LANES, part.shape[1])
    cell = iota(shape, 0)
    row = c * PX * PX + (cell // SIDE) * PX + cell % SIDE
    place = jnp.where((iota(shape, 1) == row) & (cell % SIDE < PX), 1.0, 0.0)
    return lax.dot_general(
        place, part[...], (((1,), (1,)), ((), ())), precision=HIGHEST, preferred_element_type=F32
    )


def prepare_kernel(asked, offset, part, chosen, weights):
    span = SIDE - PX + 1
    shape = (LANES, LANES)
    where = offset[0:1, :] * span + offset[1:2, :]
    corner = jnp.where(iota(shape, 0) == where, 1.0, 0.0)
    lane = iota(shape, 1)
    for r in range(2):
        slot = jnp.where(lane == asked[:, r : r + 1], 1.0, 0.0)
        chosen[pl.ds(r, LANES, stride=2), :] = lax.dot_general(
            slot, corner, (((1,), (1,)), ((), ())), preferred_element_type=F32
        )
    for c in range(3):
        weights[c] = spread(part, c)


def prepare(asked, offset, part):
    modes = part.shape[0]
    return pl.pallas_call(
        prepare_kernel,
        out_shape=(pltpu.VMEM((2 * LANES, LANES), F32), pltpu.VMEM((3, LANES, modes), F32)),
        in_specs=[VMEM_SPEC] * 3,
        out_specs=(VMEM_SPEC,) * 2,
        compiler_params=pltpu.CompilerParams(vmem_limit_bytes=VMEM_BYTES),
        name="prepare",
    )(asked, offset, part)


def early_kernel(top, chosen, weights, early, windows):
    forces = corner_forces(top[...], weights, windows)
    early[...] = jnp.dot(chosen[...], forces, precision=HIGHEST, preferred_element_type=F32)


def early_forces(top, chosen, weights):
    return pl.pallas_call(
        early_kernel,
        out_shape=pltpu.VMEM((2 * LANES, weights.shape[2]), F32),
        in_specs=[VMEM_SPEC] * 3,
        out_specs=VMEM_SPEC,
        scratch_shapes=[pltpu.VMEM((8 * LANES, LANES), F32)],
        compiler_params=pltpu.CompilerParams(vmem_limit_bytes=VMEM_BYTES),
        name="early_forces",
    )(top, chosen, weights)


def near_north_kernel(
    before, near, pack, ya, yb, chosen, weights, early, nxt, yao, ybo, ans, rim, out, ex, ey, windows, sems
):
    stores = started([(ya, yao), (yb, ybo)], sems)
    fill_north(rim, ya, yb)
    add_north(rim, pack, near, out, ex, ey, 0, 1)
    stores += started([(out, nxt.at[:, :, :, pl.ds(0, LANES)])], sems.at[pl.ds(2, 1)])
    forces = corner_forces(surface_rows(out, 0), weights, windows)
    late = jnp.dot(chosen[...], forces, precision=HIGHEST, preferred_element_type=F32)
    ans[...] = jnp.concatenate([early[...], late], axis=1)
    wait_all(stores)


def near_north(nxt, near, pack, ya, yb, chosen, weights, early):
    _, rows, cols, _ = nxt.shape
    rim = pltpu.HBM(ya.shape, F32)
    return pl.pallas_call(
        near_north_kernel,
        out_shape=(pltpu.HBM(nxt.shape, F32), rim, rim, jax.ShapeDtypeStruct((2 * LANES, LANES), F32)),
        in_specs=[HBM_SPEC] + [VMEM_SPEC] * 7,
        out_specs=(HBM_SPEC,) * 3 + (VMEM_SPEC,),
        input_output_aliases={0: 0},
        scratch_shapes=[
            pltpu.VMEM((3, rows + 4, 24, 2 * LANES), F32),
            pltpu.VMEM((3, rows, cols, LANES), F32),
            pltpu.VMEM((rows + 4, 8, 2 * LANES), F32),
            pltpu.VMEM((rows + 4, 8, 2 * LANES), F32),
            pltpu.VMEM((8 * LANES, LANES), F32),
            pltpu.SemaphoreType.DMA((3,)),
        ],
        compiler_params=pltpu.CompilerParams(vmem_limit_bytes=VMEM_BYTES),
        name="near_north",
    )(nxt, near, pack, ya, yb, chosen, weights, early)


def far_north_kernel(before, pack, ya, yb, nxt, rim, yav, ybv, pv, main, out, ex, ey, sems):
    count = out.shape[3]
    columns = pl.ds(LANES, count)
    copies = started([(ya, yav), (yb, ybv), (before.at[:, :, :, columns], main), (pack, pv)], sems)
    wait_all(copies[:2])
    fill_north(rim, yav, ybv)
    add_north(rim, pv, main, out, ex, ey, 1, 1 + count // LANES, lambda: wait_all(copies[2:]))
    wait_all(started([(out, nxt.at[:, :, :, columns])], sems.at[pl.ds(4, 1)]))


def far_north(nxt, pack, ya, yb):
    _, rows, cols, depth = nxt.shape
    rest = depth - LANES
    part = pltpu.VMEM((3, rows, cols, rest), F32)
    return pl.pallas_call(
        far_north_kernel,
        out_shape=jax.ShapeDtypeStruct(nxt.shape, F32),
        in_specs=[HBM_SPEC] * 4,
        out_specs=HBM_SPEC,
        input_output_aliases={0: 0},
        scratch_shapes=[
            pltpu.VMEM((3, rows + 4, 24, depth), F32),
            pltpu.VMEM(ya.shape, F32),
            pltpu.VMEM(ya.shape, F32),
            pltpu.VMEM(pack.shape, F32),
            part,
            part,
            pltpu.VMEM((rows + 4, 8, depth), F32),
            pltpu.VMEM((rows + 4, 8, depth), F32),
            pltpu.SemaphoreType.DMA((5,)),
        ],
        compiler_params=pltpu.CompilerParams(vmem_limit_bytes=VMEM_BYTES),
        name="far_north",
    )(nxt, pack, ya, yb)


def north_kernel(now, xa, xb, ya, yb):
    rows = now.shape[1]
    odd_x, odd_y = parity("gx"), parity("gy")

    def gather(out, edge):
        out[:, 4 : rows + 4] = now[:, :, edge : edge + 2, :]
        for rim, side in ((xa, 1 - odd_x), (xb, odd_x)):
            for c in range(3):
                out[c, pl.ds((rows + 4) * side, 4)] = rim[4 * c : 4 * c + 4, edge : edge + 2, :]

    high = SIDE - 2

    @pl.when(odd_y == 0)
    def _():
        gather(ya, high)
        gather(yb, 0)

    @pl.when(odd_y == 1)
    def _():
        gather(ya, 0)
        gather(yb, high)


def north_edges(now, xa, xb):
    _, rows, _, depth = now.shape
    out = pltpu.VMEM((3, rows + 8, 2, depth), F32)
    return pl.pallas_call(
        north_kernel,
        out_shape=(out, out),
        in_specs=[VMEM_SPEC] * 3,
        out_specs=(VMEM_SPEC, VMEM_SPEC),
        compiler_params=pltpu.CompilerParams(vmem_limit_bytes=VMEM_BYTES),
        name="north_edges",
    )(now, xa, xb)


def request_kernel(source, count, req, pos):
    shape = (LANES, LANES)
    src = source[...]
    slot = iota((1, LANES), 1)
    live = slot < count[0]
    tile = src // LANES
    local = (src % LANES).astype(F32)
    mine = jnp.where((iota(shape, 0) == tile) & live, 1.0, 0.0)
    earlier = jnp.where(iota(shape, 0) < iota(shape, 1), 1.0, 0.0)
    before = jnp.dot(mine, earlier, preferred_element_type=F32)
    rank = jnp.sum(before * mine, axis=0, keepdims=True)
    wanted = mine * local
    lane = iota(shape, 1)
    first = jnp.sum(jnp.where(rank < 0.5, wanted, 0.0), axis=1, keepdims=True)
    second = jnp.sum(jnp.where(rank > 0.5, wanted, 0.0), axis=1, keepdims=True)
    req[...] = jnp.where(lane == 0, first, jnp.where(lane == 1, second, 0.0)).astype(jnp.int32)
    pos[...] = jnp.where(live, tile * 2 + rank.astype(jnp.int32), -1)


def make_requests(source, count):
    return pl.pallas_call(
        request_kernel,
        out_shape=(
            jax.ShapeDtypeStruct((LANES, LANES), jnp.int32),
            jax.ShapeDtypeStruct((1, LANES), jnp.int32),
        ),
        in_specs=[VMEM_SPEC, SMEM_SPEC],
        out_specs=(VMEM_SPEC, VMEM_SPEC),
        compiler_params=pltpu.CompilerParams(vmem_limit_bytes=VMEM_BYTES),
        name="requests",
    )(source.reshape(1, LANES), count)


def columns_of(ker):
    taps = ker.shape[0]
    same = jnp.where(iota((taps, taps), 0) == iota((taps, taps), 1), 1.0, 0.0)
    return lax.dot_general(
        ker[...], same, (((0,), (0,)), ((), ())), precision=HIGHEST, preferred_element_type=F32
    )


def history_kernel(hist, ker, out):
    k = columns_of(ker)
    steps = hist.shape[0]
    half = hist.shape[1] // 2
    for part in range(2):
        rows = pl.ds(part * half, half)
        kp = k[part * half : (part + 1) * half]
        first = jnp.zeros((half, LANES), F32)
        second = jnp.zeros((half, LANES), F32)
        for h in range(steps):
            past = hist[h, rows, :]
            first = first + kp[:, steps - h : steps - h + 1] * past
            if h > 0:
                second = second + kp[:, steps + 1 - h : steps + 2 - h] * past
        out[0, rows, :] = first
        out[1, rows, :] = second


def history_part(hist, ker):
    return pl.pallas_call(
        history_kernel,
        out_shape=jax.ShapeDtypeStruct((2,) + hist.shape[1:], F32),
        in_specs=[VMEM_SPEC, VMEM_SPEC],
        out_specs=VMEM_SPEC,
        compiler_params=pltpu.CompilerParams(vmem_limit_bytes=VMEM_BYTES),
        name="history",
    )(hist, ker)


def response_kernel(ans, pos, base, ker, out):
    at = pos[...]
    chosen = jnp.where(iota((2 * LANES, LANES), 0) == at, 1.0, 0.0)
    forces = lax.dot_general(
        ans[...], chosen, (((0,), (0,)), ((), ())), precision=HIGHEST, preferred_element_type=F32
    )
    k = columns_of(ker)
    modes = k.shape[0]
    early, late = forces[:modes], forces[modes:]
    live = at >= 0
    out[0] = jnp.where(live, base[0] + k[:, 0:1] * early, 0.0)
    out[1] = jnp.where(live, base[1] + k[:, 0:1] * late + k[:, 1:2] * early, 0.0)


def make_responses(ans, pos, base, ker):
    return pl.pallas_call(
        response_kernel,
        out_shape=jax.ShapeDtypeStruct(base.shape, F32),
        in_specs=[VMEM_SPEC] * 4,
        out_specs=VMEM_SPEC,
        compiler_params=pltpu.CompilerParams(vmem_limit_bytes=VMEM_BYTES),
        name="responses",
    )(ans, pos, base, ker)


def swap(array, axis, first):
    pairs = []
    for low in range(first, lax.axis_size(axis) - 1, 2):
        pairs += [(low, low + 1), (low + 1, low)]
    return in_vmem(lax.ppermute(array, axis, pairs))


def east_swaps(xa, xb):
    return swap(xa, "gx", 0), swap(xb, "gx", 1)


def north_swaps(ya, yb):
    return swap(ya, "gy", 0), swap(yb, "gy", 1)


def per_device(
    disp_prev,
    disp_now,
    buoyancy,
    shear_mod,
    lame_first,
    foot_offset,
    owner_source,
    owner_count,
    force_history,
    participation,
    kernels,
):
    return steps(
        disp_prev,
        disp_now,
        tuple(in_hbm(a) for a in (buoyancy, shear_mod, lame_first)),
        foot_offset.T,
        owner_source,
        owner_count,
        force_history,
        participation.T,
        kernels.T,
    )


def exchange(array):
    rows = array.reshape(LANES, -1, LANES)
    out = lax.all_to_all(rows, ("gx", "gy"), split_axis=0, concat_axis=0, tiled=True)
    return out.reshape(array.shape)


def steps(prev, now, medium, offset, source, count, history, part, kernels):
    held = in_vmem(now)
    east = east_pack(in_hbm(now), in_hbm(prev), *medium)
    east = east_swaps(*east)
    req, pos = make_requests(source, count)
    asked = exchange(req)
    north = north_edges(held, *east)
    north = north_swaps(*north)
    base = history_part(history, kernels)
    prepared = prepare(in_vmem(asked), offset, part)
    main = first_main(held, *east, in_hbm(prev), *medium)
    north, main, base, prepared = lax.optimization_barrier((north, main, base, prepared))
    mid, ya, yb, top = first_north(*main, *north)
    north = north_swaps(ya, yb)
    early = early_forces(top, *prepared)
    disp_mid, rest, far, near, close = second_main(mid, in_hbm(now), *medium)
    north, rest, far, near, close, early = lax.optimization_barrier((north, rest, far, near, close, early))
    disp_next, ya, yb, ans = near_north(in_hbm(rest), near, close, *north, *prepared, early)
    back = exchange(ans)
    disp_next = far_north(in_hbm(disp_next), in_hbm(far), in_hbm(ya), in_hbm(yb))
    responses = make_responses(back, pos, base, kernels)
    return disp_mid, disp_next, responses


def solution(mesh):
    return jax.shard_map(
        per_device,
        mesh=mesh,
        in_specs=(
            P(None, "gx", "gy", None),
            P(None, "gx", "gy", None),
            P("gx", "gy", None),
            P("gx", "gy", None),
            P("gx", "gy", None),
            P(("gx", "gy"), None),
            P(("gx", "gy")),
            P(("gx", "gy")),
            P(None, None, ("gx", "gy")),
            P(),
            P(),
        ),
        out_specs=(
            P(None, "gx", "gy", None),
            P(None, "gx", "gy", None),
            P(None, None, ("gx", "gy")),
        ),
        check_vma=False,
    )
```

```python
import jax
import jax.numpy as jnp
from jax import lax
from jax.experimental import pallas as pl
from jax.experimental.pallas import tpu as pltpu
from jax.sharding import PartitionSpec as P


PX = 8
SIDE = 16
LANES = 128
HIGHEST = lax.Precision.HIGHEST
F32 = jnp.float32
VMEM_BYTES = 16 << 20

VMEM_SPEC = pl.BlockSpec(memory_space=pltpu.VMEM)
HBM_SPEC = pl.BlockSpec(memory_space=pltpu.HBM)
SMEM_SPEC = pl.BlockSpec(memory_space=pltpu.SMEM)


def iota(shape, axis):
    return lax.broadcasted_iota(jnp.int32, shape, axis)


def in_vmem(array):
    return pltpu.with_memory_space_constraint(array, pltpu.VMEM)


def in_hbm(array):
    return pltpu.with_memory_space_constraint(array, pltpu.HBM)


def parity(axis):
    return lax.axis_index(axis) % 2


def first_of(a1, b1, a2, b2):
    return (a1 - b1) - (a2 - b2) * 0.125


def second_of(a1, b1, a2, b2):
    return (a1 + b1) - (a2 + b2) * 0.0625


def z_four(below, columns, above):
    lane = iota(columns[0].shape, 1)
    zero = jnp.zeros_like(columns[0])
    count = len(columns)
    out = [[] for _ in columns]
    for s in (1, -1, 2, -2):
        turned = [pltpu.roll(c, (-s) % LANES, axis=1) for c in columns]
        if s > 0:
            turned.append(zero if above is None else pltpu.roll(above, LANES - s, axis=1))
        else:
            turned.insert(0, zero if below is None else pltpu.roll(below, -s, axis=1))
        for k in range(count):
            if s > 0:
                out[k].append(jnp.where(lane < LANES - s, turned[k], turned[k + 1]))
            else:
                out[k].append(jnp.where(lane >= -s, turned[k + 1], turned[k]))
    return out


def z_first(below, columns, above):
    return [first_of(*four) for four in z_four(below, columns, above)]


def step_columns(vp, prev, buoy, mu, lam, out, pack, byx, syz, first, last, ready, done):
    rows = vp.shape[1] - 4
    total = vp.shape[3] // LANES
    span = range(first, last)
    lanes = lambda k: pl.ds(k * LANES, LANES)

    def y_four(c, r, h, k):
        return [vp[c, r, pl.ds(8 + 8 * h + d, 8), lanes(k)] for d in (1, -1, 2, -2)]

    def ends(get):
        below = get(first - 1) if first > 0 else None
        above = get(last) if last < total else None
        return below, [get(k) for k in span], above

    def inner(r, carry):
        for h in range(2):
            here = pl.ds(8 * h, 8)
            core = pl.ds(8 + 8 * h, 8)
            dz = z_first(*ends(lambda k: vp[2, r, core, lanes(k)]))
            for n, k in enumerate(span):
                byx[r, here, lanes(k - first)] = first_of(*y_four(0, r, h, k))
                syz[r, here, lanes(k - first)] = first_of(*y_four(1, r, h, k)) + dz[n]
        return carry

    lax.fori_loop(0, rows + 4, inner, 0)

    def outer(i, carry):
        r = i + 2
        low = iota((8, LANES), 0) < 4
        lower = {}
        for h in range(2):
            here = pl.ds(8 * h, 8)
            core = pl.ds(8 + 8 * h, 8)

            def x_four(c, k):
                return [vp[c, r + d, core, lanes(k)] for d in (1, -1, 2, -2)]

            def derived(ref, k):
                return first_of(*[ref[r + d, here, lanes(k - first)] for d in (1, -1, 2, -2)])

            yz = z_first(*ends(lambda k: first_of(*y_four(2, r, h, k))))
            xy = z_first(*ends(lambda k: first_of(*x_four(0, k)) + first_of(*y_four(1, r, h, k))))
            along_z = [z_four(*ends(lambda k: vp[c, r, core, lanes(k)])) for c in range(3)]
            for n, k in enumerate(span):
                shear = mu[i, here, lanes(k - first)]
                both = lam[i, here, lanes(k - first)] + shear
                scale = buoy[i, here, lanes(k - first)] * 0.12
                for which, factor in enumerate((shear, both, scale)):
                    if h == 0:
                        lower[which, k] = factor
                    else:
                        pack[which, i, :, lanes(k - first)] = jnp.where(low, lower[which, k], factor)
                mixed = [derived(syz, k), derived(byx, k) + yz[n], xy[n]]
                for c in range(3):
                    centre = vp[c, r, core, lanes(k)]
                    q = [second_of(*x_four(c, k)), second_of(*y_four(c, r, h, k)), second_of(*along_z[c][n])]
                    laplace = (q[0] + q[1]) + (q[2] - centre * 5.625)
                    along = (q[c] - centre * 1.875) + mixed[c] * (1.0 / 3.0)
                    update = shear * laplace + both * along
                    out[c, i, here, lanes(k - first)] = (
                        2.0 * centre - prev[c, i, here, lanes(k - first)]
                    ) + scale * update
        return carry

    ready()
    for start in range(0, rows, rows // 4):
        lax.fori_loop(start, start + rows // 4, outer, 0)
        done(start, rows // 4)


def surface_rows(field, first):
    cells = SIDE * SIDE
    flat = jnp.zeros((8, cells), F32)
    for c in range(3):
        pick = jnp.where((iota((8, LANES), 0) == first + c) & (iota((8, LANES), 1) == 0), 1.0, 0.0)
        flat = flat + lax.dot_general(
            pick,
            field[c, :, :, 0:LANES].reshape(cells, LANES),
            (((1,), (1,)), ((), ())),
            precision=HIGHEST,
            preferred_element_type=F32,
        )
    return flat


def started(pairs, sems):
    copies = [pltpu.make_async_copy(src, dst, sems.at[n]) for n, (src, dst) in enumerate(pairs)]
    for copy in copies:
        copy.start()
    return copies


def wait_all(copies):
    for copy in copies:
        copy.wait()


def east_pack_kernel(now, prev, buoy, mu, lam, source, pa, pb, req, pos, held, sems):
    rows = now.shape[1]
    odd = parity("gx")
    pairs = []
    for out, side in ((pa, 1 - odd), (pb, odd)):
        four = pl.ds((rows - 4) * side, 4)
        two = pl.ds((rows - 2) * side, 2)
        for c in range(3):
            pairs.append((now.at[c, four], out.at[pl.ds(4 * c, 4)]))
            pairs.append((prev.at[c, two], out.at[pl.ds(12 + 2 * c, 2)]))
        for n, field in enumerate((buoy, mu, lam)):
            pairs.append((field.at[two], out.at[pl.ds(18 + 2 * n, 2)]))
    copies = started([(source, held)] + pairs, sems)
    copies[0].wait()
    build_requests(held, req, pos)
    wait_all(copies[1:])


def east_pack(now, prev, buoy, mu, lam, source):
    _, _, cols, depth = now.shape
    out = pltpu.VMEM((24, cols, depth), F32)
    return pl.pallas_call(
        east_pack_kernel,
        out_shape=(
            out,
            out,
            jax.ShapeDtypeStruct((LANES, LANES), jnp.int32),
            pltpu.VMEM((1, LANES), jnp.int32),
        ),
        in_specs=[HBM_SPEC] * 6,
        out_specs=(VMEM_SPEC,) * 4,
        scratch_shapes=[pltpu.VMEM((1, LANES), jnp.int32), pltpu.SemaphoreType.DMA((19,))],
        compiler_params=pltpu.CompilerParams(vmem_limit_bytes=VMEM_BYTES),
        name="east_pack",
    )(now, prev, buoy, mu, lam, source)


def clear_north(vp):
    none = jnp.zeros((vp.shape[0], vp.shape[1], 2, vp.shape[3]), F32)
    vp[:, :, 6:8, :] = none
    vp[:, :, 24:26, :] = none


def first_main_kernel(prev, buoy, mu, lam, now, xa, xb, out, pack, vp, pv, bv, mv, lv, byx, syz, sems):
    rows = now.shape[1]
    own = pl.ds(2, rows)
    copies = started(
        [(prev, pv.at[:, own])] + [(src, dst.at[own]) for src, dst in ((buoy, bv), (mu, mv), (lam, lv))], sems
    )
    odd = parity("gx")
    vp[:, 4 : rows + 4, 8:24, :] = now[...]
    for edge, side in ((xa, 1 - odd), (xb, odd)):
        four = pl.ds((rows + 4) * side, 4)
        two = pl.ds((rows + 2) * side, 2)
        for c in range(3):
            vp[c, four, 8:24, :] = edge[4 * c : 4 * c + 4]
            pv[c, two] = edge[12 + 2 * c : 14 + 2 * c]
        for n, field in enumerate((bv, mv, lv)):
            field[two] = edge[18 + 2 * n : 20 + 2 * n]
    clear_north(vp)
    step_columns(
        vp, pv, bv, mv, lv, out, pack, byx, syz, 0, now.shape[3] // LANES,
        lambda: wait_all(copies), lambda row, count: None,
    )


def first_main(now, xa, xb, prev, buoy, mu, lam):
    _, rows, cols, depth = now.shape
    wide = rows + 4
    one = pltpu.VMEM((wide, cols, depth), F32)
    return pl.pallas_call(
        first_main_kernel,
        out_shape=(pltpu.VMEM((3, wide, cols, depth), F32), pltpu.VMEM((3, wide, 8, depth), F32)),
        in_specs=[HBM_SPEC] * 4 + [VMEM_SPEC] * 3,
        out_specs=(VMEM_SPEC,) * 2,
        scratch_shapes=[
            pltpu.VMEM((3, wide + 4, 32, depth), F32),
            pltpu.VMEM((3, wide, cols, depth), F32),
            one,
            one,
            one,
            pltpu.VMEM((wide + 4, cols, depth), F32),
            pltpu.VMEM((wide + 4, cols, depth), F32),
            pltpu.SemaphoreType.DMA((4,)),
        ],
        compiler_params=pltpu.CompilerParams(vmem_limit_bytes=VMEM_BYTES),
        name="first_main",
    )(prev, buoy, mu, lam, now, xa, xb)


def first_north_kernel(main, pack, ya, yb, mid, ma, mb, top, rim, ex, ey):
    rows = main.shape[1] - 4
    fill_north(rim, ya, yb)
    add_north(rim, pack, main, mid, ex, ey, 0, main.shape[3] // LANES)
    odd = parity("gy")

    @pl.when(odd == 0)
    def _():
        ma[...] = mid[:, :, 14:16, :]
        mb[...] = mid[:, :, 0:2, :]

    @pl.when(odd == 1)
    def _():
        ma[...] = mid[:, :, 0:2, :]
        mb[...] = mid[:, :, 14:16, :]

    top[...] = surface_rows(mid.at[:, pl.ds(2, rows)], 0)


def first_north(main, pack, ya, yb):
    _, wide, _, depth = main.shape
    edge = pltpu.VMEM((3, wide, 2, depth), F32)
    return pl.pallas_call(
        first_north_kernel,
        out_shape=(pltpu.VMEM(main.shape, F32), edge, edge, pltpu.VMEM((8, SIDE * SIDE), F32)),
        in_specs=[VMEM_SPEC] * 4,
        out_specs=(VMEM_SPEC,) * 4,
        scratch_shapes=[
            pltpu.VMEM((3, wide + 4, 24, depth), F32),
            pltpu.VMEM((wide + 4, 8, depth), F32),
            pltpu.VMEM((wide + 4, 8, depth), F32),
        ],
        compiler_params=pltpu.CompilerParams(vmem_limit_bytes=VMEM_BYTES),
        name="first_north",
    )(main, pack, ya, yb)


def second_main_kernel(prev, buoy, mu, lam, v, mid, out, pack, vp, pv, bv, mv, lv, byx, syz, sems):
    rows = prev.shape[1]
    total = prev.shape[3] // LANES
    copies = started([(prev, pv), (buoy, bv), (mu, mv), (lam, lv)], sems)
    stores = started([(v.at[:, pl.ds(2, rows)], mid)], sems.at[pl.ds(4, 1)])
    vp[:, :, 8:24, :] = v[...]
    clear_north(vp)
    step_columns(
        vp, pv, bv, mv, lv, out, pack, byx, syz, 0, total, lambda: wait_all(copies), lambda row, count: None
    )
    wait_all(stores)


def second_main(v, prev, buoy, mu, lam):
    _, rows, cols, depth = prev.shape
    whole = pltpu.VMEM(prev.shape, F32)
    one = pltpu.VMEM((rows, cols, depth), F32)
    return pl.pallas_call(
        second_main_kernel,
        out_shape=(
            pltpu.HBM(prev.shape, F32),
            whole,
            pltpu.VMEM((3, rows, 8, depth), F32),
        ),
        in_specs=[HBM_SPEC] * 4 + [VMEM_SPEC],
        out_specs=(HBM_SPEC,) + (VMEM_SPEC,) * 2,
        scratch_shapes=[
            pltpu.VMEM((3, rows + 4, 32, depth), F32),
            whole,
            one,
            one,
            one,
            pltpu.VMEM((rows + 4, cols, depth), F32),
            pltpu.VMEM((rows + 4, cols, depth), F32),
            pltpu.SemaphoreType.DMA((5,)),
        ],
        compiler_params=pltpu.CompilerParams(vmem_limit_bytes=VMEM_BYTES),
        name="second_main",
    )(prev, buoy, mu, lam, v)


def fill_north(rim, ya, yb):
    odd_y = parity("gy")
    rim[:, :, 8:16, :] = jnp.zeros((rim.shape[0], rim.shape[1], 8, rim.shape[3]), F32)

    wide = rim.shape[3]

    @pl.when(odd_y == 0)
    def _():
        rim[:, :, 6:8, :] = yb[:, :, :, :wide]
        rim[:, :, 16:18, :] = ya[:, :, :, :wide]

    @pl.when(odd_y == 1)
    def _():
        rim[:, :, 6:8, :] = ya[:, :, :, :wide]
        rim[:, :, 16:18, :] = yb[:, :, :, :wide]


def add_north(rim, pack, main, out, ex, ey, first, last, base=0, done=None, parts=1):
    rows = rim.shape[1] - 4
    total = 3
    span = range(first, last)
    lanes = lambda k: pl.ds(k * LANES, LANES)
    local = lambda k: pl.ds((k - base) * LANES, LANES)
    below, above = max(first - 1, 0), min(last + 1, total)

    def y_four(c, r, k):
        return [rim[c, r, pl.ds(8 + d, 8), lanes(k)] for d in (1, -1, 2, -2)]

    def ends(get):
        return (
            get(first - 1) if first > 0 else None,
            [get(k) for k in span],
            get(last) if last < total else None,
        )

    def inner(r):
        for k in range(below, above):
            ey[r, :, lanes(k)] = first_of(*y_four(1, r, k))
        for k in span:
            ex[r, :, lanes(k)] = first_of(*y_four(0, r, k))

    def inner_two(pair, carry):
        inner(2 * pair)
        inner(2 * pair + 1)
        return carry

    lax.fori_loop(0, (rows + 4) // 2, inner_two, 0)

    def outer(i):
        r = i + 2
        yz = z_first(*ends(lambda k: first_of(*y_four(2, r, k))))
        xy = z_first(*ends(lambda k: ey[r, :, lanes(k)]))
        low = iota((8, LANES), 0) < 4
        for n, k in enumerate(span):

            def derived(ref):
                return first_of(*[ref[r + d, :, lanes(k)] for d in (1, -1, 2, -2)])

            shear, both, scale = [pack[which, i, :, local(k)] for which in range(3)]
            mixed = [derived(ey), derived(ex) + yz[n], xy[n]]
            for c in range(3):
                q = second_of(*y_four(c, r, k))
                along = mixed[c] * (1.0 / 3.0)
                if c == 1:
                    along = along + q
                update = scale * (shear * q + both * along)
                out[c, i, 0:8, local(k)] = main[c, i, 0:8, local(k)] + jnp.where(low, update, 0.0)
                out[c, i, 8:16, local(k)] = main[c, i, 8:16, local(k)] + jnp.where(low, 0.0, update)

    def outer_two(pair, carry):
        outer(2 * pair)
        outer(2 * pair + 1)
        return carry

    count = rows // 2 // parts
    for part in range(parts):
        lax.fori_loop(part * count, (part + 1) * count, outer_two, 0)
        if done is not None:
            done(2 * part * count, 2 * count)


def window_tables(flat, windows):
    span = SIDE - PX + 1
    halves = [flat[:, :LANES], flat[:, LANES:]]
    lane = iota((8, LANES), 1)
    windows[span * span * 8 :, :] = jnp.zeros((windows.shape[0] - span * span * 8, LANES), F32)
    for ox in range(span):
        for oy in range(span):
            half, shift = divmod(ox * SIDE + oy, LANES)
            moved = halves[half]
            if shift:
                other = pltpu.roll(halves[1], LANES - shift, axis=1) if half == 0 else jnp.zeros_like(moved)
                moved = jnp.where(lane < LANES - shift, pltpu.roll(moved, LANES - shift, axis=1), other)
            windows[pl.ds((ox * span + oy) * 8, 8), :] = moved


def corner_forces(flat, weights, windows):
    window_tables(flat, windows)
    total = jnp.zeros((LANES, weights.shape[2]), F32)
    for c in range(3):
        total = total + jnp.dot(
            windows[pl.ds(c, LANES, stride=8), :], weights[c], precision=HIGHEST, preferred_element_type=F32
        )
    return total


def spread(part, c):
    shape = (LANES, part.shape[1])
    cell = iota(shape, 0)
    row = c * PX * PX + (cell // SIDE) * PX + cell % SIDE
    place = jnp.where((iota(shape, 1) == row) & (cell % SIDE < PX), 1.0, 0.0)
    return lax.dot_general(
        place, part[...], (((1,), (1,)), ((), ())), precision=HIGHEST, preferred_element_type=F32
    )


def prepare_kernel(asked, offset, part, chosen, weights):
    span = SIDE - PX + 1
    shape = (LANES, LANES)
    where = offset[0:1, :] * span + offset[1:2, :]
    corner = jnp.where(iota(shape, 0) == where, 1.0, 0.0)
    lane = iota(shape, 1)
    for r in range(2):
        slot = jnp.where(lane == asked[:, r : r + 1], 1.0, 0.0)
        chosen[pl.ds(r, LANES, stride=2), :] = lax.dot_general(
            slot, corner, (((1,), (1,)), ((), ())), preferred_element_type=F32
        )
    for c in range(3):
        weights[c] = spread(part, c)


def prepare(asked, offset, part):
    modes = part.shape[0]
    return pl.pallas_call(
        prepare_kernel,
        out_shape=(pltpu.VMEM((2 * LANES, LANES), F32), pltpu.VMEM((3, LANES, modes), F32)),
        in_specs=[VMEM_SPEC] * 3,
        out_specs=(VMEM_SPEC,) * 2,
        compiler_params=pltpu.CompilerParams(vmem_limit_bytes=VMEM_BYTES),
        name="prepare",
    )(asked, offset, part)


def early_kernel(top, chosen, weights, early, windows):
    forces = corner_forces(top[...], weights, windows)
    early[...] = jnp.dot(chosen[...], forces, precision=HIGHEST, preferred_element_type=F32)


def early_forces(top, chosen, weights):
    return pl.pallas_call(
        early_kernel,
        out_shape=pltpu.VMEM((2 * LANES, weights.shape[2]), F32),
        in_specs=[VMEM_SPEC] * 3,
        out_specs=VMEM_SPEC,
        scratch_shapes=[pltpu.VMEM((8 * LANES, LANES), F32)],
        compiler_params=pltpu.CompilerParams(vmem_limit_bytes=VMEM_BYTES),
        name="early_forces",
    )(top, chosen, weights)


def near_north_kernel(main, pack, ya, yb, chosen, weights, early, near, ans, rim, ex, ey, windows):
    fill_north(rim, ya, yb)
    add_north(rim, pack, main, near, ex, ey, 0, 1)
    forces = corner_forces(surface_rows(near, 0), weights, windows)
    late = jnp.dot(chosen[...], forces, precision=HIGHEST, preferred_element_type=F32)
    ans[...] = jnp.concatenate([early[...], late], axis=1)


def near_north(main, pack, ya, yb, chosen, weights, early):
    _, rows, cols, _ = main.shape
    return pl.pallas_call(
        near_north_kernel,
        out_shape=(pltpu.VMEM((3, rows, cols, LANES), F32), pltpu.VMEM((2 * LANES, LANES), F32)),
        in_specs=[VMEM_SPEC] * 7,
        out_specs=(VMEM_SPEC,) * 2,
        scratch_shapes=[
            pltpu.VMEM((3, rows + 4, 24, 2 * LANES), F32),
            pltpu.VMEM((rows + 4, 8, 2 * LANES), F32),
            pltpu.VMEM((rows + 4, 8, 2 * LANES), F32),
            pltpu.VMEM((8 * LANES, LANES), F32),
        ],
        compiler_params=pltpu.CompilerParams(vmem_limit_bytes=VMEM_BYTES),
        name="near_north",
    )(main, pack, ya, yb, chosen, weights, early)


def far_north_kernel(main, pack, near, ya, yb, nxt, rim, out, ex, ey, sems):
    stores = started([(near, nxt.at[:, :, :, pl.ds(0, LANES)])], sems.at[pl.ds(0, 1)])
    columns = pl.ds(LANES, out.shape[3] - LANES)

    def done(row, count):
        part = (slice(None), pl.ds(row, count), slice(None), columns)
        stores.extend(started([(out.at[part], nxt.at[part])], sems.at[pl.ds(len(stores), 1)]))

    fill_north(rim, ya, yb)
    add_north(rim, pack, main, out, ex, ey, 1, out.shape[3] // LANES, done=done, parts=4)
    wait_all(stores)


def far_north(main, pack, near, ya, yb):
    _, rows, _, depth = main.shape
    return pl.pallas_call(
        far_north_kernel,
        out_shape=pltpu.HBM(main.shape, F32),
        in_specs=[VMEM_SPEC] * 5,
        out_specs=HBM_SPEC,
        scratch_shapes=[
            pltpu.VMEM((3, rows + 4, 24, depth), F32),
            pltpu.VMEM(main.shape, F32),
            pltpu.VMEM((rows + 4, 8, depth), F32),
            pltpu.VMEM((rows + 4, 8, depth), F32),
            pltpu.SemaphoreType.DMA((5,)),
        ],
        compiler_params=pltpu.CompilerParams(vmem_limit_bytes=VMEM_BYTES),
        name="far_north",
    )(main, pack, near, ya, yb)


def north_kernel(now, xa, xb, ya, yb):
    rows = now.shape[1]
    odd_x, odd_y = parity("gx"), parity("gy")

    def gather(out, edge):
        out[:, 4 : rows + 4] = now[:, :, edge : edge + 2, :]
        for rim, side in ((xa, 1 - odd_x), (xb, odd_x)):
            for c in range(3):
                out[c, pl.ds((rows + 4) * side, 4)] = rim[4 * c : 4 * c + 4, edge : edge + 2, :]

    high = SIDE - 2

    @pl.when(odd_y == 0)
    def _():
        gather(ya, high)
        gather(yb, 0)

    @pl.when(odd_y == 1)
    def _():
        gather(ya, 0)
        gather(yb, high)


def north_edges(now, xa, xb):
    _, rows, _, depth = now.shape
    out = pltpu.VMEM((3, rows + 8, 2, depth), F32)
    return pl.pallas_call(
        north_kernel,
        out_shape=(out, out),
        in_specs=[VMEM_SPEC] * 3,
        out_specs=(VMEM_SPEC, VMEM_SPEC),
        compiler_params=pltpu.CompilerParams(vmem_limit_bytes=VMEM_BYTES),
        name="north_edges",
    )(now, xa, xb)


def build_requests(source, req, pos):
    shape = (LANES, LANES)
    src = source[...]
    tile = src // LANES
    local = (src % LANES).astype(F32)
    mine = jnp.where(iota(shape, 0) == tile, 1.0, 0.0)
    earlier = jnp.where(iota(shape, 0) < iota(shape, 1), 1.0, 0.0)
    before = jnp.dot(mine, earlier, preferred_element_type=F32)
    rank = jnp.sum(before * mine, axis=0, keepdims=True)
    wanted = mine * local
    lane = iota(shape, 1)
    first = jnp.sum(jnp.where(rank == 0.0, wanted, 0.0), axis=1, keepdims=True)
    second = jnp.sum(jnp.where(rank == 1.0, wanted, 0.0), axis=1, keepdims=True)
    req[...] = jnp.where(lane == 0, first, jnp.where(lane == 1, second, 0.0)).astype(jnp.int32)
    pos[...] = tile * 2 + jnp.minimum(rank, 1.0).astype(jnp.int32)


def columns_of(ker):
    taps = ker.shape[0]
    same = jnp.where(iota((taps, taps), 0) == iota((taps, taps), 1), 1.0, 0.0)
    return lax.dot_general(
        ker[...], same, (((0,), (0,)), ((), ())), precision=HIGHEST, preferred_element_type=F32
    )


def history_kernel(hist, ker, out):
    k = columns_of(ker)
    steps = hist.shape[0]
    half = hist.shape[1] // 2
    for part in range(2):
        rows = pl.ds(part * half, half)
        kp = k[part * half : (part + 1) * half]
        first = jnp.zeros((half, LANES), F32)
        second = jnp.zeros((half, LANES), F32)
        for h in range(steps):
            past = hist[h, rows, :]
            first = first + kp[:, steps - h : steps - h + 1] * past
            if h > 0:
                second = second + kp[:, steps + 1 - h : steps + 2 - h] * past
        out[0, rows, :] = first
        out[1, rows, :] = second


def history_part(hist, ker):
    return pl.pallas_call(
        history_kernel,
        out_shape=pltpu.VMEM((2,) + hist.shape[1:], F32),
        in_specs=[VMEM_SPEC, VMEM_SPEC],
        out_specs=VMEM_SPEC,
        compiler_params=pltpu.CompilerParams(vmem_limit_bytes=VMEM_BYTES),
        name="history",
    )(hist, ker)


def response_kernel(ans, pos, count, base, ker, out):
    at = pos[...]
    chosen = jnp.where(iota((2 * LANES, LANES), 0) == at, 1.0, 0.0)
    forces = lax.dot_general(
        ans[...], chosen, (((0,), (0,)), ((), ())), precision=HIGHEST, preferred_element_type=F32
    )
    k = columns_of(ker)
    modes = k.shape[0]
    early, late = forces[:modes], forces[modes:]
    live = iota((1, LANES), 1) < count[...]
    out[0] = jnp.where(live, base[0] + k[:, 0:1] * early, 0.0)
    out[1] = jnp.where(live, base[1] + k[:, 0:1] * late + k[:, 1:2] * early, 0.0)


def make_responses(ans, pos, count, base, ker):
    return pl.pallas_call(
        response_kernel,
        out_shape=jax.ShapeDtypeStruct(base.shape, F32),
        in_specs=[VMEM_SPEC] * 5,
        out_specs=VMEM_SPEC,
        compiler_params=pltpu.CompilerParams(vmem_limit_bytes=VMEM_BYTES),
        name="responses",
    )(ans, pos, count.reshape(1, 1), base, ker)


def swap(array, axis, first):
    pairs = []
    for low in range(first, lax.axis_size(axis) - 1, 2):
        pairs += [(low, low + 1), (low + 1, low)]
    return in_vmem(lax.ppermute(array, axis, pairs))


def east_swaps(xa, xb):
    return swap(xa, "gx", 0), swap(xb, "gx", 1)


def north_swaps(ya, yb):
    return swap(ya, "gy", 0), swap(yb, "gy", 1)


def per_device(
    disp_prev,
    disp_now,
    buoyancy,
    shear_mod,
    lame_first,
    foot_offset,
    owner_source,
    owner_count,
    force_history,
    participation,
    kernels,
):
    return steps(
        disp_prev,
        disp_now,
        tuple(in_hbm(a) for a in (buoyancy, shear_mod, lame_first)),
        foot_offset.T,
        owner_source,
        owner_count,
        force_history,
        participation.T,
        kernels.T,
    )


def exchange(array):
    rows = array.reshape(LANES, -1, LANES)
    out = lax.all_to_all(rows, ("gx", "gy"), split_axis=0, concat_axis=0, tiled=True)
    return out.reshape(array.shape)


def steps(prev, now, medium, offset, source, count, history, part, kernels):
    held = in_vmem(now)
    pa, pb, req, pos = east_pack(
        in_hbm(now), in_hbm(prev), *medium, in_hbm(source.reshape(1, LANES))
    )
    east = east_swaps(in_vmem(pa), in_vmem(pb))
    asked = exchange(req)
    north = north_edges(held, *east)
    north = north_swaps(*north)
    prepared = prepare(in_vmem(asked), offset, part)
    main = first_main(held, *east, in_hbm(prev), *medium)
    north, main, prepared = lax.optimization_barrier((north, main, prepared))
    mid, ya, yb, top = first_north(*main, *north)
    north = north_swaps(ya, yb)
    early = early_forces(top, *prepared)
    disp_mid, main, pack = second_main(mid, in_hbm(now), *medium)
    north, main, pack, early = lax.optimization_barrier((north, main, pack, early))
    near, ans = near_north(main, pack, *north, *prepared, early)
    back = exchange(ans)
    base = in_vmem(history_part(history, kernels))
    disp_next = far_north(in_vmem(main), in_vmem(pack), in_vmem(near), *(in_vmem(a) for a in north))
    responses = make_responses(back, in_vmem(pos), count, base, kernels)
    return disp_mid, disp_next, responses


def solution(mesh):
    return jax.shard_map(
        per_device,
        mesh=mesh,
        in_specs=(
            P(None, "gx", "gy", None),
            P(None, "gx", "gy", None),
            P("gx", "gy", None),
            P("gx", "gy", None),
            P("gx", "gy", None),
            P(("gx", "gy"), None),
            P(("gx", "gy")),
            P(("gx", "gy")),
            P(None, None, ("gx", "gy")),
            P(),
            P(),
        ),
        out_specs=(
            P(None, "gx", "gy", None),
            P(None, "gx", "gy", None),
            P(None, None, ("gx", "gy")),
        ),
        check_vma=False,
    )
```

```python
import jax
import jax.numpy as jnp
from jax import lax
from jax.experimental import pallas as pl
from jax.experimental.pallas import tpu as pltpu
from jax.sharding import PartitionSpec as P


PX = 8
SIDE = 16
LANES = 128
HIGHEST = lax.Precision.HIGHEST
F32 = jnp.float32
VMEM_BYTES = 16 << 20

VMEM_SPEC = pl.BlockSpec(memory_space=pltpu.VMEM)
HBM_SPEC = pl.BlockSpec(memory_space=pltpu.HBM)
SMEM_SPEC = pl.BlockSpec(memory_space=pltpu.SMEM)


def iota(shape, axis):
    return lax.broadcasted_iota(jnp.int32, shape, axis)


def in_vmem(array):
    return pltpu.with_memory_space_constraint(array, pltpu.VMEM)


def in_hbm(array):
    return pltpu.with_memory_space_constraint(array, pltpu.HBM)


def parity(axis):
    return lax.axis_index(axis) % 2


def first_of(a1, b1, a2, b2):
    return (a1 - b1) - (a2 - b2) * 0.125


def second_of(a1, b1, a2, b2):
    return (a1 + b1) - (a2 + b2) * 0.0625


def z_four(below, columns, above):
    lane = iota(columns[0].shape, 1)
    zero = jnp.zeros_like(columns[0])
    count = len(columns)
    out = [[] for _ in columns]
    for s in (1, -1, 2, -2):
        turned = [pltpu.roll(c, (-s) % LANES, axis=1) for c in columns]
        if s > 0:
            turned.append(zero if above is None else pltpu.roll(above, LANES - s, axis=1))
        else:
            turned.insert(0, zero if below is None else pltpu.roll(below, -s, axis=1))
        for k in range(count):
            if s > 0:
                out[k].append(jnp.where(lane < LANES - s, turned[k], turned[k + 1]))
            else:
                out[k].append(jnp.where(lane >= -s, turned[k + 1], turned[k]))
    return out


def z_first(below, columns, above):
    return [first_of(*four) for four in z_four(below, columns, above)]


def north_four(lower, upper):
    sub = iota(lower.shape, 0)
    zero = jnp.zeros_like(lower)
    out = ([], [])
    for s in (1, -1, 2, -2):
        first, second = [pltpu.roll(tile, (-s) % 8, axis=0) for tile in (lower, upper)]
        if s > 0:
            out[0].append(jnp.where(sub < 8 - s, first, second))
            out[1].append(jnp.where(sub < 8 - s, second, zero))
        else:
            out[0].append(jnp.where(sub >= -s, first, zero))
            out[1].append(jnp.where(sub >= -s, second, first))
    return out


def run_step(vp, prev, buoy, mu, lam, out, pack, work, ready):
    byx, syz, dyy, dyz, qyx, qyy, qyz, qzz = work
    rows = vp.shape[1] - 4
    span = range(vp.shape[3] // LANES)
    lanes = lambda k: pl.ds(k * LANES, LANES)
    tile = lambda h: pl.ds(8 * h, 8)

    def inner(r, full):
        i = r - 2
        for h in range(2):
            four = z_four(None, [vp[2, r, tile(h), lanes(k)] for k in span], None)
            for k in span:
                syz[r, tile(h), lanes(k)] = first_of(*four[k])
                if full:
                    qzz[i, tile(h), lanes(k)] = second_of(*four[k])
        for k in span:
            for c in range(3 if full else 2):
                four = north_four(*[vp[c, r, tile(h), lanes(k)] for h in range(2)])
                for h in range(2):
                    slope = first_of(*four[h])
                    if c == 0:
                        byx[r, tile(h), lanes(k)] = slope
                    elif c == 1:
                        syz[r, tile(h), lanes(k)] = syz[r, tile(h), lanes(k)] + slope
                    if full:
                        if c > 0:
                            (dyy, dyz)[c - 1][i, tile(h), lanes(k)] = slope
                        (qyx, qyy, qyz)[c][i, tile(h), lanes(k)] = second_of(*four[h])

    def each(start, stop, full):
        def trip(r, carry):
            inner(r, full)
            return carry

        lax.fori_loop(start, stop, trip, 0)

    each(0, 2, False)
    each(2, rows + 2, True)
    each(rows + 2, rows + 4, False)
    ready()

    def outer(i, carry):
        r = i + 2
        low = iota((8, LANES), 0) < 4
        lower = {}
        for h in range(2):
            here = tile(h)

            def x_four(c, k):
                return [vp[c, r + d, here, lanes(k)] for d in (1, -1, 2, -2)]

            def derived(ref, k):
                return first_of(*[ref[r + d, here, lanes(k)] for d in (1, -1, 2, -2)])

            yz = z_first(None, [dyz[i, here, lanes(k)] for k in span], None)
            xy = z_first(None, [first_of(*x_four(0, k)) + dyy[i, here, lanes(k)] for k in span], None)
            along_z = [z_four(None, [vp[c, r, here, lanes(k)] for k in span], None) for c in range(2)]
            for k in span:
                shear = mu[i, here, lanes(k)]
                both = lam[i, here, lanes(k)] + shear
                scale = buoy[i, here, lanes(k)] * 0.12
                for which, factor in enumerate((shear, both, scale)):
                    if h == 0:
                        lower[which, k] = factor
                    else:
                        pack[which, i, :, lanes(k)] = jnp.where(low, lower[which, k], factor)
                mixed = [derived(syz, k), derived(byx, k) + yz[k], xy[k]]
                for c in range(3):
                    centre = vp[c, r, here, lanes(k)]
                    q = [
                        second_of(*x_four(c, k)),
                        (qyx, qyy, qyz)[c][i, here, lanes(k)],
                        second_of(*along_z[c][k]) if c < 2 else qzz[i, here, lanes(k)],
                    ]
                    laplace = (q[0] + q[1]) + (q[2] - centre * 5.625)
                    along = (q[c] - centre * 1.875) + mixed[c] * (1.0 / 3.0)
                    update = shear * laplace + both * along
                    out[c, i, here, lanes(k)] = (2.0 * centre - prev[c, i, here, lanes(k)]) + scale * update
        return carry

    lax.fori_loop(0, rows, outer, 0)


def step_work(rows, cols, depth):
    return [pltpu.VMEM((rows + 4, cols, depth), F32)] * 2 + [pltpu.VMEM((rows, cols, depth), F32)] * 6


def surface_rows(field, first):
    cells = SIDE * SIDE
    flat = jnp.zeros((8, cells), F32)
    for c in range(3):
        pick = jnp.where((iota((8, LANES), 0) == first + c) & (iota((8, LANES), 1) == 0), 1.0, 0.0)
        flat = flat + lax.dot_general(
            pick,
            field[c, :, :, 0:LANES].reshape(cells, LANES),
            (((1,), (1,)), ((), ())),
            precision=HIGHEST,
            preferred_element_type=F32,
        )
    return flat


def started(pairs, sems):
    copies = [pltpu.make_async_copy(src, dst, sems.at[n]) for n, (src, dst) in enumerate(pairs)]
    for copy in copies:
        copy.start()
    return copies


def wait_all(copies):
    for copy in copies:
        copy.wait()


def east_pack_kernel(now, prev, buoy, mu, lam, source, pa, pb, req, pos, held, sems):
    rows = now.shape[1]
    odd = parity("gx")
    pairs = []
    for out, side in ((pa, 1 - odd), (pb, odd)):
        four = pl.ds((rows - 4) * side, 4)
        two = pl.ds((rows - 2) * side, 2)
        for c in range(3):
            pairs.append((now.at[c, four], out.at[pl.ds(4 * c, 4)]))
            pairs.append((prev.at[c, two], out.at[pl.ds(12 + 2 * c, 2)]))
        for n, field in enumerate((buoy, mu, lam)):
            pairs.append((field.at[two], out.at[pl.ds(18 + 2 * n, 2)]))
    copies = started([(source, held)] + pairs, sems)
    copies[0].wait()
    build_requests(held, req, pos)
    wait_all(copies[1:])


def east_pack(now, prev, buoy, mu, lam, source):
    _, _, cols, depth = now.shape
    out = pltpu.VMEM((24, cols, depth), F32)
    return pl.pallas_call(
        east_pack_kernel,
        out_shape=(
            out,
            out,
            jax.ShapeDtypeStruct((LANES, LANES), jnp.int32),
            pltpu.VMEM((1, LANES), jnp.int32),
        ),
        in_specs=[HBM_SPEC] * 6,
        out_specs=(VMEM_SPEC,) * 4,
        scratch_shapes=[pltpu.VMEM((1, LANES), jnp.int32), pltpu.SemaphoreType.DMA((19,))],
        compiler_params=pltpu.CompilerParams(vmem_limit_bytes=VMEM_BYTES),
        name="east_pack",
    )(now, prev, buoy, mu, lam, source)


def first_main_kernel(prev, buoy, mu, lam, now, xa, xb, out, pack, vp, pv, bv, mv, lv, *work):
    rows = now.shape[1]
    own = pl.ds(2, rows)
    copies = started(
        [(prev, pv.at[:, own])] + [(src, dst.at[own]) for src, dst in ((buoy, bv), (mu, mv), (lam, lv))],
        work[-1],
    )
    odd = parity("gx")
    vp[:, 4 : rows + 4] = now[...]
    for edge, side in ((xa, 1 - odd), (xb, odd)):
        four = pl.ds((rows + 4) * side, 4)
        two = pl.ds((rows + 2) * side, 2)
        for c in range(3):
            vp[c, four] = edge[4 * c : 4 * c + 4]
            pv[c, two] = edge[12 + 2 * c : 14 + 2 * c]
        for n, field in enumerate((bv, mv, lv)):
            field[two] = edge[18 + 2 * n : 20 + 2 * n]
    run_step(vp, pv, bv, mv, lv, out, pack, work[:-1], lambda: wait_all(copies))


def first_main(now, xa, xb, prev, buoy, mu, lam):
    _, rows, cols, depth = now.shape
    wide = rows + 4
    one = pltpu.VMEM((wide, cols, depth), F32)
    return pl.pallas_call(
        first_main_kernel,
        out_shape=(pltpu.VMEM((3, wide, cols, depth), F32), pltpu.VMEM((3, wide, 8, depth), F32)),
        in_specs=[HBM_SPEC] * 4 + [VMEM_SPEC] * 3,
        out_specs=(VMEM_SPEC,) * 2,
        scratch_shapes=[
            pltpu.VMEM((3, wide + 4, cols, depth), F32),
            pltpu.VMEM((3, wide, cols, depth), F32),
            one,
            one,
            one,
            *step_work(wide, cols, depth),
            pltpu.SemaphoreType.DMA((4,)),
        ],
        compiler_params=pltpu.CompilerParams(vmem_limit_bytes=VMEM_BYTES),
        name="first_main",
    )(prev, buoy, mu, lam, now, xa, xb)


def first_north_kernel(main, pack, ya, yb, mid, ma, mb, top, rim, ex, ey):
    rows = main.shape[1] - 4
    fill_north(rim, ya, yb)
    add_north(rim, pack, main, mid, ex, ey, 0, main.shape[3] // LANES)
    odd = parity("gy")

    @pl.when(odd == 0)
    def _():
        ma[...] = mid[:, :, 14:16, :]
        mb[...] = mid[:, :, 0:2, :]

    @pl.when(odd == 1)
    def _():
        ma[...] = mid[:, :, 0:2, :]
        mb[...] = mid[:, :, 14:16, :]

    top[...] = surface_rows(mid.at[:, pl.ds(2, rows)], 0)


def first_north(main, pack, ya, yb):
    _, wide, _, depth = main.shape
    edge = pltpu.VMEM((3, wide, 2, depth), F32)
    return pl.pallas_call(
        first_north_kernel,
        out_shape=(pltpu.VMEM(main.shape, F32), edge, edge, pltpu.VMEM((8, SIDE * SIDE), F32)),
        in_specs=[VMEM_SPEC] * 4,
        out_specs=(VMEM_SPEC,) * 4,
        scratch_shapes=[
            pltpu.VMEM((3, wide + 4, 24, depth), F32),
            pltpu.VMEM((wide + 4, 8, depth), F32),
            pltpu.VMEM((wide + 4, 8, depth), F32),
        ],
        compiler_params=pltpu.CompilerParams(vmem_limit_bytes=VMEM_BYTES),
        name="first_north",
    )(main, pack, ya, yb)


def second_main_kernel(prev, buoy, mu, lam, vp, mid, out, pack, pv, bv, mv, lv, *work):
    sems = work[-1]
    rows = prev.shape[1]
    copies = started([(prev, pv), (buoy, bv), (mu, mv), (lam, lv)], sems)
    stores = started([(vp.at[:, pl.ds(2, rows)], mid)], sems.at[pl.ds(4, 1)])
    run_step(vp, pv, bv, mv, lv, out, pack, work[:-1], lambda: wait_all(copies))
    wait_all(stores)


def second_main(v, prev, buoy, mu, lam):
    _, rows, cols, depth = prev.shape
    whole = pltpu.VMEM(prev.shape, F32)
    one = pltpu.VMEM((rows, cols, depth), F32)
    return pl.pallas_call(
        second_main_kernel,
        out_shape=(pltpu.HBM(prev.shape, F32), whole, pltpu.VMEM((3, rows, 8, depth), F32)),
        in_specs=[HBM_SPEC] * 4 + [VMEM_SPEC],
        out_specs=(HBM_SPEC,) + (VMEM_SPEC,) * 2,
        scratch_shapes=[
            whole,
            one,
            one,
            one,
            *step_work(rows, cols, depth),
            pltpu.SemaphoreType.DMA((5,)),
        ],
        compiler_params=pltpu.CompilerParams(vmem_limit_bytes=VMEM_BYTES),
        name="second_main",
    )(prev, buoy, mu, lam, v)


def fill_north(rim, ya, yb):
    odd_y = parity("gy")
    rim[:, :, 8:16, :] = jnp.zeros((rim.shape[0], rim.shape[1], 8, rim.shape[3]), F32)

    wide = rim.shape[3]

    @pl.when(odd_y == 0)
    def _():
        rim[:, :, 6:8, :] = yb[:, :, :, :wide]
        rim[:, :, 16:18, :] = ya[:, :, :, :wide]

    @pl.when(odd_y == 1)
    def _():
        rim[:, :, 6:8, :] = ya[:, :, :, :wide]
        rim[:, :, 16:18, :] = yb[:, :, :, :wide]


def add_north(rim, pack, main, out, ex, ey, first, last, base=0, done=None, parts=1):
    rows = rim.shape[1] - 4
    total = 3
    span = range(first, last)
    lanes = lambda k: pl.ds(k * LANES, LANES)
    local = lambda k: pl.ds((k - base) * LANES, LANES)
    below, above = max(first - 1, 0), min(last + 1, total)

    def y_four(c, r, k):
        return [rim[c, r, pl.ds(8 + d, 8), lanes(k)] for d in (1, -1, 2, -2)]

    def ends(get):
        return (
            get(first - 1) if first > 0 else None,
            [get(k) for k in span],
            get(last) if last < total else None,
        )

    def inner(r):
        for k in range(below, above):
            ey[r, :, lanes(k)] = first_of(*y_four(1, r, k))
        for k in span:
            ex[r, :, lanes(k)] = first_of(*y_four(0, r, k))

    def inner_two(pair, carry):
        inner(2 * pair)
        inner(2 * pair + 1)
        return carry

    lax.fori_loop(0, (rows + 4) // 2, inner_two, 0)

    def outer(i):
        r = i + 2
        yz = z_first(*ends(lambda k: first_of(*y_four(2, r, k))))
        xy = z_first(*ends(lambda k: ey[r, :, lanes(k)]))
        low = iota((8, LANES), 0) < 4
        for n, k in enumerate(span):

            def derived(ref):
                return first_of(*[ref[r + d, :, lanes(k)] for d in (1, -1, 2, -2)])

            shear, both, scale = [pack[which, i, :, local(k)] for which in range(3)]
            mixed = [derived(ey), derived(ex) + yz[n], xy[n]]
            for c in range(3):
                q = second_of(*y_four(c, r, k))
                along = mixed[c] * (1.0 / 3.0)
                if c == 1:
                    along = along + q
                update = scale * (shear * q + both * along)
                out[c, i, 0:8, local(k)] = main[c, i, 0:8, local(k)] + jnp.where(low, update, 0.0)
                out[c, i, 8:16, local(k)] = main[c, i, 8:16, local(k)] + jnp.where(low, 0.0, update)

    def outer_two(pair, carry):
        outer(2 * pair)
        outer(2 * pair + 1)
        return carry

    count = rows // 2 // parts
    for part in range(parts):
        lax.fori_loop(part * count, (part + 1) * count, outer_two, 0)
        if done is not None:
            done(2 * part * count, 2 * count)


def window_tables(flat, windows):
    span = SIDE - PX + 1
    halves = [flat[:, :LANES], flat[:, LANES:]]
    lane = iota((8, LANES), 1)
    windows[span * span * 8 :, :] = jnp.zeros((windows.shape[0] - span * span * 8, LANES), F32)
    for ox in range(span):
        for oy in range(span):
            half, shift = divmod(ox * SIDE + oy, LANES)
            moved = halves[half]
            if shift:
                other = pltpu.roll(halves[1], LANES - shift, axis=1) if half == 0 else jnp.zeros_like(moved)
                moved = jnp.where(lane < LANES - shift, pltpu.roll(moved, LANES - shift, axis=1), other)
            windows[pl.ds((ox * span + oy) * 8, 8), :] = moved


def corner_forces(flat, weights, windows):
    window_tables(flat, windows)
    total = jnp.zeros((LANES, weights.shape[2]), F32)
    for c in range(3):
        total = total + jnp.dot(
            windows[pl.ds(c, LANES, stride=8), :], weights[c], precision=HIGHEST, preferred_element_type=F32
        )
    return total


def spread(part, c):
    shape = (LANES, part.shape[1])
    cell = iota(shape, 0)
    row = c * PX * PX + (cell // SIDE) * PX + cell % SIDE
    place = jnp.where((iota(shape, 1) == row) & (cell % SIDE < PX), 1.0, 0.0)
    return lax.dot_general(
        place, part[...], (((1,), (1,)), ((), ())), precision=HIGHEST, preferred_element_type=F32
    )


def prepare_kernel(asked, offset, part, chosen, weights):
    span = SIDE - PX + 1
    shape = (LANES, LANES)
    where = offset[0:1, :] * span + offset[1:2, :]
    corner = jnp.where(iota(shape, 0) == where, 1.0, 0.0)
    lane = iota(shape, 1)
    for r in range(2):
        slot = jnp.where(lane == asked[:, r : r + 1], 1.0, 0.0)
        chosen[pl.ds(r, LANES, stride=2), :] = lax.dot_general(
            slot, corner, (((1,), (1,)), ((), ())), preferred_element_type=F32
        )
    for c in range(3):
        weights[c] = spread(part, c)


def prepare(asked, offset, part):
    modes = part.shape[0]
    return pl.pallas_call(
        prepare_kernel,
        out_shape=(pltpu.VMEM((2 * LANES, LANES), F32), pltpu.VMEM((3, LANES, modes), F32)),
        in_specs=[VMEM_SPEC] * 3,
        out_specs=(VMEM_SPEC,) * 2,
        compiler_params=pltpu.CompilerParams(vmem_limit_bytes=VMEM_BYTES),
        name="prepare",
    )(asked, offset, part)


def early_kernel(top, chosen, weights, early, windows):
    forces = corner_forces(top[...], weights, windows)
    early[...] = jnp.dot(chosen[...], forces, precision=HIGHEST, preferred_element_type=F32)


def early_forces(top, chosen, weights):
    return pl.pallas_call(
        early_kernel,
        out_shape=pltpu.VMEM((2 * LANES, weights.shape[2]), F32),
        in_specs=[VMEM_SPEC] * 3,
        out_specs=VMEM_SPEC,
        scratch_shapes=[pltpu.VMEM((8 * LANES, LANES), F32)],
        compiler_params=pltpu.CompilerParams(vmem_limit_bytes=VMEM_BYTES),
        name="early_forces",
    )(top, chosen, weights)


def near_north_kernel(main, pack, ya, yb, chosen, weights, early, near, ans, rim, ex, ey, windows):
    fill_north(rim, ya, yb)
    add_north(rim, pack, main, near, ex, ey, 0, 1)
    forces = corner_forces(surface_rows(near, 0), weights, windows)
    late = jnp.dot(chosen[...], forces, precision=HIGHEST, preferred_element_type=F32)
    ans[...] = jnp.concatenate([early[...], late], axis=1)


def near_north(main, pack, ya, yb, chosen, weights, early):
    _, rows, cols, _ = main.shape
    return pl.pallas_call(
        near_north_kernel,
        out_shape=(pltpu.VMEM((3, rows, cols, LANES), F32), pltpu.VMEM((2 * LANES, LANES), F32)),
        in_specs=[VMEM_SPEC] * 7,
        out_specs=(VMEM_SPEC,) * 2,
        scratch_shapes=[
            pltpu.VMEM((3, rows + 4, 24, 2 * LANES), F32),
            pltpu.VMEM((rows + 4, 8, 2 * LANES), F32),
            pltpu.VMEM((rows + 4, 8, 2 * LANES), F32),
            pltpu.VMEM((8 * LANES, LANES), F32),
        ],
        compiler_params=pltpu.CompilerParams(vmem_limit_bytes=VMEM_BYTES),
        name="near_north",
    )(main, pack, ya, yb, chosen, weights, early)


def far_north_kernel(main, pack, near, ya, yb, nxt, rim, out, ex, ey, sems):
    stores = started([(near, nxt.at[:, :, :, pl.ds(0, LANES)])], sems.at[pl.ds(0, 1)])
    columns = pl.ds(LANES, out.shape[3] - LANES)

    def done(row, count):
        part = (slice(None), pl.ds(row, count), slice(None), columns)
        stores.extend(started([(out.at[part], nxt.at[part])], sems.at[pl.ds(len(stores), 1)]))

    fill_north(rim, ya, yb)
    add_north(rim, pack, main, out, ex, ey, 1, out.shape[3] // LANES, done=done, parts=4)
    wait_all(stores)


def far_north(main, pack, near, ya, yb):
    _, rows, _, depth = main.shape
    return pl.pallas_call(
        far_north_kernel,
        out_shape=pltpu.HBM(main.shape, F32),
        in_specs=[VMEM_SPEC] * 5,
        out_specs=HBM_SPEC,
        scratch_shapes=[
            pltpu.VMEM((3, rows + 4, 24, depth), F32),
            pltpu.VMEM(main.shape, F32),
            pltpu.VMEM((rows + 4, 8, depth), F32),
            pltpu.VMEM((rows + 4, 8, depth), F32),
            pltpu.SemaphoreType.DMA((5,)),
        ],
        compiler_params=pltpu.CompilerParams(vmem_limit_bytes=VMEM_BYTES),
        name="far_north",
    )(main, pack, near, ya, yb)


def north_kernel(now, xa, xb, ya, yb):
    rows = now.shape[1]
    odd_x, odd_y = parity("gx"), parity("gy")

    def gather(out, edge):
        out[:, 4 : rows + 4] = now[:, :, edge : edge + 2, :]
        for rim, side in ((xa, 1 - odd_x), (xb, odd_x)):
            for c in range(3):
                out[c, pl.ds((rows + 4) * side, 4)] = rim[4 * c : 4 * c + 4, edge : edge + 2, :]

    high = SIDE - 2

    @pl.when(odd_y == 0)
    def _():
        gather(ya, high)
        gather(yb, 0)

    @pl.when(odd_y == 1)
    def _():
        gather(ya, 0)
        gather(yb, high)


def north_edges(now, xa, xb):
    _, rows, _, depth = now.shape
    out = pltpu.VMEM((3, rows + 8, 2, depth), F32)
    return pl.pallas_call(
        north_kernel,
        out_shape=(out, out),
        in_specs=[VMEM_SPEC] * 3,
        out_specs=(VMEM_SPEC, VMEM_SPEC),
        compiler_params=pltpu.CompilerParams(vmem_limit_bytes=VMEM_BYTES),
        name="north_edges",
    )(now, xa, xb)


def build_requests(source, req, pos):
    shape = (LANES, LANES)
    src = source[...]
    tile = src // LANES
    local = (src % LANES).astype(F32)
    mine = jnp.where(iota(shape, 0) == tile, 1.0, 0.0)
    earlier = jnp.where(iota(shape, 0) < iota(shape, 1), 1.0, 0.0)
    before = jnp.dot(mine, earlier, preferred_element_type=F32)
    rank = jnp.sum(before * mine, axis=0, keepdims=True)
    wanted = mine * local
    lane = iota(shape, 1)
    first = jnp.sum(jnp.where(rank == 0.0, wanted, 0.0), axis=1, keepdims=True)
    second = jnp.sum(jnp.where(rank == 1.0, wanted, 0.0), axis=1, keepdims=True)
    req[...] = jnp.where(lane == 0, first, jnp.where(lane == 1, second, 0.0)).astype(jnp.int32)
    pos[...] = tile * 2 + jnp.minimum(rank, 1.0).astype(jnp.int32)


def columns_of(ker):
    taps = ker.shape[0]
    same = jnp.where(iota((taps, taps), 0) == iota((taps, taps), 1), 1.0, 0.0)
    return lax.dot_general(
        ker[...], same, (((0,), (0,)), ((), ())), precision=HIGHEST, preferred_element_type=F32
    )


def history_kernel(hist, ker, out):
    k = columns_of(ker)
    steps = hist.shape[0]
    half = hist.shape[1] // 2
    for part in range(2):
        rows = pl.ds(part * half, half)
        kp = k[part * half : (part + 1) * half]
        first = jnp.zeros((half, LANES), F32)
        second = jnp.zeros((half, LANES), F32)
        for h in range(steps):
            past = hist[h, rows, :]
            first = first + kp[:, steps - h : steps - h + 1] * past
            if h > 0:
                second = second + kp[:, steps + 1 - h : steps + 2 - h] * past
        out[0, rows, :] = first
        out[1, rows, :] = second


def history_part(hist, ker):
    return pl.pallas_call(
        history_kernel,
        out_shape=pltpu.VMEM((2,) + hist.shape[1:], F32),
        in_specs=[VMEM_SPEC, VMEM_SPEC],
        out_specs=VMEM_SPEC,
        compiler_params=pltpu.CompilerParams(vmem_limit_bytes=VMEM_BYTES),
        name="history",
    )(hist, ker)


def response_kernel(ans, pos, count, base, ker, out):
    at = pos[...]
    chosen = jnp.where(iota((2 * LANES, LANES), 0) == at, 1.0, 0.0)
    forces = lax.dot_general(
        ans[...], chosen, (((0,), (0,)), ((), ())), precision=HIGHEST, preferred_element_type=F32
    )
    k = columns_of(ker)
    modes = k.shape[0]
    early, late = forces[:modes], forces[modes:]
    live = iota((1, LANES), 1) < count[...]
    out[0] = jnp.where(live, base[0] + k[:, 0:1] * early, 0.0)
    out[1] = jnp.where(live, base[1] + k[:, 0:1] * late + k[:, 1:2] * early, 0.0)


def make_responses(ans, pos, count, base, ker):
    return pl.pallas_call(
        response_kernel,
        out_shape=jax.ShapeDtypeStruct(base.shape, F32),
        in_specs=[VMEM_SPEC] * 5,
        out_specs=VMEM_SPEC,
        compiler_params=pltpu.CompilerParams(vmem_limit_bytes=VMEM_BYTES),
        name="responses",
    )(ans, pos, count.reshape(1, 1), base, ker)


def swap(array, axis, first):
    pairs = []
    for low in range(first, lax.axis_size(axis) - 1, 2):
        pairs += [(low, low + 1), (low + 1, low)]
    return in_vmem(lax.ppermute(array, axis, pairs))


def east_swaps(xa, xb):
    return swap(xa, "gx", 0), swap(xb, "gx", 1)


def north_swaps(ya, yb):
    return swap(ya, "gy", 0), swap(yb, "gy", 1)


def per_device(
    disp_prev,
    disp_now,
    buoyancy,
    shear_mod,
    lame_first,
    foot_offset,
    owner_source,
    owner_count,
    force_history,
    participation,
    kernels,
):
    return steps(
        disp_prev,
        disp_now,
        tuple(in_hbm(a) for a in (buoyancy, shear_mod, lame_first)),
        foot_offset.T,
        owner_source,
        owner_count,
        force_history,
        participation.T,
        kernels.T,
    )


def exchange(array, place=lambda rows: rows):
    rows = place(array.reshape(LANES, -1, LANES))
    out = lax.all_to_all(rows, ("gx", "gy"), split_axis=0, concat_axis=0)
    return out.reshape(array.shape)


def steps(prev, now, medium, offset, source, count, history, part, kernels):
    held = in_vmem(now)
    pa, pb, req, pos = east_pack(
        in_hbm(now), in_hbm(prev), *medium, in_hbm(source.reshape(1, LANES))
    )
    east = east_swaps(in_vmem(pa), in_vmem(pb))
    asked = exchange(req)
    north = north_edges(held, *east)
    north = north_swaps(*north)
    prepared = prepare(in_vmem(asked), offset, part)
    main = first_main(held, *east, in_hbm(prev), *medium)
    north, main, prepared = lax.optimization_barrier((north, main, prepared))
    mid, ya, yb, top = first_north(*main, *north)
    north = north_swaps(ya, yb)
    early = early_forces(top, *prepared)
    disp_mid, main, pack = second_main(mid, in_hbm(now), *medium)
    north, main, pack, early = lax.optimization_barrier((north, main, pack, early))
    near, ans = near_north(main, pack, *north, *prepared, early)
    back = exchange(ans)
    base = in_vmem(history_part(history, kernels))
    disp_next = far_north(in_vmem(main), in_vmem(pack), in_vmem(near), *(in_vmem(a) for a in north))
    responses = make_responses(back, in_vmem(pos), count, base, kernels)
    return disp_mid, disp_next, responses


def solution(mesh):
    return jax.shard_map(
        per_device,
        mesh=mesh,
        in_specs=(
            P(None, "gx", "gy", None),
            P(None, "gx", "gy", None),
            P("gx", "gy", None),
            P("gx", "gy", None),
            P("gx", "gy", None),
            P(("gx", "gy"), None),
            P(("gx", "gy")),
            P(("gx", "gy")),
            P(None, None, ("gx", "gy")),
            P(),
            P(),
        ),
        out_specs=(
            P(None, "gx", "gy", None),
            P(None, "gx", "gy", None),
            P(None, None, ("gx", "gy")),
        ),
        check_vma=False,
    )
```

```python
import jax
import jax.numpy as jnp
from jax import lax
from jax.experimental import pallas as pl
from jax.experimental.pallas import tpu as pltpu
from jax.sharding import PartitionSpec as P


PX = 8
SIDE = 16
LANES = 128
HIGHEST = lax.Precision.HIGHEST
F32 = jnp.float32
VMEM_BYTES = 16 << 20

VMEM_SPEC = pl.BlockSpec(memory_space=pltpu.VMEM)
HBM_SPEC = pl.BlockSpec(memory_space=pltpu.HBM)
SMEM_SPEC = pl.BlockSpec(memory_space=pltpu.SMEM)


def iota(shape, axis):
    return lax.broadcasted_iota(jnp.int32, shape, axis)


def in_vmem(array):
    return pltpu.with_memory_space_constraint(array, pltpu.VMEM)


def in_hbm(array):
    return pltpu.with_memory_space_constraint(array, pltpu.HBM)


def parity(axis):
    return lax.axis_index(axis) % 2


def first_of(a1, b1, a2, b2):
    return (a1 - b1) - (a2 - b2) * 0.125


def second_of(a1, b1, a2, b2):
    return (a1 + b1) - (a2 + b2) * 0.0625


def z_four(below, columns, above):
    lane = iota(columns[0].shape, 1)
    zero = jnp.zeros_like(columns[0])
    count = len(columns)
    out = [[] for _ in columns]
    for s in (1, -1, 2, -2):
        turned = [pltpu.roll(c, (-s) % LANES, axis=1) for c in columns]
        if s > 0:
            turned.append(zero if above is None else pltpu.roll(above, LANES - s, axis=1))
        else:
            turned.insert(0, zero if below is None else pltpu.roll(below, -s, axis=1))
        for k in range(count):
            if s > 0:
                out[k].append(jnp.where(lane < LANES - s, turned[k], turned[k + 1]))
            else:
                out[k].append(jnp.where(lane >= -s, turned[k + 1], turned[k]))
    return out


def z_first(below, columns, above):
    return [first_of(*four) for four in z_four(below, columns, above)]


def north_four(lower, upper):
    sub = iota(lower.shape, 0)
    zero = jnp.zeros_like(lower)
    out = ([], [])
    for s in (1, -1, 2, -2):
        first, second = [pltpu.roll(tile, (-s) % 8, axis=0) for tile in (lower, upper)]
        if s > 0:
            out[0].append(jnp.where(sub < 8 - s, first, second))
            out[1].append(jnp.where(sub < 8 - s, second, zero))
        else:
            out[0].append(jnp.where(sub >= -s, first, zero))
            out[1].append(jnp.where(sub >= -s, second, first))
    return out


def run_step(vp, prev, buoy, mu, lam, out, pack, work, ready):
    byx, syz, dyy, dyz, qyx, qyy, qyz, qzz = work
    rows = vp.shape[1] - 4
    span = range(vp.shape[3] // LANES)
    lanes = lambda k: pl.ds(k * LANES, LANES)
    tile = lambda h: pl.ds(8 * h, 8)

    def inner(r, full):
        i = r - 2
        for h in range(2):
            four = z_four(None, [vp[2, r, tile(h), lanes(k)] for k in span], None)
            for k in span:
                syz[r, tile(h), lanes(k)] = first_of(*four[k])
                if full:
                    qzz[i, tile(h), lanes(k)] = second_of(*four[k])
        for k in span:
            for c in range(3 if full else 2):
                four = north_four(*[vp[c, r, tile(h), lanes(k)] for h in range(2)])
                for h in range(2):
                    slope = first_of(*four[h])
                    if c == 0:
                        byx[r, tile(h), lanes(k)] = slope
                    elif c == 1:
                        syz[r, tile(h), lanes(k)] = syz[r, tile(h), lanes(k)] + slope
                    if full:
                        if c > 0:
                            (dyy, dyz)[c - 1][i, tile(h), lanes(k)] = slope
                        (qyx, qyy, qyz)[c][i, tile(h), lanes(k)] = second_of(*four[h])

    def each(start, stop, full):
        def trip(r, carry):
            inner(r, full)
            return carry

        lax.fori_loop(start, stop, trip, 0)

    each(0, 2, False)
    each(2, rows + 2, True)
    each(rows + 2, rows + 4, False)
    ready()

    def outer(i, carry):
        r = i + 2
        low = iota((8, LANES), 0) < 4
        lower = {}
        for h in range(2):
            here = tile(h)

            def x_four(c, k):
                return [vp[c, r + d, here, lanes(k)] for d in (1, -1, 2, -2)]

            def derived(ref, k):
                return first_of(*[ref[r + d, here, lanes(k)] for d in (1, -1, 2, -2)])

            yz = z_first(None, [dyz[i, here, lanes(k)] for k in span], None)
            xy = z_first(None, [first_of(*x_four(0, k)) + dyy[i, here, lanes(k)] for k in span], None)
            along_z = [z_four(None, [vp[c, r, here, lanes(k)] for k in span], None) for c in range(2)]
            for k in span:
                shear = mu[i, here, lanes(k)]
                both = lam[i, here, lanes(k)] + shear
                scale = buoy[i, here, lanes(k)] * 0.12
                for which, factor in enumerate((shear, both, scale)):
                    if h == 0:
                        lower[which, k] = factor
                    else:
                        pack[which, i, :, lanes(k)] = jnp.where(low, lower[which, k], factor)
                mixed = [derived(syz, k), derived(byx, k) + yz[k], xy[k]]
                for c in range(3):
                    centre = vp[c, r, here, lanes(k)]
                    q = [
                        second_of(*x_four(c, k)),
                        (qyx, qyy, qyz)[c][i, here, lanes(k)],
                        second_of(*along_z[c][k]) if c < 2 else qzz[i, here, lanes(k)],
                    ]
                    laplace = (q[0] + q[1]) + (q[2] - centre * 5.625)
                    along = (q[c] - centre * 1.875) + mixed[c] * (1.0 / 3.0)
                    update = shear * laplace + both * along
                    out[c, i, here, lanes(k)] = (2.0 * centre - prev[c, i, here, lanes(k)]) + scale * update
        return carry

    lax.fori_loop(0, rows, outer, 0)


def step_work(rows, cols, depth):
    return [pltpu.VMEM((rows + 4, cols, depth), F32)] * 2 + [pltpu.VMEM((rows, cols, depth), F32)] * 6


def surface_rows(field, first):
    cells = SIDE * SIDE
    flat = jnp.zeros((8, cells), F32)
    for c in range(3):
        pick = jnp.where((iota((8, LANES), 0) == first + c) & (iota((8, LANES), 1) == 0), 1.0, 0.0)
        flat = flat + lax.dot_general(
            pick,
            field[c, :, :, 0:LANES].reshape(cells, LANES),
            (((1,), (1,)), ((), ())),
            precision=HIGHEST,
            preferred_element_type=F32,
        )
    return flat


def started(pairs, sems):
    copies = [pltpu.make_async_copy(src, dst, sems.at[n]) for n, (src, dst) in enumerate(pairs)]
    for copy in copies:
        copy.start()
    return copies


def wait_all(copies):
    for copy in copies:
        copy.wait()


def east_pack_kernel(now, prev, buoy, mu, lam, source, pa, pb, held, sems):
    rows = now.shape[1]
    odd = parity("gx")
    pairs = []
    for out, side in ((pa, 1 - odd), (pb, odd)):
        four = pl.ds((rows - 4) * side, 4)
        two = pl.ds((rows - 2) * side, 2)
        for c in range(3):
            pairs.append((now.at[c, four], out.at[pl.ds(4 * c, 4)]))
            pairs.append((prev.at[c, two], out.at[pl.ds(12 + 2 * c, 2)]))
        for n, field in enumerate((buoy, mu, lam)):
            pairs.append((field.at[two], out.at[pl.ds(18 + 2 * n, 2)]))
    wait_all(started(pairs + [(source, held)], sems))


def east_pack(now, prev, buoy, mu, lam, source):
    _, _, cols, depth = now.shape
    out = pltpu.VMEM((24, cols, depth), F32)
    return pl.pallas_call(
        east_pack_kernel,
        out_shape=(
            out,
            out,
            pltpu.VMEM((1, LANES), jnp.int32),
        ),
        in_specs=[HBM_SPEC] * 6,
        out_specs=(VMEM_SPEC,) * 3,
        scratch_shapes=[pltpu.SemaphoreType.DMA((19,))],
        compiler_params=pltpu.CompilerParams(vmem_limit_bytes=VMEM_BYTES),
        name="east_pack",
    )(now, prev, buoy, mu, lam, source)


def first_main_kernel(prev, buoy, mu, lam, now, xa, xb, out, pack, vp, pv, bv, mv, lv, *work):
    rows = now.shape[1]
    own = pl.ds(2, rows)
    copies = started(
        [(prev, pv.at[:, own])] + [(src, dst.at[own]) for src, dst in ((buoy, bv), (mu, mv), (lam, lv))],
        work[-1],
    )
    odd = parity("gx")
    vp[:, 4 : rows + 4] = now[...]
    for edge, side in ((xa, 1 - odd), (xb, odd)):
        four = pl.ds((rows + 4) * side, 4)
        two = pl.ds((rows + 2) * side, 2)
        for c in range(3):
            vp[c, four] = edge[4 * c : 4 * c + 4]
            pv[c, two] = edge[12 + 2 * c : 14 + 2 * c]
        for n, field in enumerate((bv, mv, lv)):
            field[two] = edge[18 + 2 * n : 20 + 2 * n]
    run_step(vp, pv, bv, mv, lv, out, pack, work[:-1], lambda: wait_all(copies))


def first_main(now, xa, xb, prev, buoy, mu, lam):
    _, rows, cols, depth = now.shape
    wide = rows + 4
    one = pltpu.VMEM((wide, cols, depth), F32)
    return pl.pallas_call(
        first_main_kernel,
        out_shape=(pltpu.VMEM((3, wide, cols, depth), F32), pltpu.VMEM((3, wide, 8, depth), F32)),
        in_specs=[HBM_SPEC] * 4 + [VMEM_SPEC] * 3,
        out_specs=(VMEM_SPEC,) * 2,
        scratch_shapes=[
            pltpu.VMEM((3, wide + 4, cols, depth), F32),
            pltpu.VMEM((3, wide, cols, depth), F32),
            one,
            one,
            one,
            *step_work(wide, cols, depth),
            pltpu.SemaphoreType.DMA((4,)),
        ],
        compiler_params=pltpu.CompilerParams(vmem_limit_bytes=VMEM_BYTES),
        name="first_main",
    )(prev, buoy, mu, lam, now, xa, xb)


def first_north_kernel(main, pack, ya, yb, mid, ma, mb, top, rim, ex, ey):
    rows = main.shape[1] - 4
    fill_north(rim, ya, yb)
    add_north(rim, pack, main, mid, ex, ey, 0, main.shape[3] // LANES)
    odd = parity("gy")

    @pl.when(odd == 0)
    def _():
        ma[...] = mid[:, :, 14:16, :]
        mb[...] = mid[:, :, 0:2, :]

    @pl.when(odd == 1)
    def _():
        ma[...] = mid[:, :, 0:2, :]
        mb[...] = mid[:, :, 14:16, :]

    top[...] = surface_rows(mid.at[:, pl.ds(2, rows)], 0)


def first_north(main, pack, ya, yb):
    _, wide, _, depth = main.shape
    edge = pltpu.VMEM((3, wide, 2, depth), F32)
    return pl.pallas_call(
        first_north_kernel,
        out_shape=(pltpu.VMEM(main.shape, F32), edge, edge, pltpu.VMEM((8, SIDE * SIDE), F32)),
        in_specs=[VMEM_SPEC] * 4,
        out_specs=(VMEM_SPEC,) * 4,
        scratch_shapes=[
            pltpu.VMEM((3, wide + 4, 24, depth), F32),
            pltpu.VMEM((wide + 4, 8, depth), F32),
            pltpu.VMEM((wide + 4, 8, depth), F32),
        ],
        compiler_params=pltpu.CompilerParams(vmem_limit_bytes=VMEM_BYTES),
        name="first_north",
    )(main, pack, ya, yb)


def second_main_kernel(prev, buoy, mu, lam, vp, mid, out, pack, pv, bv, mv, lv, *work):
    sems = work[-1]
    rows = prev.shape[1]
    copies = started([(prev, pv), (buoy, bv), (mu, mv), (lam, lv)], sems)
    stores = started([(vp.at[:, pl.ds(2, rows)], mid)], sems.at[pl.ds(4, 1)])
    run_step(vp, pv, bv, mv, lv, out, pack, work[:-1], lambda: wait_all(copies))
    wait_all(stores)


def second_main(v, prev, buoy, mu, lam):
    _, rows, cols, depth = prev.shape
    whole = pltpu.VMEM(prev.shape, F32)
    one = pltpu.VMEM((rows, cols, depth), F32)
    return pl.pallas_call(
        second_main_kernel,
        out_shape=(pltpu.HBM(prev.shape, F32), whole, pltpu.VMEM((3, rows, 8, depth), F32)),
        in_specs=[HBM_SPEC] * 4 + [VMEM_SPEC],
        out_specs=(HBM_SPEC,) + (VMEM_SPEC,) * 2,
        scratch_shapes=[
            whole,
            one,
            one,
            one,
            *step_work(rows, cols, depth),
            pltpu.SemaphoreType.DMA((5,)),
        ],
        compiler_params=pltpu.CompilerParams(vmem_limit_bytes=VMEM_BYTES),
        name="second_main",
    )(prev, buoy, mu, lam, v)


def fill_north(rim, ya, yb):
    odd_y = parity("gy")
    rim[:, :, 8:16, :] = jnp.zeros((rim.shape[0], rim.shape[1], 8, rim.shape[3]), F32)

    wide = rim.shape[3]

    @pl.when(odd_y == 0)
    def _():
        rim[:, :, 6:8, :] = yb[:, :, :, :wide]
        rim[:, :, 16:18, :] = ya[:, :, :, :wide]

    @pl.when(odd_y == 1)
    def _():
        rim[:, :, 6:8, :] = ya[:, :, :, :wide]
        rim[:, :, 16:18, :] = yb[:, :, :, :wide]


def add_north(rim, pack, main, out, ex, ey, first, last, base=0, done=None, parts=1):
    rows = rim.shape[1] - 4
    total = 3
    span = range(first, last)
    lanes = lambda k: pl.ds(k * LANES, LANES)
    local = lambda k: pl.ds((k - base) * LANES, LANES)
    below, above = max(first - 1, 0), min(last + 1, total)

    def y_four(c, r, k):
        return [rim[c, r, pl.ds(8 + d, 8), lanes(k)] for d in (1, -1, 2, -2)]

    def ends(get):
        return (
            get(first - 1) if first > 0 else None,
            [get(k) for k in span],
            get(last) if last < total else None,
        )

    def inner(r):
        for k in range(below, above):
            ey[r, :, lanes(k)] = first_of(*y_four(1, r, k))
        for k in span:
            ex[r, :, lanes(k)] = first_of(*y_four(0, r, k))

    def inner_two(pair, carry):
        inner(2 * pair)
        inner(2 * pair + 1)
        return carry

    lax.fori_loop(0, (rows + 4) // 2, inner_two, 0)

    def outer(i):
        r = i + 2
        yz = z_first(*ends(lambda k: first_of(*y_four(2, r, k))))
        xy = z_first(*ends(lambda k: ey[r, :, lanes(k)]))
        low = iota((8, LANES), 0) < 4
        for n, k in enumerate(span):

            def derived(ref):
                return first_of(*[ref[r + d, :, lanes(k)] for d in (1, -1, 2, -2)])

            shear, both, scale = [pack[which, i, :, local(k)] for which in range(3)]
            mixed = [derived(ey), derived(ex) + yz[n], xy[n]]
            for c in range(3):
                q = second_of(*y_four(c, r, k))
                along = mixed[c] * (1.0 / 3.0)
                if c == 1:
                    along = along + q
                update = scale * (shear * q + both * along)
                out[c, i, 0:8, local(k)] = main[c, i, 0:8, local(k)] + jnp.where(low, update, 0.0)
                out[c, i, 8:16, local(k)] = main[c, i, 8:16, local(k)] + jnp.where(low, 0.0, update)

    def outer_two(pair, carry):
        outer(2 * pair)
        outer(2 * pair + 1)
        return carry

    count = rows // 2 // parts
    for part in range(parts):
        lax.fori_loop(part * count, (part + 1) * count, outer_two, 0)
        if done is not None:
            done(2 * part * count, 2 * count)


def window_tables(flat, windows):
    span = SIDE - PX + 1
    halves = [flat[:, :LANES], flat[:, LANES:]]
    lane = iota((8, LANES), 1)
    windows[span * span * 8 :, :] = jnp.zeros((windows.shape[0] - span * span * 8, LANES), F32)
    for ox in range(span):
        for oy in range(span):
            half, shift = divmod(ox * SIDE + oy, LANES)
            moved = halves[half]
            if shift:
                other = pltpu.roll(halves[1], LANES - shift, axis=1) if half == 0 else jnp.zeros_like(moved)
                moved = jnp.where(lane < LANES - shift, pltpu.roll(moved, LANES - shift, axis=1), other)
            windows[pl.ds((ox * span + oy) * 8, 8), :] = moved


def corner_forces(flat, weights, windows):
    window_tables(flat, windows)
    total = jnp.zeros((LANES, weights.shape[2]), F32)
    for c in range(3):
        total = total + jnp.dot(
            windows[pl.ds(c, LANES, stride=8), :], weights[c], precision=HIGHEST, preferred_element_type=F32
        )
    return total


def spread(part, c):
    shape = (LANES, part.shape[1])
    cell = iota(shape, 0)
    row = c * PX * PX + (cell // SIDE) * PX + cell % SIDE
    place = jnp.where((iota(shape, 1) == row) & (cell % SIDE < PX), 1.0, 0.0)
    return lax.dot_general(
        place, part[...], (((1,), (1,)), ((), ())), precision=HIGHEST, preferred_element_type=F32
    )


def prepare_kernel(asked, offset, part, chosen, weights):
    span = SIDE - PX + 1
    shape = (LANES, LANES)
    where = offset[0:1, :] * span + offset[1:2, :]
    corner = jnp.where(iota(shape, 0) == where, 1.0, 0.0)
    lane = iota(shape, 1)
    for r in range(2):
        slot = jnp.where(lane == asked[:, r : r + 1], 1.0, 0.0)
        chosen[pl.ds(r, LANES, stride=2), :] = lax.dot_general(
            slot, corner, (((1,), (1,)), ((), ())), preferred_element_type=F32
        )
    for c in range(3):
        weights[c] = spread(part, c)


def prepare(asked, offset, part):
    modes = part.shape[0]
    return pl.pallas_call(
        prepare_kernel,
        out_shape=(pltpu.VMEM((2 * LANES, LANES), F32), pltpu.VMEM((3, LANES, modes), F32)),
        in_specs=[VMEM_SPEC] * 3,
        out_specs=(VMEM_SPEC,) * 2,
        compiler_params=pltpu.CompilerParams(vmem_limit_bytes=VMEM_BYTES),
        name="prepare",
    )(asked, offset, part)


def early_kernel(top, chosen, weights, early, windows):
    forces = corner_forces(top[...], weights, windows)
    early[...] = jnp.dot(chosen[...], forces, precision=HIGHEST, preferred_element_type=F32)


def early_forces(top, chosen, weights):
    return pl.pallas_call(
        early_kernel,
        out_shape=pltpu.VMEM((2 * LANES, weights.shape[2]), F32),
        in_specs=[VMEM_SPEC] * 3,
        out_specs=VMEM_SPEC,
        scratch_shapes=[pltpu.VMEM((8 * LANES, LANES), F32)],
        compiler_params=pltpu.CompilerParams(vmem_limit_bytes=VMEM_BYTES),
        name="early_forces",
    )(top, chosen, weights)


def near_north_kernel(main, pack, ya, yb, chosen, weights, early, near, ans, rim, ex, ey, windows):
    fill_north(rim, ya, yb)
    add_north(rim, pack, main, near, ex, ey, 0, 1)
    forces = corner_forces(surface_rows(near, 0), weights, windows)
    late = jnp.dot(chosen[...], forces, precision=HIGHEST, preferred_element_type=F32)
    ans[...] = jnp.concatenate([early[...], late], axis=1)


def near_north(main, pack, ya, yb, chosen, weights, early):
    _, rows, cols, _ = main.shape
    return pl.pallas_call(
        near_north_kernel,
        out_shape=(pltpu.VMEM((3, rows, cols, LANES), F32), pltpu.VMEM((2 * LANES, LANES), F32)),
        in_specs=[VMEM_SPEC] * 7,
        out_specs=(VMEM_SPEC,) * 2,
        scratch_shapes=[
            pltpu.VMEM((3, rows + 4, 24, 2 * LANES), F32),
            pltpu.VMEM((rows + 4, 8, 2 * LANES), F32),
            pltpu.VMEM((rows + 4, 8, 2 * LANES), F32),
            pltpu.VMEM((8 * LANES, LANES), F32),
        ],
        compiler_params=pltpu.CompilerParams(vmem_limit_bytes=VMEM_BYTES),
        name="near_north",
    )(main, pack, ya, yb, chosen, weights, early)


def far_north_kernel(main, pack, near, ya, yb, nxt, rim, out, ex, ey, sems):
    stores = started([(near, nxt.at[:, :, :, pl.ds(0, LANES)])], sems.at[pl.ds(0, 1)])
    columns = pl.ds(LANES, out.shape[3] - LANES)

    def done(row, count):
        part = (slice(None), pl.ds(row, count), slice(None), columns)
        stores.extend(started([(out.at[part], nxt.at[part])], sems.at[pl.ds(len(stores), 1)]))

    fill_north(rim, ya, yb)
    add_north(rim, pack, main, out, ex, ey, 1, out.shape[3] // LANES, done=done, parts=4)
    wait_all(stores)


def far_north(main, pack, near, ya, yb):
    _, rows, _, depth = main.shape
    return pl.pallas_call(
        far_north_kernel,
        out_shape=pltpu.HBM(main.shape, F32),
        in_specs=[VMEM_SPEC] * 5,
        out_specs=HBM_SPEC,
        scratch_shapes=[
            pltpu.VMEM((3, rows + 4, 24, depth), F32),
            pltpu.VMEM(main.shape, F32),
            pltpu.VMEM((rows + 4, 8, depth), F32),
            pltpu.VMEM((rows + 4, 8, depth), F32),
            pltpu.SemaphoreType.DMA((5,)),
        ],
        compiler_params=pltpu.CompilerParams(vmem_limit_bytes=VMEM_BYTES),
        name="far_north",
    )(main, pack, near, ya, yb)


def north_kernel(now, xa, xb, ya, yb):
    rows = now.shape[1]
    odd_x, odd_y = parity("gx"), parity("gy")

    def gather(out, edge):
        out[:, 4 : rows + 4] = now[:, :, edge : edge + 2, :]
        for rim, side in ((xa, 1 - odd_x), (xb, odd_x)):
            for c in range(3):
                out[c, pl.ds((rows + 4) * side, 4)] = rim[4 * c : 4 * c + 4, edge : edge + 2, :]

    high = SIDE - 2

    @pl.when(odd_y == 0)
    def _():
        gather(ya, high)
        gather(yb, 0)

    @pl.when(odd_y == 1)
    def _():
        gather(ya, 0)
        gather(yb, high)


def north_edges(now, xa, xb):
    _, rows, _, depth = now.shape
    out = pltpu.VMEM((3, rows + 8, 2, depth), F32)
    return pl.pallas_call(
        north_kernel,
        out_shape=(out, out),
        in_specs=[VMEM_SPEC] * 3,
        out_specs=(VMEM_SPEC, VMEM_SPEC),
        compiler_params=pltpu.CompilerParams(vmem_limit_bytes=VMEM_BYTES),
        name="north_edges",
    )(now, xa, xb)


def request_kernel(source, req, pos):
    shape = (LANES, LANES)
    src = source[...]
    tile = src // LANES
    local = (src % LANES).astype(F32)
    mine = jnp.where(iota(shape, 0) == tile, 1.0, 0.0)
    earlier = jnp.where(iota(shape, 0) < iota(shape, 1), 1.0, 0.0)
    before = jnp.dot(mine, earlier, preferred_element_type=F32)
    rank = jnp.sum(before * mine, axis=0, keepdims=True)
    wanted = mine * local
    lane = iota(shape, 1)
    first = jnp.sum(jnp.where(rank == 0.0, wanted, 0.0), axis=1, keepdims=True)
    second = jnp.sum(jnp.where(rank == 1.0, wanted, 0.0), axis=1, keepdims=True)
    req[...] = jnp.where(lane == 0, first, jnp.where(lane == 1, second, 0.0)).astype(jnp.int32)
    pos[...] = tile * 2 + jnp.minimum(rank, 1.0).astype(jnp.int32)


def make_requests(source):
    return pl.pallas_call(
        request_kernel,
        out_shape=(pltpu.VMEM((LANES, LANES), jnp.int32), pltpu.VMEM((1, LANES), jnp.int32)),
        in_specs=[VMEM_SPEC],
        out_specs=(VMEM_SPEC,) * 2,
        compiler_params=pltpu.CompilerParams(vmem_limit_bytes=VMEM_BYTES),
        name="requests",
    )(source)


def columns_of(ker):
    taps = ker.shape[0]
    same = jnp.where(iota((taps, taps), 0) == iota((taps, taps), 1), 1.0, 0.0)
    return lax.dot_general(
        ker[...], same, (((0,), (0,)), ((), ())), precision=HIGHEST, preferred_element_type=F32
    )


def history_kernel(hist, ker, out):
    k = columns_of(ker)
    steps = hist.shape[0]
    half = hist.shape[1] // 2
    for part in range(2):
        rows = pl.ds(part * half, half)
        kp = k[part * half : (part + 1) * half]
        first = jnp.zeros((half, LANES), F32)
        second = jnp.zeros((half, LANES), F32)
        for h in range(steps):
            past = hist[h, rows, :]
            first = first + kp[:, steps - h : steps - h + 1] * past
            if h > 0:
                second = second + kp[:, steps + 1 - h : steps + 2 - h] * past
        out[0, rows, :] = first
        out[1, rows, :] = second


def history_part(hist, ker):
    return pl.pallas_call(
        history_kernel,
        out_shape=pltpu.VMEM((2,) + hist.shape[1:], F32),
        in_specs=[VMEM_SPEC, VMEM_SPEC],
        out_specs=VMEM_SPEC,
        compiler_params=pltpu.CompilerParams(vmem_limit_bytes=VMEM_BYTES),
        name="history",
    )(hist, ker)


def response_kernel(ans, pos, count, base, ker, out):
    at = pos[...]
    chosen = jnp.where(iota((2 * LANES, LANES), 0) == at, 1.0, 0.0)
    forces = lax.dot_general(
        ans[...], chosen, (((0,), (0,)), ((), ())), precision=HIGHEST, preferred_element_type=F32
    )
    k = columns_of(ker)
    modes = k.shape[0]
    early, late = forces[:modes], forces[modes:]
    live = iota((1, LANES), 1) < count[...]
    out[0] = jnp.where(live, base[0] + k[:, 0:1] * early, 0.0)
    out[1] = jnp.where(live, base[1] + k[:, 0:1] * late + k[:, 1:2] * early, 0.0)


def make_responses(ans, pos, count, base, ker):
    return pl.pallas_call(
        response_kernel,
        out_shape=jax.ShapeDtypeStruct(base.shape, F32),
        in_specs=[VMEM_SPEC] * 5,
        out_specs=VMEM_SPEC,
        compiler_params=pltpu.CompilerParams(vmem_limit_bytes=VMEM_BYTES),
        name="responses",
    )(ans, pos, count.reshape(1, 1), base, ker)


def swap(array, axis, first):
    pairs = []
    for low in range(first, lax.axis_size(axis) - 1, 2):
        pairs += [(low, low + 1), (low + 1, low)]
    return in_vmem(lax.ppermute(array, axis, pairs))


def east_swaps(xa, xb):
    return swap(xa, "gx", 0), swap(xb, "gx", 1)


def north_swaps(ya, yb):
    return swap(ya, "gy", 0), swap(yb, "gy", 1)


def per_device(
    disp_prev,
    disp_now,
    buoyancy,
    shear_mod,
    lame_first,
    foot_offset,
    owner_source,
    owner_count,
    force_history,
    participation,
    kernels,
):
    return steps(
        disp_prev,
        disp_now,
        tuple(in_hbm(a) for a in (buoyancy, shear_mod, lame_first)),
        foot_offset.T,
        owner_source,
        owner_count,
        force_history,
        participation.T,
        kernels.T,
    )


def exchange(array, place=lambda rows: rows):
    rows = place(array.reshape(LANES, -1, LANES))
    out = lax.all_to_all(rows, ("gx", "gy"), split_axis=0, concat_axis=0)
    return out.reshape(array.shape)


def steps(prev, now, medium, offset, source, count, history, part, kernels):
    held = in_vmem(now)
    pa, pb, slots = east_pack(
        in_hbm(now), in_hbm(prev), *medium, in_hbm(source.reshape(1, LANES))
    )
    east = east_swaps(in_vmem(pa), in_vmem(pb))
    req, pos = make_requests(in_vmem(slots))
    asked = exchange(req)
    north = north_edges(held, *east)
    north = north_swaps(*north)
    main = first_main(held, *east, in_hbm(prev), *medium)
    north, main = lax.optimization_barrier((north, main))
    mid, ya, yb, top = first_north(*main, *north)
    north = north_swaps(ya, yb)
    prepared = prepare(in_vmem(asked), offset, part)
    early = early_forces(top, *prepared)
    disp_mid, main, pack = second_main(mid, in_hbm(now), *medium)
    north, main, pack, early = lax.optimization_barrier((north, main, pack, early))
    near, ans = near_north(main, pack, *north, *prepared, early)
    back = exchange(ans)
    base = in_vmem(history_part(history, kernels))
    disp_next = far_north(in_vmem(main), in_vmem(pack), in_vmem(near), *(in_vmem(a) for a in north))
    responses = make_responses(back, in_vmem(pos), count, base, kernels)
    return disp_mid, disp_next, responses


def solution(mesh):
    return jax.shard_map(
        per_device,
        mesh=mesh,
        in_specs=(
            P(None, "gx", "gy", None),
            P(None, "gx", "gy", None),
            P("gx", "gy", None),
            P("gx", "gy", None),
            P("gx", "gy", None),
            P(("gx", "gy"), None),
            P(("gx", "gy")),
            P(("gx", "gy")),
            P(None, None, ("gx", "gy")),
            P(),
            P(),
        ),
        out_specs=(
            P(None, "gx", "gy", None),
            P(None, "gx", "gy", None),
            P(None, None, ("gx", "gy")),
        ),
        check_vma=False,
    )
```

```python
import jax
import jax.numpy as jnp
from jax import lax
from jax.experimental import pallas as pl
from jax.experimental.pallas import tpu as pltpu
from jax.sharding import PartitionSpec as P


PX = 8
SIDE = 16
LANES = 128
HIGHEST = lax.Precision.HIGHEST
F32 = jnp.float32
VMEM_BYTES = 16 << 20

VMEM_SPEC = pl.BlockSpec(memory_space=pltpu.VMEM)
HBM_SPEC = pl.BlockSpec(memory_space=pltpu.HBM)
SMEM_SPEC = pl.BlockSpec(memory_space=pltpu.SMEM)


def iota(shape, axis):
    return lax.broadcasted_iota(jnp.int32, shape, axis)


def in_vmem(array):
    return pltpu.with_memory_space_constraint(array, pltpu.VMEM)


def in_hbm(array):
    return pltpu.with_memory_space_constraint(array, pltpu.HBM)


def parity(axis):
    return lax.axis_index(axis) % 2


def first_of(a1, b1, a2, b2):
    return (a1 - b1) - (a2 - b2) * 0.125


def second_of(a1, b1, a2, b2):
    return (a1 + b1) - (a2 + b2) * 0.0625


def z_four(below, columns, above):
    lane = iota(columns[0].shape, 1)
    zero = jnp.zeros_like(columns[0])
    count = len(columns)
    out = [[] for _ in columns]
    for s in (1, -1, 2, -2):
        turned = [pltpu.roll(c, (-s) % LANES, axis=1) for c in columns]
        if s > 0:
            turned.append(zero if above is None else pltpu.roll(above, LANES - s, axis=1))
        else:
            turned.insert(0, zero if below is None else pltpu.roll(below, -s, axis=1))
        for k in range(count):
            if s > 0:
                out[k].append(jnp.where(lane < LANES - s, turned[k], turned[k + 1]))
            else:
                out[k].append(jnp.where(lane >= -s, turned[k + 1], turned[k]))
    return out


def z_first(below, columns, above):
    return [first_of(*four) for four in z_four(below, columns, above)]


def north_four(lower, upper):
    sub = iota(lower.shape, 0)
    zero = jnp.zeros_like(lower)
    out = ([], [])
    for s in (1, -1, 2, -2):
        first, second = [pltpu.roll(tile, (-s) % 8, axis=0) for tile in (lower, upper)]
        if s > 0:
            out[0].append(jnp.where(sub < 8 - s, first, second))
            out[1].append(jnp.where(sub < 8 - s, second, zero))
        else:
            out[0].append(jnp.where(sub >= -s, first, zero))
            out[1].append(jnp.where(sub >= -s, second, first))
    return out


def run_step(vp, prev, buoy, mu, lam, out, pack, work, ready):
    byx, syz, dyy, dyz, qyx, qyy, qyz, qzz = work
    rows = vp.shape[1] - 4
    span = range(vp.shape[3] // LANES)
    lanes = lambda k: pl.ds(k * LANES, LANES)
    tile = lambda h: pl.ds(8 * h, 8)

    def inner(r, full):
        i = r - 2
        for h in range(2):
            four = z_four(None, [vp[2, r, tile(h), lanes(k)] for k in span], None)
            for k in span:
                syz[r, tile(h), lanes(k)] = first_of(*four[k])
                if full:
                    qzz[i, tile(h), lanes(k)] = second_of(*four[k])
        for k in span:
            for c in range(3 if full else 2):
                four = north_four(*[vp[c, r, tile(h), lanes(k)] for h in range(2)])
                for h in range(2):
                    slope = first_of(*four[h])
                    if c == 0:
                        byx[r, tile(h), lanes(k)] = slope
                    elif c == 1:
                        syz[r, tile(h), lanes(k)] = syz[r, tile(h), lanes(k)] + slope
                    if full:
                        if c > 0:
                            (dyy, dyz)[c - 1][i, tile(h), lanes(k)] = slope
                        (qyx, qyy, qyz)[c][i, tile(h), lanes(k)] = second_of(*four[h])

    def each(start, stop, full):
        def trip(r, carry):
            inner(r, full)
            return carry

        lax.fori_loop(start, stop, trip, 0)

    each(0, 2, False)
    each(2, rows + 2, True)
    each(rows + 2, rows + 4, False)
    ready()

    def outer(i, carry):
        r = i + 2
        low = iota((8, LANES), 0) < 4
        lower = {}
        for h in range(2):
            here = tile(h)

            def x_four(c, k):
                return [vp[c, r + d, here, lanes(k)] for d in (1, -1, 2, -2)]

            def derived(ref, k):
                return first_of(*[ref[r + d, here, lanes(k)] for d in (1, -1, 2, -2)])

            yz = z_first(None, [dyz[i, here, lanes(k)] for k in span], None)
            xy = z_first(None, [first_of(*x_four(0, k)) + dyy[i, here, lanes(k)] for k in span], None)
            along_z = [z_four(None, [vp[c, r, here, lanes(k)] for k in span], None) for c in range(2)]
            for k in span:
                shear = mu[i, here, lanes(k)]
                both = lam[i, here, lanes(k)] + shear
                scale = buoy[i, here, lanes(k)] * 0.12
                for which, factor in enumerate((shear, both, scale)):
                    if h == 0:
                        lower[which, k] = factor
                    else:
                        pack[which, i, :, lanes(k)] = jnp.where(low, lower[which, k], factor)
                mixed = [derived(syz, k), derived(byx, k) + yz[k], xy[k]]
                for c in range(3):
                    centre = vp[c, r, here, lanes(k)]
                    q = [
                        second_of(*x_four(c, k)),
                        (qyx, qyy, qyz)[c][i, here, lanes(k)],
                        second_of(*along_z[c][k]) if c < 2 else qzz[i, here, lanes(k)],
                    ]
                    laplace = (q[0] + q[1]) + (q[2] - centre * 5.625)
                    along = (q[c] - centre * 1.875) + mixed[c] * (1.0 / 3.0)
                    update = shear * laplace + both * along
                    out[c, i, here, lanes(k)] = (2.0 * centre - prev[c, i, here, lanes(k)]) + scale * update
        return carry

    lax.fori_loop(0, rows, outer, 0)


def step_work(rows, cols, depth):
    return [pltpu.VMEM((rows + 4, cols, depth), F32)] * 2 + [pltpu.VMEM((rows, cols, depth), F32)] * 6


def surface_rows(field, first):
    cells = SIDE * SIDE
    flat = jnp.zeros((8, cells), F32)
    for c in range(3):
        pick = jnp.where((iota((8, LANES), 0) == first + c) & (iota((8, LANES), 1) == 0), 1.0, 0.0)
        flat = flat + lax.dot_general(
            pick,
            field[c, :, :, 0:LANES].reshape(cells, LANES),
            (((1,), (1,)), ((), ())),
            precision=HIGHEST,
            preferred_element_type=F32,
        )
    return flat


def started(pairs, sems):
    copies = [pltpu.make_async_copy(src, dst, sems.at[n]) for n, (src, dst) in enumerate(pairs)]
    for copy in copies:
        copy.start()
    return copies


def wait_all(copies):
    for copy in copies:
        copy.wait()


def east_pack_kernel(now, prev, buoy, mu, lam, source, pa, pb, low, high, req, pos, held, sems):
    rows = now.shape[1]
    odd = parity("gx")
    pairs = []
    for out, side in ((pa, 1 - odd), (pb, odd)):
        four = pl.ds((rows - 4) * side, 4)
        two = pl.ds((rows - 2) * side, 2)
        for c in range(3):
            pairs.append((now.at[c, four], out.at[pl.ds(4 * c, 4)]))
            pairs.append((prev.at[c, two], out.at[pl.ds(12 + 2 * c, 2)]))
        for n, field in enumerate((buoy, mu, lam)):
            pairs.append((field.at[two], out.at[pl.ds(18 + 2 * n, 2)]))
    cols = now.shape[2]
    pairs.append((now.at[:, :, pl.ds(0, 2)], low))
    pairs.append((now.at[:, :, pl.ds(cols - 2, 2)], high))
    copies = started([(source, held)] + pairs, sems)
    copies[0].wait()
    build_requests(held, req, pos)
    wait_all(copies[1:])


def east_pack(now, prev, buoy, mu, lam, source):
    _, rows, cols, depth = now.shape
    out = pltpu.VMEM((24, cols, depth), F32)
    side = pltpu.VMEM((3, rows, 2, depth), F32)
    return pl.pallas_call(
        east_pack_kernel,
        out_shape=(
            out,
            out,
            side,
            side,
            jax.ShapeDtypeStruct((LANES, LANES), jnp.int32),
            pltpu.VMEM((1, LANES), jnp.int32),
        ),
        in_specs=[HBM_SPEC] * 6,
        out_specs=(VMEM_SPEC,) * 6,
        scratch_shapes=[pltpu.VMEM((1, LANES), jnp.int32), pltpu.SemaphoreType.DMA((21,))],
        compiler_params=pltpu.CompilerParams(vmem_limit_bytes=VMEM_BYTES),
        name="east_pack",
    )(now, prev, buoy, mu, lam, source)


def first_main_kernel(prev, buoy, mu, lam, now, xa, xb, out, pack, vp, pv, bv, mv, lv, *work):
    rows = now.shape[1]
    own = pl.ds(2, rows)
    copies = started(
        [(now, vp.at[:, pl.ds(4, rows)]), (prev, pv.at[:, own])] + [(src, dst.at[own]) for src, dst in ((buoy, bv), (mu, mv), (lam, lv))],
        work[-1],
    )
    odd = parity("gx")
    for edge, side in ((xa, 1 - odd), (xb, odd)):
        four = pl.ds((rows + 4) * side, 4)
        two = pl.ds((rows + 2) * side, 2)
        for c in range(3):
            vp[c, four] = edge[4 * c : 4 * c + 4]
            pv[c, two] = edge[12 + 2 * c : 14 + 2 * c]
        for n, field in enumerate((bv, mv, lv)):
            field[two] = edge[18 + 2 * n : 20 + 2 * n]
    copies[0].wait()
    run_step(vp, pv, bv, mv, lv, out, pack, work[:-1], lambda: wait_all(copies[1:]))


def first_main(now, xa, xb, prev, buoy, mu, lam):
    _, rows, cols, depth = now.shape
    wide = rows + 4
    one = pltpu.VMEM((wide, cols, depth), F32)
    return pl.pallas_call(
        first_main_kernel,
        out_shape=(pltpu.VMEM((3, wide, cols, depth), F32), pltpu.VMEM((3, wide, 8, depth), F32)),
        in_specs=[HBM_SPEC] * 5 + [VMEM_SPEC] * 2,
        out_specs=(VMEM_SPEC,) * 2,
        scratch_shapes=[
            pltpu.VMEM((3, wide + 4, cols, depth), F32),
            pltpu.VMEM((3, wide, cols, depth), F32),
            one,
            one,
            one,
            *step_work(wide, cols, depth),
            pltpu.SemaphoreType.DMA((5,)),
        ],
        compiler_params=pltpu.CompilerParams(vmem_limit_bytes=VMEM_BYTES),
        name="first_main",
    )(prev, buoy, mu, lam, now, xa, xb)


def first_north_kernel(main, pack, ya, yb, mid, ma, mb, top, rim, ex, ey):
    rows = main.shape[1] - 4
    fill_north(rim, ya, yb)
    add_north(rim, pack, main, mid, ex, ey, 0, main.shape[3] // LANES)
    odd = parity("gy")

    @pl.when(odd == 0)
    def _():
        ma[...] = mid[:, :, 14:16, :]
        mb[...] = mid[:, :, 0:2, :]

    @pl.when(odd == 1)
    def _():
        ma[...] = mid[:, :, 0:2, :]
        mb[...] = mid[:, :, 14:16, :]

    top[...] = surface_rows(mid.at[:, pl.ds(2, rows)], 0)


def first_north(main, pack, ya, yb):
    _, wide, _, depth = main.shape
    edge = pltpu.VMEM((3, wide, 2, depth), F32)
    return pl.pallas_call(
        first_north_kernel,
        out_shape=(pltpu.VMEM(main.shape, F32), edge, edge, pltpu.VMEM((8, SIDE * SIDE), F32)),
        in_specs=[VMEM_SPEC] * 4,
        out_specs=(VMEM_SPEC,) * 4,
        scratch_shapes=[
            pltpu.VMEM((3, wide + 4, 24, depth), F32),
            pltpu.VMEM((wide + 4, 8, depth), F32),
            pltpu.VMEM((wide + 4, 8, depth), F32),
        ],
        compiler_params=pltpu.CompilerParams(vmem_limit_bytes=VMEM_BYTES),
        name="first_north",
    )(main, pack, ya, yb)


def second_main_kernel(prev, buoy, mu, lam, vp, mid, out, pack, pv, bv, mv, lv, *work):
    sems = work[-1]
    rows = prev.shape[1]
    copies = started([(prev, pv), (buoy, bv), (mu, mv), (lam, lv)], sems)
    stores = started([(vp.at[:, pl.ds(2, rows)], mid)], sems.at[pl.ds(4, 1)])
    run_step(vp, pv, bv, mv, lv, out, pack, work[:-1], lambda: wait_all(copies))
    wait_all(stores)


def second_main(v, prev, buoy, mu, lam):
    _, rows, cols, depth = prev.shape
    whole = pltpu.VMEM(prev.shape, F32)
    one = pltpu.VMEM((rows, cols, depth), F32)
    return pl.pallas_call(
        second_main_kernel,
        out_shape=(pltpu.HBM(prev.shape, F32), whole, pltpu.VMEM((3, rows, 8, depth), F32)),
        in_specs=[HBM_SPEC] * 4 + [VMEM_SPEC],
        out_specs=(HBM_SPEC,) + (VMEM_SPEC,) * 2,
        scratch_shapes=[
            whole,
            one,
            one,
            one,
            *step_work(rows, cols, depth),
            pltpu.SemaphoreType.DMA((5,)),
        ],
        compiler_params=pltpu.CompilerParams(vmem_limit_bytes=VMEM_BYTES),
        name="second_main",
    )(prev, buoy, mu, lam, v)


def fill_north(rim, ya, yb):
    odd_y = parity("gy")
    rim[:, :, 8:16, :] = jnp.zeros((rim.shape[0], rim.shape[1], 8, rim.shape[3]), F32)

    wide = rim.shape[3]

    @pl.when(odd_y == 0)
    def _():
        rim[:, :, 6:8, :] = yb[:, :, :, :wide]
        rim[:, :, 16:18, :] = ya[:, :, :, :wide]

    @pl.when(odd_y == 1)
    def _():
        rim[:, :, 6:8, :] = ya[:, :, :, :wide]
        rim[:, :, 16:18, :] = yb[:, :, :, :wide]


def add_north(rim, pack, main, out, ex, ey, first, last, base=0, done=None, parts=1):
    rows = rim.shape[1] - 4
    total = 3
    span = range(first, last)
    lanes = lambda k: pl.ds(k * LANES, LANES)
    local = lambda k: pl.ds((k - base) * LANES, LANES)
    below, above = max(first - 1, 0), min(last + 1, total)

    def y_four(c, r, k):
        return [rim[c, r, pl.ds(8 + d, 8), lanes(k)] for d in (1, -1, 2, -2)]

    def ends(get):
        return (
            get(first - 1) if first > 0 else None,
            [get(k) for k in span],
            get(last) if last < total else None,
        )

    def inner(r):
        for k in range(below, above):
            ey[r, :, lanes(k)] = first_of(*y_four(1, r, k))
        for k in span:
            ex[r, :, lanes(k)] = first_of(*y_four(0, r, k))

    def inner_two(pair, carry):
        inner(2 * pair)
        inner(2 * pair + 1)
        return carry

    lax.fori_loop(0, (rows + 4) // 2, inner_two, 0)

    def outer(i):
        r = i + 2
        yz = z_first(*ends(lambda k: first_of(*y_four(2, r, k))))
        xy = z_first(*ends(lambda k: ey[r, :, lanes(k)]))
        low = iota((8, LANES), 0) < 4
        for n, k in enumerate(span):

            def derived(ref):
                return first_of(*[ref[r + d, :, lanes(k)] for d in (1, -1, 2, -2)])

            shear, both, scale = [pack[which, i, :, local(k)] for which in range(3)]
            mixed = [derived(ey), derived(ex) + yz[n], xy[n]]
            for c in range(3):
                q = second_of(*y_four(c, r, k))
                along = mixed[c] * (1.0 / 3.0)
                if c == 1:
                    along = along + q
                update = scale * (shear * q + both * along)
                out[c, i, 0:8, local(k)] = main[c, i, 0:8, local(k)] + jnp.where(low, update, 0.0)
                out[c, i, 8:16, local(k)] = main[c, i, 8:16, local(k)] + jnp.where(low, 0.0, update)

    def outer_two(pair, carry):
        outer(2 * pair)
        outer(2 * pair + 1)
        return carry

    count = rows // 2 // parts
    for part in range(parts):
        lax.fori_loop(part * count, (part + 1) * count, outer_two, 0)
        if done is not None:
            done(2 * part * count, 2 * count)


def window_tables(flat, windows):
    span = SIDE - PX + 1
    halves = [flat[:, :LANES], flat[:, LANES:]]
    lane = iota((8, LANES), 1)
    windows[span * span * 8 :, :] = jnp.zeros((windows.shape[0] - span * span * 8, LANES), F32)
    for ox in range(span):
        for oy in range(span):
            half, shift = divmod(ox * SIDE + oy, LANES)
            moved = halves[half]
            if shift:
                other = pltpu.roll(halves[1], LANES - shift, axis=1) if half == 0 else jnp.zeros_like(moved)
                moved = jnp.where(lane < LANES - shift, pltpu.roll(moved, LANES - shift, axis=1), other)
            windows[pl.ds((ox * span + oy) * 8, 8), :] = moved


def corner_forces(flat, weights, windows):
    window_tables(flat, windows)
    total = jnp.zeros((LANES, weights.shape[2]), F32)
    for c in range(3):
        total = total + jnp.dot(
            windows[pl.ds(c, LANES, stride=8), :], weights[c], precision=HIGHEST, preferred_element_type=F32
        )
    return total


def spread(part, c):
    shape = (LANES, part.shape[1])
    cell = iota(shape, 0)
    row = c * PX * PX + (cell // SIDE) * PX + cell % SIDE
    place = jnp.where((iota(shape, 1) == row) & (cell % SIDE < PX), 1.0, 0.0)
    return lax.dot_general(
        place, part[...], (((1,), (1,)), ((), ())), precision=HIGHEST, preferred_element_type=F32
    )


def prepare_kernel(asked, offset, part, chosen, weights):
    span = SIDE - PX + 1
    shape = (LANES, LANES)
    where = offset[0:1, :] * span + offset[1:2, :]
    corner = jnp.where(iota(shape, 0) == where, 1.0, 0.0)
    lane = iota(shape, 1)
    for r in range(2):
        slot = jnp.where(lane == asked[:, r : r + 1], 1.0, 0.0)
        chosen[pl.ds(r, LANES, stride=2), :] = lax.dot_general(
            slot, corner, (((1,), (1,)), ((), ())), preferred_element_type=F32
        )
    for c in range(3):
        weights[c] = spread(part, c)


def prepare(asked, offset, part):
    modes = part.shape[0]
    return pl.pallas_call(
        prepare_kernel,
        out_shape=(pltpu.VMEM((2 * LANES, LANES), F32), pltpu.VMEM((3, LANES, modes), F32)),
        in_specs=[VMEM_SPEC] * 3,
        out_specs=(VMEM_SPEC,) * 2,
        compiler_params=pltpu.CompilerParams(vmem_limit_bytes=VMEM_BYTES),
        name="prepare",
    )(asked, offset, part)


def early_kernel(top, chosen, weights, early, windows):
    forces = corner_forces(top[...], weights, windows)
    early[...] = jnp.dot(chosen[...], forces, precision=HIGHEST, preferred_element_type=F32)


def early_forces(top, chosen, weights):
    return pl.pallas_call(
        early_kernel,
        out_shape=pltpu.VMEM((2 * LANES, weights.shape[2]), F32),
        in_specs=[VMEM_SPEC] * 3,
        out_specs=VMEM_SPEC,
        scratch_shapes=[pltpu.VMEM((8 * LANES, LANES), F32)],
        compiler_params=pltpu.CompilerParams(vmem_limit_bytes=VMEM_BYTES),
        name="early_forces",
    )(top, chosen, weights)


def near_north_kernel(main, pack, ya, yb, chosen, weights, early, near, ans, rim, ex, ey, windows):
    fill_north(rim, ya, yb)
    add_north(rim, pack, main, near, ex, ey, 0, 1)
    forces = corner_forces(surface_rows(near, 0), weights, windows)
    late = jnp.dot(chosen[...], forces, precision=HIGHEST, preferred_element_type=F32)
    ans[...] = jnp.concatenate([early[...], late], axis=1)


def near_north(main, pack, ya, yb, chosen, weights, early):
    _, rows, cols, _ = main.shape
    return pl.pallas_call(
        near_north_kernel,
        out_shape=(pltpu.VMEM((3, rows, cols, LANES), F32), pltpu.VMEM((2 * LANES, LANES), F32)),
        in_specs=[VMEM_SPEC] * 7,
        out_specs=(VMEM_SPEC,) * 2,
        scratch_shapes=[
            pltpu.VMEM((3, rows + 4, 24, 2 * LANES), F32),
            pltpu.VMEM((rows + 4, 8, 2 * LANES), F32),
            pltpu.VMEM((rows + 4, 8, 2 * LANES), F32),
            pltpu.VMEM((8 * LANES, LANES), F32),
        ],
        compiler_params=pltpu.CompilerParams(vmem_limit_bytes=VMEM_BYTES),
        name="near_north",
    )(main, pack, ya, yb, chosen, weights, early)


def far_north_kernel(main, pack, near, ya, yb, nxt, rim, out, ex, ey, sems):
    stores = started([(near, nxt.at[:, :, :, pl.ds(0, LANES)])], sems.at[pl.ds(0, 1)])
    columns = pl.ds(LANES, out.shape[3] - LANES)

    def done(row, count):
        part = (slice(None), pl.ds(row, count), slice(None), columns)
        stores.extend(started([(out.at[part], nxt.at[part])], sems.at[pl.ds(len(stores), 1)]))

    fill_north(rim, ya, yb)
    add_north(rim, pack, main, out, ex, ey, 1, out.shape[3] // LANES, done=done, parts=4)
    wait_all(stores)


def far_north(main, pack, near, ya, yb):
    _, rows, _, depth = main.shape
    return pl.pallas_call(
        far_north_kernel,
        out_shape=pltpu.HBM(main.shape, F32),
        in_specs=[VMEM_SPEC] * 5,
        out_specs=HBM_SPEC,
        scratch_shapes=[
            pltpu.VMEM((3, rows + 4, 24, depth), F32),
            pltpu.VMEM(main.shape, F32),
            pltpu.VMEM((rows + 4, 8, depth), F32),
            pltpu.VMEM((rows + 4, 8, depth), F32),
            pltpu.SemaphoreType.DMA((5,)),
        ],
        compiler_params=pltpu.CompilerParams(vmem_limit_bytes=VMEM_BYTES),
        name="far_north",
    )(main, pack, near, ya, yb)


def north_kernel(low, high, xa, xb, ya, yb):
    rows = low.shape[1]
    odd_x, odd_y = parity("gx"), parity("gy")

    def gather(out, own, edge):
        out[:, 4 : rows + 4] = own[...]
        for rim, side in ((xa, 1 - odd_x), (xb, odd_x)):
            for c in range(3):
                out[c, pl.ds((rows + 4) * side, 4)] = rim[4 * c : 4 * c + 4, edge : edge + 2, :]

    last = SIDE - 2

    @pl.when(odd_y == 0)
    def _():
        gather(ya, high, last)
        gather(yb, low, 0)

    @pl.when(odd_y == 1)
    def _():
        gather(ya, low, 0)
        gather(yb, high, last)


def north_edges(low, high, xa, xb):
    _, rows, two, depth = low.shape
    out = pltpu.VMEM((3, rows + 8, two, depth), F32)
    return pl.pallas_call(
        north_kernel,
        out_shape=(out, out),
        in_specs=[VMEM_SPEC] * 4,
        out_specs=(VMEM_SPEC, VMEM_SPEC),
        compiler_params=pltpu.CompilerParams(vmem_limit_bytes=VMEM_BYTES),
        name="north_edges",
    )(low, high, xa, xb)


def build_requests(source, req, pos):
    shape = (LANES, LANES)
    src = source[...]
    tile = src // LANES
    local = (src % LANES).astype(F32)
    mine = jnp.where(iota(shape, 0) == tile, 1.0, 0.0)
    earlier = jnp.where(iota(shape, 0) < iota(shape, 1), 1.0, 0.0)
    before = jnp.dot(mine, earlier, preferred_element_type=F32)
    rank = jnp.sum(before * mine, axis=0, keepdims=True)
    wanted = mine * local
    lane = iota(shape, 1)
    first = jnp.sum(jnp.where(rank == 0.0, wanted, 0.0), axis=1, keepdims=True)
    second = jnp.sum(jnp.where(rank == 1.0, wanted, 0.0), axis=1, keepdims=True)
    req[...] = jnp.where(lane == 0, first, jnp.where(lane == 1, second, 0.0)).astype(jnp.int32)
    pos[...] = tile * 2 + jnp.minimum(rank, 1.0).astype(jnp.int32)


def columns_of(ker):
    taps = ker.shape[0]
    same = jnp.where(iota((taps, taps), 0) == iota((taps, taps), 1), 1.0, 0.0)
    return lax.dot_general(
        ker[...], same, (((0,), (0,)), ((), ())), precision=HIGHEST, preferred_element_type=F32
    )


def history_kernel(hist, ker, out):
    k = columns_of(ker)
    steps = hist.shape[0]
    half = hist.shape[1] // 2
    for part in range(2):
        rows = pl.ds(part * half, half)
        kp = k[part * half : (part + 1) * half]
        first = jnp.zeros((half, LANES), F32)
        second = jnp.zeros((half, LANES), F32)
        for h in range(steps):
            past = hist[h, rows, :]
            first = first + kp[:, steps - h : steps - h + 1] * past
            if h > 0:
                second = second + kp[:, steps + 1 - h : steps + 2 - h] * past
        out[0, rows, :] = first
        out[1, rows, :] = second


def history_part(hist, ker):
    return pl.pallas_call(
        history_kernel,
        out_shape=pltpu.VMEM((2,) + hist.shape[1:], F32),
        in_specs=[VMEM_SPEC, VMEM_SPEC],
        out_specs=VMEM_SPEC,
        compiler_params=pltpu.CompilerParams(vmem_limit_bytes=VMEM_BYTES),
        name="history",
    )(hist, ker)


def response_kernel(ans, pos, count, base, ker, out):
    at = pos[...]
    chosen = jnp.where(iota((2 * LANES, LANES), 0) == at, 1.0, 0.0)
    forces = lax.dot_general(
        ans[...], chosen, (((0,), (0,)), ((), ())), precision=HIGHEST, preferred_element_type=F32
    )
    k = columns_of(ker)
    modes = k.shape[0]
    early, late = forces[:modes], forces[modes:]
    live = iota((1, LANES), 1) < count[...]
    out[0] = jnp.where(live, base[0] + k[:, 0:1] * early, 0.0)
    out[1] = jnp.where(live, base[1] + k[:, 0:1] * late + k[:, 1:2] * early, 0.0)


def make_responses(ans, pos, count, base, ker):
    return pl.pallas_call(
        response_kernel,
        out_shape=jax.ShapeDtypeStruct(base.shape, F32),
        in_specs=[VMEM_SPEC] * 5,
        out_specs=VMEM_SPEC,
        compiler_params=pltpu.CompilerParams(vmem_limit_bytes=VMEM_BYTES),
        name="responses",
    )(ans, pos, count.reshape(1, 1), base, ker)


def swap(array, axis, first):
    pairs = []
    for low in range(first, lax.axis_size(axis) - 1, 2):
        pairs += [(low, low + 1), (low + 1, low)]
    return in_vmem(lax.ppermute(array, axis, pairs))


def east_swaps(xa, xb):
    return swap(xa, "gx", 0), swap(xb, "gx", 1)


def north_swaps(ya, yb):
    return swap(ya, "gy", 0), swap(yb, "gy", 1)


def per_device(
    disp_prev,
    disp_now,
    buoyancy,
    shear_mod,
    lame_first,
    foot_offset,
    owner_source,
    owner_count,
    force_history,
    participation,
    kernels,
):
    return steps(
        disp_prev,
        disp_now,
        tuple(in_hbm(a) for a in (buoyancy, shear_mod, lame_first)),
        foot_offset.T,
        owner_source,
        owner_count,
        force_history,
        participation.T,
        kernels.T,
    )


def exchange(array, place=lambda rows: rows):
    rows = place(array.reshape(LANES, -1, LANES))
    out = lax.all_to_all(rows, ("gx", "gy"), split_axis=0, concat_axis=0)
    return out.reshape(array.shape)


def steps(prev, now, medium, offset, source, count, history, part, kernels):
    pa, pb, low, high, req, pos = east_pack(
        in_hbm(now), in_hbm(prev), *medium, in_hbm(source.reshape(1, LANES))
    )
    east = east_swaps(in_vmem(pa), in_vmem(pb))
    asked = exchange(req)
    north = north_edges(in_vmem(low), in_vmem(high), *east)
    north = north_swaps(*north)
    main = first_main(in_hbm(now), *east, in_hbm(prev), *medium)
    north, main = lax.optimization_barrier((north, main))
    mid, ya, yb, top = first_north(*main, *north)
    north = north_swaps(ya, yb)
    prepared = prepare(in_vmem(asked), offset, part)
    early = early_forces(top, *prepared)
    disp_mid, main, pack = second_main(mid, in_hbm(now), *medium)
    north, main, pack, early = lax.optimization_barrier((north, main, pack, early))
    near, ans = near_north(main, pack, *north, *prepared, early)
    back = exchange(ans)
    base = in_vmem(history_part(history, kernels))
    disp_next = far_north(in_vmem(main), in_vmem(pack), in_vmem(near), *(in_vmem(a) for a in north))
    responses = make_responses(back, in_vmem(pos), count, base, kernels)
    return disp_mid, disp_next, responses


def solution(mesh):
    return jax.shard_map(
        per_device,
        mesh=mesh,
        in_specs=(
            P(None, "gx", "gy", None),
            P(None, "gx", "gy", None),
            P("gx", "gy", None),
            P("gx", "gy", None),
            P("gx", "gy", None),
            P(("gx", "gy"), None),
            P(("gx", "gy")),
            P(("gx", "gy")),
            P(None, None, ("gx", "gy")),
            P(),
            P(),
        ),
        out_specs=(
            P(None, "gx", "gy", None),
            P(None, "gx", "gy", None),
            P(None, None, ("gx", "gy")),
        ),
        check_vma=False,
    )
```

```python
import jax
import jax.numpy as jnp
from jax import lax
from jax.experimental import pallas as pl
from jax.experimental.pallas import tpu as pltpu
from jax.sharding import PartitionSpec as P


PX = 8
SIDE = 16
LANES = 128
HIGHEST = lax.Precision.HIGHEST
F32 = jnp.float32
VMEM_BYTES = 16 << 20

VMEM_SPEC = pl.BlockSpec(memory_space=pltpu.VMEM)
HBM_SPEC = pl.BlockSpec(memory_space=pltpu.HBM)
SMEM_SPEC = pl.BlockSpec(memory_space=pltpu.SMEM)


def iota(shape, axis):
    return lax.broadcasted_iota(jnp.int32, shape, axis)


def in_vmem(array):
    return pltpu.with_memory_space_constraint(array, pltpu.VMEM)


def in_hbm(array):
    return pltpu.with_memory_space_constraint(array, pltpu.HBM)


def parity(axis):
    return lax.axis_index(axis) % 2


def first_of(a1, b1, a2, b2):
    return (a1 - b1) - (a2 - b2) * 0.125


def second_of(a1, b1, a2, b2):
    return (a1 + b1) - (a2 + b2) * 0.0625


def z_four(below, columns, above):
    lane = iota(columns[0].shape, 1)
    zero = jnp.zeros_like(columns[0])
    count = len(columns)
    out = [[] for _ in columns]
    for s in (1, -1, 2, -2):
        turned = [pltpu.roll(c, (-s) % LANES, axis=1) for c in columns]
        if s > 0:
            turned.append(zero if above is None else pltpu.roll(above, LANES - s, axis=1))
        else:
            turned.insert(0, zero if below is None else pltpu.roll(below, -s, axis=1))
        for k in range(count):
            if s > 0:
                out[k].append(jnp.where(lane < LANES - s, turned[k], turned[k + 1]))
            else:
                out[k].append(jnp.where(lane >= -s, turned[k + 1], turned[k]))
    return out


def z_first(below, columns, above):
    return [first_of(*four) for four in z_four(below, columns, above)]


def north_four(lower, upper):
    sub = iota(lower.shape, 0)
    zero = jnp.zeros_like(lower)
    out = ([], [])
    for s in (1, -1, 2, -2):
        first, second = [pltpu.roll(tile, (-s) % 8, axis=0) for tile in (lower, upper)]
        if s > 0:
            out[0].append(jnp.where(sub < 8 - s, first, second))
            out[1].append(jnp.where(sub < 8 - s, second, zero))
        else:
            out[0].append(jnp.where(sub >= -s, first, zero))
            out[1].append(jnp.where(sub >= -s, second, first))
    return out


def run_step(vp, prev, buoy, mu, lam, out, pack, work, ready):
    byx, syz, dyy, dyz, qyx, qyy, qyz, qzz = work
    rows = vp.shape[1] - 4
    span = range(vp.shape[3] // LANES)
    lanes = lambda k: pl.ds(k * LANES, LANES)
    tile = lambda h: pl.ds(8 * h, 8)

    def inner(r, full):
        i = r - 2
        for h in range(2):
            four = z_four(None, [vp[2, r, tile(h), lanes(k)] for k in span], None)
            for k in span:
                syz[r, tile(h), lanes(k)] = first_of(*four[k])
                if full:
                    qzz[i, tile(h), lanes(k)] = second_of(*four[k])
        for k in span:
            for c in range(3 if full else 2):
                four = north_four(*[vp[c, r, tile(h), lanes(k)] for h in range(2)])
                for h in range(2):
                    slope = first_of(*four[h])
                    if c == 0:
                        byx[r, tile(h), lanes(k)] = slope
                    elif c == 1:
                        syz[r, tile(h), lanes(k)] = syz[r, tile(h), lanes(k)] + slope
                    if full:
                        if c > 0:
                            (dyy, dyz)[c - 1][i, tile(h), lanes(k)] = slope
                        (qyx, qyy, qyz)[c][i, tile(h), lanes(k)] = second_of(*four[h])

    def each(start, stop, full):
        def trip(r, carry):
            inner(r, full)
            return carry

        lax.fori_loop(start, stop, trip, 0)

    each(0, 2, False)
    each(2, rows + 2, True)
    each(rows + 2, rows + 4, False)
    ready()

    def outer(i, carry):
        r = i + 2
        low = iota((8, LANES), 0) < 4
        lower = {}
        for h in range(2):
            here = tile(h)

            def x_four(c, k):
                return [vp[c, r + d, here, lanes(k)] for d in (1, -1, 2, -2)]

            def derived(ref, k):
                return first_of(*[ref[r + d, here, lanes(k)] for d in (1, -1, 2, -2)])

            yz = z_first(None, [dyz[i, here, lanes(k)] for k in span], None)
            xy = z_first(None, [first_of(*x_four(0, k)) + dyy[i, here, lanes(k)] for k in span], None)
            along_z = [z_four(None, [vp[c, r, here, lanes(k)] for k in span], None) for c in range(2)]
            for k in span:
                shear = mu[i, here, lanes(k)]
                both = lam[i, here, lanes(k)] + shear
                scale = buoy[i, here, lanes(k)] * 0.12
                for which, factor in enumerate((shear, both, scale)):
                    if h == 0:
                        lower[which, k] = factor
                    else:
                        pack[which, i, :, lanes(k)] = jnp.where(low, lower[which, k], factor)
                mixed = [derived(syz, k), derived(byx, k) + yz[k], xy[k]]
                for c in range(3):
                    centre = vp[c, r, here, lanes(k)]
                    q = [
                        second_of(*x_four(c, k)),
                        (qyx, qyy, qyz)[c][i, here, lanes(k)],
                        second_of(*along_z[c][k]) if c < 2 else qzz[i, here, lanes(k)],
                    ]
                    laplace = (q[0] + q[1]) + (q[2] - centre * 5.625)
                    along = (q[c] - centre * 1.875) + mixed[c] * (1.0 / 3.0)
                    update = shear * laplace + both * along
                    out[c, i, here, lanes(k)] = (2.0 * centre - prev[c, i, here, lanes(k)]) + scale * update
        return carry

    lax.fori_loop(0, rows, outer, 0)


def step_work(rows, cols, depth):
    return [pltpu.VMEM((rows + 4, cols, depth), F32)] * 2 + [pltpu.VMEM((rows, cols, depth), F32)] * 6


def surface_rows(field, first):
    cells = SIDE * SIDE
    flat = jnp.zeros((8, cells), F32)
    for c in range(3):
        pick = jnp.where((iota((8, LANES), 0) == first + c) & (iota((8, LANES), 1) == 0), 1.0, 0.0)
        flat = flat + lax.dot_general(
            pick,
            field[c, :, :, 0:LANES].reshape(cells, LANES),
            (((1,), (1,)), ((), ())),
            precision=HIGHEST,
            preferred_element_type=F32,
        )
    return flat


def started(pairs, sems):
    copies = [pltpu.make_async_copy(src, dst, sems.at[n]) for n, (src, dst) in enumerate(pairs)]
    for copy in copies:
        copy.start()
    return copies


def wait_all(copies):
    for copy in copies:
        copy.wait()


def east_pack_kernel(now, prev, buoy, mu, lam, source, pa, pb, low, high, req, pos, held, sems):
    rows = now.shape[1]
    odd = parity("gx")
    pairs = []
    for out, side in ((pa, 1 - odd), (pb, odd)):
        four = pl.ds((rows - 4) * side, 4)
        two = pl.ds((rows - 2) * side, 2)
        for c in range(3):
            pairs.append((now.at[c, four], out.at[pl.ds(4 * c, 4)]))
            pairs.append((prev.at[c, two], out.at[pl.ds(12 + 2 * c, 2)]))
        for n, field in enumerate((buoy, mu, lam)):
            pairs.append((field.at[two], out.at[pl.ds(18 + 2 * n, 2)]))
    cols = now.shape[2]
    pairs.append((now.at[:, :, pl.ds(0, 2)], low))
    pairs.append((now.at[:, :, pl.ds(cols - 2, 2)], high))
    copies = started([(source, held)] + pairs, sems)
    copies[0].wait()
    build_requests(held, req, pos)
    wait_all(copies[1:])


def east_pack(now, prev, buoy, mu, lam, source):
    _, rows, cols, depth = now.shape
    out = pltpu.VMEM((24, cols, depth), F32)
    side = pltpu.VMEM((3, rows, 2, depth), F32)
    return pl.pallas_call(
        east_pack_kernel,
        out_shape=(
            out,
            out,
            side,
            side,
            jax.ShapeDtypeStruct((LANES, LANES), jnp.int32),
            pltpu.VMEM((1, LANES), jnp.int32),
        ),
        in_specs=[HBM_SPEC] * 6,
        out_specs=(VMEM_SPEC,) * 6,
        scratch_shapes=[pltpu.VMEM((1, LANES), jnp.int32), pltpu.SemaphoreType.DMA((21,))],
        compiler_params=pltpu.CompilerParams(vmem_limit_bytes=VMEM_BYTES),
        name="east_pack",
    )(now, prev, buoy, mu, lam, source)


def first_main_kernel(prev, buoy, mu, lam, now, xa, xb, out, pack, vp, pv, bv, mv, lv, *work):
    rows = now.shape[1]
    own = pl.ds(2, rows)
    copies = started(
        [(now, vp.at[:, pl.ds(4, rows)]), (prev, pv.at[:, own])] + [(src, dst.at[own]) for src, dst in ((buoy, bv), (mu, mv), (lam, lv))],
        work[-1],
    )
    odd = parity("gx")
    for edge, side in ((xa, 1 - odd), (xb, odd)):
        four = pl.ds((rows + 4) * side, 4)
        two = pl.ds((rows + 2) * side, 2)
        for c in range(3):
            vp[c, four] = edge[4 * c : 4 * c + 4]
            pv[c, two] = edge[12 + 2 * c : 14 + 2 * c]
        for n, field in enumerate((bv, mv, lv)):
            field[two] = edge[18 + 2 * n : 20 + 2 * n]
    copies[0].wait()
    run_step(vp, pv, bv, mv, lv, out, pack, work[:-1], lambda: wait_all(copies[1:]))


def first_main(now, xa, xb, prev, buoy, mu, lam):
    _, rows, cols, depth = now.shape
    wide = rows + 4
    one = pltpu.VMEM((wide, cols, depth), F32)
    return pl.pallas_call(
        first_main_kernel,
        out_shape=(pltpu.VMEM((3, wide, cols, depth), F32), pltpu.VMEM((3, wide, 8, depth), F32)),
        in_specs=[HBM_SPEC] * 5 + [VMEM_SPEC] * 2,
        out_specs=(VMEM_SPEC,) * 2,
        scratch_shapes=[
            pltpu.VMEM((3, wide + 4, cols, depth), F32),
            pltpu.VMEM((3, wide, cols, depth), F32),
            one,
            one,
            one,
            *step_work(wide, cols, depth),
            pltpu.SemaphoreType.DMA((5,)),
        ],
        compiler_params=pltpu.CompilerParams(vmem_limit_bytes=VMEM_BYTES),
        name="first_main",
    )(prev, buoy, mu, lam, now, xa, xb)


def first_north_kernel(main, pack, ya, yb, mid, ma, mb, top, rim, ex, ey):
    rows = main.shape[1] - 4
    fill_north(rim, ya, yb)
    add_north(rim, pack, main, mid, ex, ey, 0, main.shape[3] // LANES)
    odd = parity("gy")

    wide = rows + 4

    def gather(edge, first):
        cells = slice(first, first + 2)
        edge[0:wide] = mid[0, :, cells, :]
        edge[wide : 2 * wide] = mid[1, :, cells, :]
        edge[2 * wide :] = mid[2, 2 : wide - 2, cells, :]

    @pl.when(odd == 0)
    def _():
        gather(ma, 14)
        gather(mb, 0)

    @pl.when(odd == 1)
    def _():
        gather(ma, 0)
        gather(mb, 14)

    top[...] = surface_rows(mid.at[:, pl.ds(2, rows)], 0)


def first_north(main, pack, ya, yb):
    _, wide, _, depth = main.shape
    edge = pltpu.VMEM((3 * wide - 4, 2, depth), F32)
    return pl.pallas_call(
        first_north_kernel,
        out_shape=(pltpu.VMEM(main.shape, F32), edge, edge, pltpu.VMEM((8, SIDE * SIDE), F32)),
        in_specs=[VMEM_SPEC] * 4,
        out_specs=(VMEM_SPEC,) * 4,
        scratch_shapes=[
            pltpu.VMEM((3, wide + 4, 8, depth), F32),
            pltpu.VMEM((wide + 4, 8, depth), F32),
            pltpu.VMEM((wide + 4, 8, depth), F32),
        ],
        compiler_params=pltpu.CompilerParams(vmem_limit_bytes=VMEM_BYTES),
        name="first_north",
    )(main, pack, ya, yb)


def second_main_kernel(prev, buoy, mu, lam, vp, mid, out, pack, pv, bv, mv, lv, *work):
    sems = work[-1]
    rows = prev.shape[1]
    copies = started([(prev, pv), (buoy, bv), (mu, mv), (lam, lv)], sems)
    stores = started([(vp.at[:, pl.ds(2, rows)], mid)], sems.at[pl.ds(4, 1)])
    run_step(vp, pv, bv, mv, lv, out, pack, work[:-1], lambda: wait_all(copies))
    wait_all(stores)


def second_main(v, prev, buoy, mu, lam):
    _, rows, cols, depth = prev.shape
    whole = pltpu.VMEM(prev.shape, F32)
    one = pltpu.VMEM((rows, cols, depth), F32)
    return pl.pallas_call(
        second_main_kernel,
        out_shape=(pltpu.HBM(prev.shape, F32), whole, pltpu.VMEM((3, rows, 8, depth), F32)),
        in_specs=[HBM_SPEC] * 4 + [VMEM_SPEC],
        out_specs=(HBM_SPEC,) + (VMEM_SPEC,) * 2,
        scratch_shapes=[
            whole,
            one,
            one,
            one,
            *step_work(rows, cols, depth),
            pltpu.SemaphoreType.DMA((5,)),
        ],
        compiler_params=pltpu.CompilerParams(vmem_limit_bytes=VMEM_BYTES),
        name="second_main",
    )(prev, buoy, mu, lam, v)


def fill_north(rim, ya, yb):
    odd_y = parity("gy")
    rows, wide = rim.shape[1], rim.shape[3]
    rim[:, :, 2:6, :] = jnp.zeros((rim.shape[0], rows, 4, wide), F32)

    def place(edge, first):
        cells = slice(first, first + 2)
        rim[0, :, cells, :] = edge[0:rows, :, :wide]
        rim[1, :, cells, :] = edge[rows : 2 * rows, :, :wide]
        rim[2, 2 : rows - 2, cells, :] = edge[2 * rows :, :, :wide]

    @pl.when(odd_y == 0)
    def _():
        place(yb, 0)
        place(ya, 6)

    @pl.when(odd_y == 1)
    def _():
        place(ya, 0)
        place(yb, 6)


def add_north(rim, pack, main, out, ex, ey, first, last, base=0, done=None, parts=1):
    rows = rim.shape[1] - 4
    total = 3
    span = range(first, last)
    lanes = lambda k: pl.ds(k * LANES, LANES)
    local = lambda k: pl.ds((k - base) * LANES, LANES)
    below, above = max(first - 1, 0), min(last + 1, total)

    sub = iota((8, LANES), 0)
    low = sub < 4

    def rim_parts(c, r, k):
        two = rim[c, r, :, lanes(k)]
        one = jnp.where(sub == 7, pltpu.roll(two, 1, axis=0), 0.0)
        return jnp.where(sub == 0, pltpu.roll(two, 7, axis=0), one), two

    def slope(c, r, k):
        one, two = rim_parts(c, r, k)
        change = one - two * 0.125
        return jnp.where(low, -change, change)

    def bend(c, r, k):
        one, two = rim_parts(c, r, k)
        return one - two * 0.0625

    def ends(get):
        return (
            get(first - 1) if first > 0 else None,
            [get(k) for k in span],
            get(last) if last < total else None,
        )

    def inner(r):
        for k in range(below, above):
            ey[r, :, lanes(k)] = slope(1, r, k)
        for k in span:
            ex[r, :, lanes(k)] = slope(0, r, k)

    def inner_two(pair, carry):
        inner(2 * pair)
        inner(2 * pair + 1)
        return carry

    lax.fori_loop(0, (rows + 4) // 2, inner_two, 0)

    def outer(i):
        r = i + 2
        yz = z_first(*ends(lambda k: slope(2, r, k)))
        xy = z_first(*ends(lambda k: ey[r, :, lanes(k)]))
        for n, k in enumerate(span):

            def derived(ref):
                return first_of(*[ref[r + d, :, lanes(k)] for d in (1, -1, 2, -2)])

            shear, both, scale = [pack[which, i, :, local(k)] for which in range(3)]
            mixed = [derived(ey), derived(ex) + yz[n], xy[n]]
            for c in range(3):
                q = bend(c, r, k)
                along = mixed[c] * (1.0 / 3.0)
                if c == 1:
                    along = along + q
                update = scale * (shear * q + both * along)
                out[c, i, 0:8, local(k)] = main[c, i, 0:8, local(k)] + jnp.where(low, update, 0.0)
                out[c, i, 8:16, local(k)] = main[c, i, 8:16, local(k)] + jnp.where(low, 0.0, update)

    def outer_two(pair, carry):
        outer(2 * pair)
        outer(2 * pair + 1)
        return carry

    count = rows // 2 // parts
    for part in range(parts):
        lax.fori_loop(part * count, (part + 1) * count, outer_two, 0)
        if done is not None:
            done(2 * part * count, 2 * count)


def window_tables(flat, windows):
    span = SIDE - PX + 1
    halves = [flat[:, :LANES], flat[:, LANES:]]
    lane = iota((8, LANES), 1)
    windows[span * span * 8 :, :] = jnp.zeros((windows.shape[0] - span * span * 8, LANES), F32)
    for ox in range(span):
        for oy in range(span):
            half, shift = divmod(ox * SIDE + oy, LANES)
            moved = halves[half]
            if shift:
                other = pltpu.roll(halves[1], LANES - shift, axis=1) if half == 0 else jnp.zeros_like(moved)
                moved = jnp.where(lane < LANES - shift, pltpu.roll(moved, LANES - shift, axis=1), other)
            windows[pl.ds((ox * span + oy) * 8, 8), :] = moved


def corner_forces(flat, weights, windows):
    window_tables(flat, windows)
    total = jnp.zeros((LANES, weights.shape[2]), F32)
    for c in range(3):
        total = total + jnp.dot(
            windows[pl.ds(c, LANES, stride=8), :], weights[c], precision=HIGHEST, preferred_element_type=F32
        )
    return total


def spread(part, c):
    shape = (LANES, part.shape[1])
    cell = iota(shape, 0)
    row = c * PX * PX + (cell // SIDE) * PX + cell % SIDE
    place = jnp.where((iota(shape, 1) == row) & (cell % SIDE < PX), 1.0, 0.0)
    return lax.dot_general(
        place, part[...], (((1,), (1,)), ((), ())), precision=HIGHEST, preferred_element_type=F32
    )


def prepare_kernel(asked, offset, part, chosen, weights):
    span = SIDE - PX + 1
    shape = (LANES, LANES)
    where = offset[0:1, :] * span + offset[1:2, :]
    corner = jnp.where(iota(shape, 0) == where, 1.0, 0.0)
    lane = iota(shape, 1)
    for r in range(2):
        slot = jnp.where(lane == asked[:, r : r + 1], 1.0, 0.0)
        chosen[pl.ds(r, LANES, stride=2), :] = lax.dot_general(
            slot, corner, (((1,), (1,)), ((), ())), preferred_element_type=F32
        )
    for c in range(3):
        weights[c] = spread(part, c)


def prepare(asked, offset, part):
    modes = part.shape[0]
    return pl.pallas_call(
        prepare_kernel,
        out_shape=(pltpu.VMEM((2 * LANES, LANES), F32), pltpu.VMEM((3, LANES, modes), F32)),
        in_specs=[VMEM_SPEC] * 3,
        out_specs=(VMEM_SPEC,) * 2,
        compiler_params=pltpu.CompilerParams(vmem_limit_bytes=VMEM_BYTES),
        name="prepare",
    )(asked, offset, part)


def early_kernel(top, chosen, weights, early, windows):
    forces = corner_forces(top[...], weights, windows)
    early[...] = jnp.dot(chosen[...], forces, precision=HIGHEST, preferred_element_type=F32)


def early_forces(top, chosen, weights):
    return pl.pallas_call(
        early_kernel,
        out_shape=pltpu.VMEM((2 * LANES, weights.shape[2]), F32),
        in_specs=[VMEM_SPEC] * 3,
        out_specs=VMEM_SPEC,
        scratch_shapes=[pltpu.VMEM((8 * LANES, LANES), F32)],
        compiler_params=pltpu.CompilerParams(vmem_limit_bytes=VMEM_BYTES),
        name="early_forces",
    )(top, chosen, weights)


def near_north_kernel(main, pack, ya, yb, chosen, weights, early, near, ans, rim, ex, ey, windows):
    fill_north(rim, ya, yb)
    add_north(rim, pack, main, near, ex, ey, 0, 1)
    forces = corner_forces(surface_rows(near, 0), weights, windows)
    late = jnp.dot(chosen[...], forces, precision=HIGHEST, preferred_element_type=F32)
    ans[...] = jnp.concatenate([early[...], late], axis=1)


def near_north(main, pack, ya, yb, chosen, weights, early):
    _, rows, cols, _ = main.shape
    return pl.pallas_call(
        near_north_kernel,
        out_shape=(pltpu.VMEM((3, rows, cols, LANES), F32), pltpu.VMEM((2 * LANES, LANES), F32)),
        in_specs=[VMEM_SPEC] * 7,
        out_specs=(VMEM_SPEC,) * 2,
        scratch_shapes=[
            pltpu.VMEM((3, rows + 4, 8, 2 * LANES), F32),
            pltpu.VMEM((rows + 4, 8, 2 * LANES), F32),
            pltpu.VMEM((rows + 4, 8, 2 * LANES), F32),
            pltpu.VMEM((8 * LANES, LANES), F32),
        ],
        compiler_params=pltpu.CompilerParams(vmem_limit_bytes=VMEM_BYTES),
        name="near_north",
    )(main, pack, ya, yb, chosen, weights, early)


def far_north_kernel(main, pack, near, ya, yb, nxt, rim, out, ex, ey, sems):
    stores = started([(near, nxt.at[:, :, :, pl.ds(0, LANES)])], sems.at[pl.ds(0, 1)])
    columns = pl.ds(LANES, out.shape[3] - LANES)

    def done(row, count):
        part = (slice(None), pl.ds(row, count), slice(None), columns)
        stores.extend(started([(out.at[part], nxt.at[part])], sems.at[pl.ds(len(stores), 1)]))

    fill_north(rim, ya, yb)
    add_north(rim, pack, main, out, ex, ey, 1, out.shape[3] // LANES, done=done, parts=4)
    wait_all(stores)


def far_north(main, pack, near, ya, yb):
    _, rows, _, depth = main.shape
    return pl.pallas_call(
        far_north_kernel,
        out_shape=pltpu.HBM(main.shape, F32),
        in_specs=[VMEM_SPEC] * 5,
        out_specs=HBM_SPEC,
        scratch_shapes=[
            pltpu.VMEM((3, rows + 4, 8, depth), F32),
            pltpu.VMEM(main.shape, F32),
            pltpu.VMEM((rows + 4, 8, depth), F32),
            pltpu.VMEM((rows + 4, 8, depth), F32),
            pltpu.SemaphoreType.DMA((5,)),
        ],
        compiler_params=pltpu.CompilerParams(vmem_limit_bytes=VMEM_BYTES),
        name="far_north",
    )(main, pack, near, ya, yb)


def north_kernel(low, high, xa, xb, ya, yb):
    rows = low.shape[1]
    odd_x, odd_y = parity("gx"), parity("gy")

    wide = rows + 8

    def gather(out, own, edge):
        cells = slice(edge, edge + 2)
        for c in range(3):
            start = c * wide + (2 if c == 2 else 4)
            out[start : start + rows] = own[c]
        for rim, side in ((xa, 1 - odd_x), (xb, odd_x)):
            for c in range(2):
                out[pl.ds(c * wide + (rows + 4) * side, 4)] = rim[4 * c : 4 * c + 4, cells, :]
            out[pl.ds(2 * wide + (rows + 2) * side, 2)] = rim[pl.ds(10 - 2 * side, 2), cells, :]

    last = SIDE - 2

    @pl.when(odd_y == 0)
    def _():
        gather(ya, high, last)
        gather(yb, low, 0)

    @pl.when(odd_y == 1)
    def _():
        gather(ya, low, 0)
        gather(yb, high, last)


def north_edges(low, high, xa, xb):
    _, rows, two, depth = low.shape
    out = pltpu.VMEM((3 * (rows + 8) - 4, two, depth), F32)
    return pl.pallas_call(
        north_kernel,
        out_shape=(out, out),
        in_specs=[VMEM_SPEC] * 4,
        out_specs=(VMEM_SPEC, VMEM_SPEC),
        compiler_params=pltpu.CompilerParams(vmem_limit_bytes=VMEM_BYTES),
        name="north_edges",
    )(low, high, xa, xb)


def build_requests(source, req, pos):
    shape = (LANES, LANES)
    src = source[...]
    tile = src // LANES
    local = (src % LANES).astype(F32)
    mine = jnp.where(iota(shape, 0) == tile, 1.0, 0.0)
    earlier = jnp.where(iota(shape, 0) < iota(shape, 1), 1.0, 0.0)
    before = jnp.dot(mine, earlier, preferred_element_type=F32)
    rank = jnp.sum(before * mine, axis=0, keepdims=True)
    wanted = mine * local
    lane = iota(shape, 1)
    first = jnp.sum(jnp.where(rank == 0.0, wanted, 0.0), axis=1, keepdims=True)
    second = jnp.sum(jnp.where(rank == 1.0, wanted, 0.0), axis=1, keepdims=True)
    req[...] = jnp.where(lane == 0, first, jnp.where(lane == 1, second, 0.0)).astype(jnp.int32)
    pos[...] = tile * 2 + jnp.minimum(rank, 1.0).astype(jnp.int32)


def columns_of(ker):
    taps = ker.shape[0]
    same = jnp.where(iota((taps, taps), 0) == iota((taps, taps), 1), 1.0, 0.0)
    return lax.dot_general(
        ker[...], same, (((0,), (0,)), ((), ())), precision=HIGHEST, preferred_element_type=F32
    )


def history_kernel(hist, ker, out):
    k = columns_of(ker)
    steps = hist.shape[0]
    half = hist.shape[1] // 2
    for part in range(2):
        rows = pl.ds(part * half, half)
        kp = k[part * half : (part + 1) * half]
        first = jnp.zeros((half, LANES), F32)
        second = jnp.zeros((half, LANES), F32)
        for h in range(steps):
            past = hist[h, rows, :]
            first = first + kp[:, steps - h : steps - h + 1] * past
            if h > 0:
                second = second + kp[:, steps + 1 - h : steps + 2 - h] * past
        out[0, rows, :] = first
        out[1, rows, :] = second


def history_part(hist, ker):
    return pl.pallas_call(
        history_kernel,
        out_shape=pltpu.VMEM((2,) + hist.shape[1:], F32),
        in_specs=[VMEM_SPEC, VMEM_SPEC],
        out_specs=VMEM_SPEC,
        compiler_params=pltpu.CompilerParams(vmem_limit_bytes=VMEM_BYTES),
        name="history",
    )(hist, ker)


def response_kernel(ans, pos, count, base, ker, out):
    at = pos[...]
    chosen = jnp.where(iota((2 * LANES, LANES), 0) == at, 1.0, 0.0)
    forces = lax.dot_general(
        ans[...], chosen, (((0,), (0,)), ((), ())), precision=HIGHEST, preferred_element_type=F32
    )
    k = columns_of(ker)
    modes = k.shape[0]
    early, late = forces[:modes], forces[modes:]
    live = iota((1, LANES), 1) < count[...]
    out[0] = jnp.where(live, base[0] + k[:, 0:1] * early, 0.0)
    out[1] = jnp.where(live, base[1] + k[:, 0:1] * late + k[:, 1:2] * early, 0.0)


def make_responses(ans, pos, count, base, ker):
    return pl.pallas_call(
        response_kernel,
        out_shape=jax.ShapeDtypeStruct(base.shape, F32),
        in_specs=[VMEM_SPEC] * 5,
        out_specs=VMEM_SPEC,
        compiler_params=pltpu.CompilerParams(vmem_limit_bytes=VMEM_BYTES),
        name="responses",
    )(ans, pos, count.reshape(1, 1), base, ker)


def swap(array, axis, first):
    pairs = []
    for low in range(first, lax.axis_size(axis) - 1, 2):
        pairs += [(low, low + 1), (low + 1, low)]
    return in_vmem(lax.ppermute(array, axis, pairs))


def east_swaps(xa, xb):
    return swap(xa, "gx", 0), swap(xb, "gx", 1)


def north_swaps(ya, yb):
    return swap(ya, "gy", 0), swap(yb, "gy", 1)


def per_device(
    disp_prev,
    disp_now,
    buoyancy,
    shear_mod,
    lame_first,
    foot_offset,
    owner_source,
    owner_count,
    force_history,
    participation,
    kernels,
):
    return steps(
        disp_prev,
        disp_now,
        tuple(in_hbm(a) for a in (buoyancy, shear_mod, lame_first)),
        foot_offset.T,
        owner_source,
        owner_count,
        force_history,
        participation.T,
        kernels.T,
    )


def exchange(array, place=lambda rows: rows):
    rows = place(array.reshape(LANES, -1, LANES))
    out = lax.all_to_all(rows, ("gx", "gy"), split_axis=0, concat_axis=0)
    return out.reshape(array.shape)


def steps(prev, now, medium, offset, source, count, history, part, kernels):
    pa, pb, low, high, req, pos = east_pack(
        in_hbm(now), in_hbm(prev), *medium, in_hbm(source.reshape(1, LANES))
    )
    east = east_swaps(in_vmem(pa), in_vmem(pb))
    asked = exchange(req)
    north = north_edges(in_vmem(low), in_vmem(high), *east)
    north = north_swaps(*north)
    main = first_main(in_hbm(now), *east, in_hbm(prev), *medium)
    north, main = lax.optimization_barrier((north, main))
    mid, ya, yb, top = first_north(*main, *north)
    north = north_swaps(ya, yb)
    prepared = prepare(in_vmem(asked), offset, part)
    early = early_forces(top, *prepared)
    disp_mid, main, pack = second_main(mid, in_hbm(now), *medium)
    north, main, pack, early = lax.optimization_barrier((north, main, pack, early))
    near, ans = near_north(main, pack, *north, *prepared, early)
    back = exchange(ans)
    base = in_vmem(history_part(history, kernels))
    disp_next = far_north(in_vmem(main), in_vmem(pack), in_vmem(near), *(in_vmem(a) for a in north))
    responses = make_responses(back, in_vmem(pos), count, base, kernels)
    return disp_mid, disp_next, responses


def solution(mesh):
    return jax.shard_map(
        per_device,
        mesh=mesh,
        in_specs=(
            P(None, "gx", "gy", None),
            P(None, "gx", "gy", None),
            P("gx", "gy", None),
            P("gx", "gy", None),
            P("gx", "gy", None),
            P(("gx", "gy"), None),
            P(("gx", "gy")),
            P(("gx", "gy")),
            P(None, None, ("gx", "gy")),
            P(),
            P(),
        ),
        out_specs=(
            P(None, "gx", "gy", None),
            P(None, "gx", "gy", None),
            P(None, None, ("gx", "gy")),
        ),
        check_vma=False,
    )
```

```python
import jax
import jax.numpy as jnp
from jax import lax
from jax.experimental import pallas as pl
from jax.experimental.pallas import tpu as pltpu
from jax.sharding import PartitionSpec as P


PX = 8
SIDE = 16
LANES = 128
HIGHEST = lax.Precision.HIGHEST
F32 = jnp.float32
VMEM_BYTES = 16 << 20

VMEM_SPEC = pl.BlockSpec(memory_space=pltpu.VMEM)
HBM_SPEC = pl.BlockSpec(memory_space=pltpu.HBM)
SMEM_SPEC = pl.BlockSpec(memory_space=pltpu.SMEM)


def iota(shape, axis):
    return lax.broadcasted_iota(jnp.int32, shape, axis)


def in_vmem(array):
    return pltpu.with_memory_space_constraint(array, pltpu.VMEM)


def in_hbm(array):
    return pltpu.with_memory_space_constraint(array, pltpu.HBM)


def parity(axis):
    return lax.axis_index(axis) % 2


def first_of(a1, b1, a2, b2):
    return (a1 - b1) - (a2 - b2) * 0.125


def second_of(a1, b1, a2, b2):
    return (a1 + b1) - (a2 + b2) * 0.0625


def z_four(below, columns, above):
    lane = iota(columns[0].shape, 1)
    zero = jnp.zeros_like(columns[0])
    count = len(columns)
    out = [[] for _ in columns]
    for s in (1, -1, 2, -2):
        turned = [pltpu.roll(c, (-s) % LANES, axis=1) for c in columns]
        if s > 0:
            turned.append(zero if above is None else pltpu.roll(above, LANES - s, axis=1))
        else:
            turned.insert(0, zero if below is None else pltpu.roll(below, -s, axis=1))
        for k in range(count):
            if s > 0:
                out[k].append(jnp.where(lane < LANES - s, turned[k], turned[k + 1]))
            else:
                out[k].append(jnp.where(lane >= -s, turned[k + 1], turned[k]))
    return out


def z_first(below, columns, above):
    return [first_of(*four) for four in z_four(below, columns, above)]


def north_four(lower, upper):
    sub = iota(lower.shape, 0)
    zero = jnp.zeros_like(lower)
    out = ([], [])
    for s in (1, -1, 2, -2):
        first, second = [pltpu.roll(tile, (-s) % 8, axis=0) for tile in (lower, upper)]
        if s > 0:
            out[0].append(jnp.where(sub < 8 - s, first, second))
            out[1].append(jnp.where(sub < 8 - s, second, zero))
        else:
            out[0].append(jnp.where(sub >= -s, first, zero))
            out[1].append(jnp.where(sub >= -s, second, first))
    return out


def run_step(vp, prev, buoy, mu, lam, out, pack, work, ready, arrived=None, late=0):
    byx, syz, dyy, dyz, qyx, qyy, qyz, qzz = work
    rows = vp.shape[1] - 4
    span = range(vp.shape[3] // LANES)
    lanes = lambda k: pl.ds(k * LANES, LANES)
    tile = lambda h: pl.ds(8 * h, 8)

    def inner(r, full):
        i = r - 2
        for h in range(2):
            four = z_four(None, [vp[2, r, tile(h), lanes(k)] for k in span], None)
            for k in span:
                syz[r, tile(h), lanes(k)] = first_of(*four[k])
                if full:
                    qzz[i, tile(h), lanes(k)] = second_of(*four[k])
        for k in span:
            for c in range(3 if full else 2):
                four = north_four(*[vp[c, r, tile(h), lanes(k)] for h in range(2)])
                for h in range(2):
                    slope = first_of(*four[h])
                    if c == 0:
                        byx[r, tile(h), lanes(k)] = slope
                    elif c == 1:
                        syz[r, tile(h), lanes(k)] = syz[r, tile(h), lanes(k)] + slope
                    if full:
                        if c > 0:
                            (dyy, dyz)[c - 1][i, tile(h), lanes(k)] = slope
                        (qyx, qyy, qyz)[c][i, tile(h), lanes(k)] = second_of(*four[h])

    def each(start, stop, full):
        def trip(pair, carry):
            inner(start + 2 * pair, full)
            inner(start + 2 * pair + 1, full)
            return carry

        lax.fori_loop(0, (stop - start) // 2, trip, 0)

    each(0, 2, False)
    each(rows + 2, rows + 4, False)
    if arrived is not None:
        each(2, late, True)
        each(rows + 4 - late, rows + 2, True)
        arrived()
    start = max(2, late)
    each(start, rows + 4 - start, True)
    ready()

    def outer(i):
        r = i + 2
        low = iota((8, LANES), 0) < 4
        lower = {}
        for h in range(2):
            here = tile(h)

            def x_four(c, k):
                return [vp[c, r + d, here, lanes(k)] for d in (1, -1, 2, -2)]

            def derived(ref, k):
                return first_of(*[ref[r + d, here, lanes(k)] for d in (1, -1, 2, -2)])

            yz = z_first(None, [dyz[i, here, lanes(k)] for k in span], None)
            xy = z_first(None, [first_of(*x_four(0, k)) + dyy[i, here, lanes(k)] for k in span], None)
            along_z = [z_four(None, [vp[c, r, here, lanes(k)] for k in span], None) for c in range(2)]
            for k in span:
                shear = mu[i, here, lanes(k)]
                both = lam[i, here, lanes(k)] + shear
                scale = buoy[i, here, lanes(k)] * 0.12
                for which, factor in enumerate((shear, both, scale)):
                    if h == 0:
                        lower[which, k] = factor
                    else:
                        pack[which, i, :, lanes(k)] = jnp.where(low, lower[which, k], factor)
                mixed = [derived(syz, k), derived(byx, k) + yz[k], xy[k]]
                for c in range(3):
                    centre = vp[c, r, here, lanes(k)]
                    q = [
                        second_of(*x_four(c, k)),
                        (qyx, qyy, qyz)[c][i, here, lanes(k)],
                        second_of(*along_z[c][k]) if c < 2 else qzz[i, here, lanes(k)],
                    ]
                    laplace = (q[0] + q[1]) + (q[2] - centre * 5.625)
                    along = (q[c] - centre * 1.875) + mixed[c] * (1.0 / 3.0)
                    update = shear * laplace + both * along
                    out[c, i, here, lanes(k)] = (2.0 * centre - prev[c, i, here, lanes(k)]) + scale * update

    def outer_two(pair, carry):
        outer(2 * pair)
        outer(2 * pair + 1)
        return carry

    lax.fori_loop(0, rows // 2, outer_two, 0)


def step_work(rows, cols, depth):
    return [pltpu.VMEM((rows + 4, cols, depth), F32)] * 2 + [pltpu.VMEM((rows, cols, depth), F32)] * 6


def surface_rows(field, first):
    cells = SIDE * SIDE
    flat = jnp.zeros((8, cells), F32)
    for c in range(3):
        pick = jnp.where((iota((8, LANES), 0) == first + c) & (iota((8, LANES), 1) == 0), 1.0, 0.0)
        flat = flat + lax.dot_general(
            pick,
            field[c, :, :, 0:LANES].reshape(cells, LANES),
            (((1,), (1,)), ((), ())),
            precision=HIGHEST,
            preferred_element_type=F32,
        )
    return flat


def started(pairs, sems):
    copies = [pltpu.make_async_copy(src, dst, sems.at[n]) for n, (src, dst) in enumerate(pairs)]
    for copy in copies:
        copy.start()
    return copies


def wait_all(copies):
    for copy in copies:
        copy.wait()


def east_pack_kernel(now, prev, buoy, mu, lam, source, pa, pb, low, high, req, pos, held, sems):
    rows = now.shape[1]
    odd = parity("gx")
    pairs = []
    for out, side in ((pa, 1 - odd), (pb, odd)):
        four = pl.ds((rows - 4) * side, 4)
        two = pl.ds((rows - 2) * side, 2)
        for c in range(3):
            pairs.append((now.at[c, four], out.at[pl.ds(4 * c, 4)]))
            pairs.append((prev.at[c, two], out.at[pl.ds(12 + 2 * c, 2)]))
        for n, field in enumerate((buoy, mu, lam)):
            pairs.append((field.at[two], out.at[pl.ds(18 + 2 * n, 2)]))
    cols = now.shape[2]
    pairs.append((now.at[:, :, pl.ds(0, 2)], low))
    pairs.append((now.at[:, :, pl.ds(cols - 2, 2)], high))
    copies = started([(source, held)] + pairs, sems)
    copies[0].wait()
    build_requests(held, req, pos)
    wait_all(copies[1:])


def east_pack(now, prev, buoy, mu, lam, source):
    _, rows, cols, depth = now.shape
    out = pltpu.VMEM((24, cols, depth), F32)
    side = pltpu.VMEM((3, rows, 2, depth), F32)
    return pl.pallas_call(
        east_pack_kernel,
        out_shape=(
            out,
            out,
            side,
            side,
            jax.ShapeDtypeStruct((LANES, LANES), jnp.int32),
            pltpu.VMEM((1, LANES), jnp.int32),
        ),
        in_specs=[HBM_SPEC] * 6,
        out_specs=(VMEM_SPEC,) * 6,
        scratch_shapes=[pltpu.VMEM((1, LANES), jnp.int32), pltpu.SemaphoreType.DMA((21,))],
        compiler_params=pltpu.CompilerParams(vmem_limit_bytes=VMEM_BYTES),
        name="east_pack",
    )(now, prev, buoy, mu, lam, source)


def first_main_kernel(prev, buoy, mu, lam, now, xa, xb, out, pack, vp, pv, bv, mv, lv, *work):
    rows = now.shape[1]
    own = pl.ds(2, rows)
    copies = started(
        [(now, vp.at[:, pl.ds(4, rows)]), (prev, pv.at[:, own])] + [(src, dst.at[own]) for src, dst in ((buoy, bv), (mu, mv), (lam, lv))],
        work[-1],
    )
    odd = parity("gx")
    for edge, side in ((xa, 1 - odd), (xb, odd)):
        four = pl.ds((rows + 4) * side, 4)
        two = pl.ds((rows + 2) * side, 2)
        for c in range(3):
            vp[c, four] = edge[4 * c : 4 * c + 4]
            pv[c, two] = edge[12 + 2 * c : 14 + 2 * c]
        for n, field in enumerate((bv, mv, lv)):
            field[two] = edge[18 + 2 * n : 20 + 2 * n]
    run_step(
        vp, pv, bv, mv, lv, out, pack, work[:-1], lambda: wait_all(copies[1:]), arrived=copies[0].wait, late=4
    )


def first_main(now, xa, xb, prev, buoy, mu, lam):
    _, rows, cols, depth = now.shape
    wide = rows + 4
    one = pltpu.VMEM((wide, cols, depth), F32)
    return pl.pallas_call(
        first_main_kernel,
        out_shape=(pltpu.VMEM((3, wide, cols, depth), F32), pltpu.VMEM((3, wide, 8, depth), F32)),
        in_specs=[HBM_SPEC] * 5 + [VMEM_SPEC] * 2,
        out_specs=(VMEM_SPEC,) * 2,
        scratch_shapes=[
            pltpu.VMEM((3, wide + 4, cols, depth), F32),
            pltpu.VMEM((3, wide, cols, depth), F32),
            one,
            one,
            one,
            *step_work(wide, cols, depth),
            pltpu.SemaphoreType.DMA((5,)),
        ],
        compiler_params=pltpu.CompilerParams(vmem_limit_bytes=VMEM_BYTES),
        name="first_main",
    )(prev, buoy, mu, lam, now, xa, xb)


def first_north_kernel(main, pack, ya, yb, mid, ma, mb, top, rim, ex, ey):
    rows = main.shape[1] - 4
    fill_north(rim, ya, yb)
    add_north(rim, pack, main, mid, ex, ey, 0, main.shape[3] // LANES)
    odd = parity("gy")

    wide = rows + 4

    def gather(edge, first):
        cells = slice(first, first + 2)
        edge[0:wide] = mid[0, :, cells, :]
        edge[wide : 2 * wide] = mid[1, :, cells, :]
        edge[2 * wide :] = mid[2, 2 : wide - 2, cells, :]

    @pl.when(odd == 0)
    def _():
        gather(ma, 14)
        gather(mb, 0)

    @pl.when(odd == 1)
    def _():
        gather(ma, 0)
        gather(mb, 14)

    top[...] = surface_rows(mid.at[:, pl.ds(2, rows)], 0)


def first_north(main, pack, ya, yb):
    _, wide, _, depth = main.shape
    edge = pltpu.VMEM((3 * wide - 4, 2, depth), F32)
    return pl.pallas_call(
        first_north_kernel,
        out_shape=(pltpu.VMEM(main.shape, F32), edge, edge, pltpu.VMEM((8, SIDE * SIDE), F32)),
        in_specs=[VMEM_SPEC] * 4,
        out_specs=(VMEM_SPEC,) * 4,
        scratch_shapes=[
            pltpu.VMEM((3, wide + 4, 8, depth), F32),
            pltpu.VMEM((wide + 4, 8, depth), F32),
            pltpu.VMEM((wide + 4, 8, depth), F32),
        ],
        compiler_params=pltpu.CompilerParams(vmem_limit_bytes=VMEM_BYTES),
        name="first_north",
    )(main, pack, ya, yb)


def second_main_kernel(prev, buoy, mu, lam, vp, mid, out, pack, pv, bv, mv, lv, *work):
    sems = work[-1]
    rows = prev.shape[1]
    copies = started([(prev, pv), (buoy, bv), (mu, mv), (lam, lv)], sems)
    stores = started([(vp.at[:, pl.ds(2, rows)], mid)], sems.at[pl.ds(4, 1)])
    run_step(vp, pv, bv, mv, lv, out, pack, work[:-1], lambda: wait_all(copies))
    wait_all(stores)


def second_main(v, prev, buoy, mu, lam):
    _, rows, cols, depth = prev.shape
    whole = pltpu.VMEM(prev.shape, F32)
    one = pltpu.VMEM((rows, cols, depth), F32)
    return pl.pallas_call(
        second_main_kernel,
        out_shape=(pltpu.HBM(prev.shape, F32), whole, pltpu.VMEM((3, rows, 8, depth), F32)),
        in_specs=[HBM_SPEC] * 4 + [VMEM_SPEC],
        out_specs=(HBM_SPEC,) + (VMEM_SPEC,) * 2,
        scratch_shapes=[
            whole,
            one,
            one,
            one,
            *step_work(rows, cols, depth),
            pltpu.SemaphoreType.DMA((5,)),
        ],
        compiler_params=pltpu.CompilerParams(vmem_limit_bytes=VMEM_BYTES),
        name="second_main",
    )(prev, buoy, mu, lam, v)


def fill_north(rim, ya, yb):
    odd_y = parity("gy")
    rows, wide = rim.shape[1], rim.shape[3]
    rim[:, :, 2:6, :] = jnp.zeros((rim.shape[0], rows, 4, wide), F32)

    def place(edge, first):
        cells = slice(first, first + 2)
        rim[0, :, cells, :] = edge[0:rows, :, :wide]
        rim[1, :, cells, :] = edge[rows : 2 * rows, :, :wide]
        rim[2, 2 : rows - 2, cells, :] = edge[2 * rows :, :, :wide]

    @pl.when(odd_y == 0)
    def _():
        place(yb, 0)
        place(ya, 6)

    @pl.when(odd_y == 1)
    def _():
        place(ya, 0)
        place(yb, 6)


def add_north(rim, pack, main, out, ex, ey, first, last, base=0, done=None, parts=1):
    rows = rim.shape[1] - 4
    total = 3
    span = range(first, last)
    lanes = lambda k: pl.ds(k * LANES, LANES)
    local = lambda k: pl.ds((k - base) * LANES, LANES)
    below, above = max(first - 1, 0), min(last + 1, total)

    sub = iota((8, LANES), 0)
    low = sub < 4

    def rim_parts(c, r, k):
        two = rim[c, r, :, lanes(k)]
        one = jnp.where(sub == 7, pltpu.roll(two, 1, axis=0), 0.0)
        return jnp.where(sub == 0, pltpu.roll(two, 7, axis=0), one), two

    def slope(c, r, k):
        one, two = rim_parts(c, r, k)
        change = one - two * 0.125
        return jnp.where(low, -change, change)

    def bend(c, r, k):
        one, two = rim_parts(c, r, k)
        return one - two * 0.0625

    def ends(get):
        return (
            get(first - 1) if first > 0 else None,
            [get(k) for k in span],
            get(last) if last < total else None,
        )

    def inner(r):
        for k in range(below, above):
            ey[r, :, lanes(k)] = slope(1, r, k)
        for k in span:
            ex[r, :, lanes(k)] = slope(0, r, k)

    def inner_two(pair, carry):
        inner(2 * pair)
        inner(2 * pair + 1)
        return carry

    lax.fori_loop(0, (rows + 4) // 2, inner_two, 0)

    def outer(i):
        r = i + 2
        yz = z_first(*ends(lambda k: slope(2, r, k)))
        xy = z_first(*ends(lambda k: ey[r, :, lanes(k)]))
        for n, k in enumerate(span):

            def derived(ref):
                return first_of(*[ref[r + d, :, lanes(k)] for d in (1, -1, 2, -2)])

            shear, both, scale = [pack[which, i, :, local(k)] for which in range(3)]
            mixed = [derived(ey), derived(ex) + yz[n], xy[n]]
            for c in range(3):
                q = bend(c, r, k)
                along = mixed[c] * (1.0 / 3.0)
                if c == 1:
                    along = along + q
                update = scale * (shear * q + both * along)
                out[c, i, 0:8, local(k)] = main[c, i, 0:8, local(k)] + jnp.where(low, update, 0.0)
                out[c, i, 8:16, local(k)] = main[c, i, 8:16, local(k)] + jnp.where(low, 0.0, update)

    def outer_two(pair, carry):
        outer(2 * pair)
        outer(2 * pair + 1)
        return carry

    count = rows // 2 // parts
    for part in range(parts):
        lax.fori_loop(part * count, (part + 1) * count, outer_two, 0)
        if done is not None:
            done(2 * part * count, 2 * count)


def window_tables(flat, windows):
    span = SIDE - PX + 1
    halves = [flat[:, :LANES], flat[:, LANES:]]
    lane = iota((8, LANES), 1)
    windows[span * span * 8 :, :] = jnp.zeros((windows.shape[0] - span * span * 8, LANES), F32)
    for ox in range(span):
        for oy in range(span):
            half, shift = divmod(ox * SIDE + oy, LANES)
            moved = halves[half]
            if shift:
                other = pltpu.roll(halves[1], LANES - shift, axis=1) if half == 0 else jnp.zeros_like(moved)
                moved = jnp.where(lane < LANES - shift, pltpu.roll(moved, LANES - shift, axis=1), other)
            windows[pl.ds((ox * span + oy) * 8, 8), :] = moved


def corner_forces(flat, weights, windows):
    window_tables(flat, windows)
    both = []
    for n in range(2):
        total = jnp.zeros((LANES, weights.shape[2]), F32)
        for c in range(3):
            total = total + jnp.dot(
                windows[pl.ds(3 * n + c, LANES, stride=8), :],
                weights[c],
                precision=HIGHEST,
                preferred_element_type=F32,
            )
        both.append(total)
    return jnp.concatenate(both, axis=1)


def spread(part, c):
    shape = (LANES, part.shape[1])
    cell = iota(shape, 0)
    row = c * PX * PX + (cell // SIDE) * PX + cell % SIDE
    place = jnp.where((iota(shape, 1) == row) & (cell % SIDE < PX), 1.0, 0.0)
    return lax.dot_general(
        place, part[...], (((1,), (1,)), ((), ())), precision=HIGHEST, preferred_element_type=F32
    )


def prepare_kernel(asked, offset, part, chosen, weights):
    span = SIDE - PX + 1
    shape = (LANES, LANES)
    where = offset[0:1, :] * span + offset[1:2, :]
    corner = jnp.where(iota(shape, 0) == where, 1.0, 0.0)
    lane = iota(shape, 1)
    for r in range(2):
        slot = jnp.where(lane == asked[:, r : r + 1], 1.0, 0.0)
        chosen[pl.ds(r, LANES, stride=2), :] = lax.dot_general(
            slot, corner, (((1,), (1,)), ((), ())), preferred_element_type=F32
        )
    for c in range(3):
        weights[c] = spread(part, c)


def prepare(asked, offset, part):
    modes = part.shape[0]
    return pl.pallas_call(
        prepare_kernel,
        out_shape=(pltpu.VMEM((2 * LANES, LANES), F32), pltpu.VMEM((3, LANES, modes), F32)),
        in_specs=[VMEM_SPEC] * 3,
        out_specs=(VMEM_SPEC,) * 2,
        compiler_params=pltpu.CompilerParams(vmem_limit_bytes=VMEM_BYTES),
        name="prepare",
    )(asked, offset, part)


def near_north_kernel(main, pack, ya, yb, top, chosen, weights, near, ans, rim, ex, ey, windows):
    fill_north(rim, ya, yb)
    add_north(rim, pack, main, near, ex, ey, 0, 1)
    forces = corner_forces(top[...] + surface_rows(near, 3), weights, windows)
    ans[...] = jnp.dot(chosen[...], forces, precision=HIGHEST, preferred_element_type=F32)


def near_north(main, pack, ya, yb, top, chosen, weights):
    _, rows, cols, _ = main.shape
    return pl.pallas_call(
        near_north_kernel,
        out_shape=(pltpu.VMEM((3, rows, cols, LANES), F32), pltpu.VMEM((2 * LANES, LANES), F32)),
        in_specs=[VMEM_SPEC] * 7,
        out_specs=(VMEM_SPEC,) * 2,
        scratch_shapes=[
            pltpu.VMEM((3, rows + 4, 8, 2 * LANES), F32),
            pltpu.VMEM((rows + 4, 8, 2 * LANES), F32),
            pltpu.VMEM((rows + 4, 8, 2 * LANES), F32),
            pltpu.VMEM((8 * LANES, LANES), F32),
        ],
        compiler_params=pltpu.CompilerParams(vmem_limit_bytes=VMEM_BYTES),
        name="near_north",
    )(main, pack, ya, yb, top, chosen, weights)


def far_north_kernel(main, pack, near, ya, yb, nxt, rim, out, ex, ey, sems):
    stores = started([(near, nxt.at[:, :, :, pl.ds(0, LANES)])], sems.at[pl.ds(0, 1)])
    columns = pl.ds(LANES, out.shape[3] - LANES)

    def done(row, count):
        part = (slice(None), pl.ds(row, count), slice(None), columns)
        stores.extend(started([(out.at[part], nxt.at[part])], sems.at[pl.ds(len(stores), 1)]))

    fill_north(rim, ya, yb)
    add_north(rim, pack, main, out, ex, ey, 1, out.shape[3] // LANES, done=done, parts=4)
    wait_all(stores)


def far_north(main, pack, near, ya, yb):
    _, rows, _, depth = main.shape
    return pl.pallas_call(
        far_north_kernel,
        out_shape=pltpu.HBM(main.shape, F32),
        in_specs=[VMEM_SPEC] * 5,
        out_specs=HBM_SPEC,
        scratch_shapes=[
            pltpu.VMEM((3, rows + 4, 8, depth), F32),
            pltpu.VMEM(main.shape, F32),
            pltpu.VMEM((rows + 4, 8, depth), F32),
            pltpu.VMEM((rows + 4, 8, depth), F32),
            pltpu.SemaphoreType.DMA((5,)),
        ],
        compiler_params=pltpu.CompilerParams(vmem_limit_bytes=VMEM_BYTES),
        name="far_north",
    )(main, pack, near, ya, yb)


def north_kernel(low, high, xa, xb, ya, yb):
    rows = low.shape[1]
    odd_x, odd_y = parity("gx"), parity("gy")

    wide = rows + 8

    def gather(out, own, edge):
        cells = slice(edge, edge + 2)
        for c in range(3):
            start = c * wide + (2 if c == 2 else 4)
            out[start : start + rows] = own[c]
        for rim, side in ((xa, 1 - odd_x), (xb, odd_x)):
            for c in range(2):
                out[pl.ds(c * wide + (rows + 4) * side, 4)] = rim[4 * c : 4 * c + 4, cells, :]
            out[pl.ds(2 * wide + (rows + 2) * side, 2)] = rim[pl.ds(10 - 2 * side, 2), cells, :]

    last = SIDE - 2

    @pl.when(odd_y == 0)
    def _():
        gather(ya, high, last)
        gather(yb, low, 0)

    @pl.when(odd_y == 1)
    def _():
        gather(ya, low, 0)
        gather(yb, high, last)


def north_edges(low, high, xa, xb):
    _, rows, two, depth = low.shape
    out = pltpu.VMEM((3 * (rows + 8) - 4, two, depth), F32)
    return pl.pallas_call(
        north_kernel,
        out_shape=(out, out),
        in_specs=[VMEM_SPEC] * 4,
        out_specs=(VMEM_SPEC, VMEM_SPEC),
        compiler_params=pltpu.CompilerParams(vmem_limit_bytes=VMEM_BYTES),
        name="north_edges",
    )(low, high, xa, xb)


def build_requests(source, req, pos):
    shape = (LANES, LANES)
    src = source[...]
    tile = src // LANES
    local = (src % LANES).astype(F32)
    mine = jnp.where(iota(shape, 0) == tile, 1.0, 0.0)
    earlier = jnp.where(iota(shape, 0) < iota(shape, 1), 1.0, 0.0)
    before = jnp.dot(mine, earlier, preferred_element_type=F32)
    rank = jnp.sum(before * mine, axis=0, keepdims=True)
    wanted = mine * local
    lane = iota(shape, 1)
    first = jnp.sum(jnp.where(rank == 0.0, wanted, 0.0), axis=1, keepdims=True)
    second = jnp.sum(jnp.where(rank == 1.0, wanted, 0.0), axis=1, keepdims=True)
    req[...] = jnp.where(lane == 0, first, jnp.where(lane == 1, second, 0.0)).astype(jnp.int32)
    pos[...] = tile * 2 + jnp.minimum(rank, 1.0).astype(jnp.int32)


def columns_of(ker):
    taps = ker.shape[0]
    same = jnp.where(iota((taps, taps), 0) == iota((taps, taps), 1), 1.0, 0.0)
    return lax.dot_general(
        ker[...], same, (((0,), (0,)), ((), ())), precision=HIGHEST, preferred_element_type=F32
    )


def history_kernel(hist, ker, out):
    k = columns_of(ker)
    steps = hist.shape[0]
    half = hist.shape[1] // 2
    for part in range(2):
        rows = pl.ds(part * half, half)
        kp = k[part * half : (part + 1) * half]
        first = jnp.zeros((half, LANES), F32)
        second = jnp.zeros((half, LANES), F32)
        for h in range(steps):
            past = hist[h, rows, :]
            first = first + kp[:, steps - h : steps - h + 1] * past
            if h > 0:
                second = second + kp[:, steps + 1 - h : steps + 2 - h] * past
        out[0, rows, :] = first
        out[1, rows, :] = second


def history_part(hist, ker):
    return pl.pallas_call(
        history_kernel,
        out_shape=pltpu.VMEM((2,) + hist.shape[1:], F32),
        in_specs=[VMEM_SPEC, VMEM_SPEC],
        out_specs=VMEM_SPEC,
        compiler_params=pltpu.CompilerParams(vmem_limit_bytes=VMEM_BYTES),
        name="history",
    )(hist, ker)


def response_kernel(ans, pos, count, base, ker, out):
    at = pos[...]
    chosen = jnp.where(iota((2 * LANES, LANES), 0) == at, 1.0, 0.0)
    forces = lax.dot_general(
        ans[...], chosen, (((0,), (0,)), ((), ())), precision=HIGHEST, preferred_element_type=F32
    )
    k = columns_of(ker)
    modes = k.shape[0]
    early, late = forces[:modes], forces[modes:]
    live = iota((1, LANES), 1) < count[...]
    out[0] = jnp.where(live, base[0] + k[:, 0:1] * early, 0.0)
    out[1] = jnp.where(live, base[1] + k[:, 0:1] * late + k[:, 1:2] * early, 0.0)


def make_responses(ans, pos, count, base, ker):
    return pl.pallas_call(
        response_kernel,
        out_shape=jax.ShapeDtypeStruct(base.shape, F32),
        in_specs=[VMEM_SPEC] * 5,
        out_specs=VMEM_SPEC,
        compiler_params=pltpu.CompilerParams(vmem_limit_bytes=VMEM_BYTES),
        name="responses",
    )(ans, pos, count.reshape(1, 1), base, ker)


def swap(array, axis, first):
    pairs = []
    for low in range(first, lax.axis_size(axis) - 1, 2):
        pairs += [(low, low + 1), (low + 1, low)]
    return in_vmem(lax.ppermute(array, axis, pairs))


def east_swaps(xa, xb):
    return swap(xa, "gx", 0), swap(xb, "gx", 1)


def north_swaps(ya, yb):
    return swap(ya, "gy", 0), swap(yb, "gy", 1)


def per_device(
    disp_prev,
    disp_now,
    buoyancy,
    shear_mod,
    lame_first,
    foot_offset,
    owner_source,
    owner_count,
    force_history,
    participation,
    kernels,
):
    return steps(
        disp_prev,
        disp_now,
        tuple(in_hbm(a) for a in (buoyancy, shear_mod, lame_first)),
        foot_offset.T,
        owner_source,
        owner_count,
        force_history,
        participation.T,
        kernels.T,
    )


def exchange(array, place=lambda rows: rows):
    rows = place(array.reshape(LANES, -1, LANES))
    out = lax.all_to_all(rows, ("gx", "gy"), split_axis=0, concat_axis=0)
    return out.reshape(array.shape)


def steps(prev, now, medium, offset, source, count, history, part, kernels):
    pa, pb, low, high, req, pos = east_pack(
        in_hbm(now), in_hbm(prev), *medium, in_hbm(source.reshape(1, LANES))
    )
    east = east_swaps(in_vmem(pa), in_vmem(pb))
    asked = exchange(req)
    north = north_edges(in_vmem(low), in_vmem(high), *east)
    north = north_swaps(*north)
    main = first_main(in_hbm(now), *east, in_hbm(prev), *medium)
    north, main = lax.optimization_barrier((north, main))
    mid, ya, yb, top = first_north(*main, *north)
    north = north_swaps(ya, yb)
    prepared = prepare(in_vmem(asked), offset, part)
    disp_mid, main, pack = second_main(mid, in_hbm(now), *medium)
    north, main, pack, prepared = lax.optimization_barrier((north, main, pack, prepared))
    near, ans = near_north(main, pack, *north, in_vmem(top), *prepared)
    back = exchange(ans)
    base = in_vmem(history_part(history, kernels))
    disp_next = far_north(in_vmem(main), in_vmem(pack), in_vmem(near), *(in_vmem(a) for a in north))
    responses = make_responses(back, in_vmem(pos), count, base, kernels)
    return disp_mid, disp_next, responses


def solution(mesh):
    return jax.shard_map(
        per_device,
        mesh=mesh,
        in_specs=(
            P(None, "gx", "gy", None),
            P(None, "gx", "gy", None),
            P("gx", "gy", None),
            P("gx", "gy", None),
            P("gx", "gy", None),
            P(("gx", "gy"), None),
            P(("gx", "gy")),
            P(("gx", "gy")),
            P(None, None, ("gx", "gy")),
            P(),
            P(),
        ),
        out_specs=(
            P(None, "gx", "gy", None),
            P(None, "gx", "gy", None),
            P(None, None, ("gx", "gy")),
        ),
        check_vma=False,
    )
```

```python
import jax
import jax.numpy as jnp
from jax import lax
from jax.experimental import pallas as pl
from jax.experimental.pallas import tpu as pltpu
from jax.sharding import PartitionSpec as P


PX = 8
SIDE = 16
LANES = 128
HIGHEST = lax.Precision.HIGHEST
F32 = jnp.float32
VMEM_BYTES = 16 << 20

VMEM_SPEC = pl.BlockSpec(memory_space=pltpu.VMEM)
HBM_SPEC = pl.BlockSpec(memory_space=pltpu.HBM)
SMEM_SPEC = pl.BlockSpec(memory_space=pltpu.SMEM)


def iota(shape, axis):
    return lax.broadcasted_iota(jnp.int32, shape, axis)


def in_vmem(array):
    return pltpu.with_memory_space_constraint(array, pltpu.VMEM)


def in_hbm(array):
    return pltpu.with_memory_space_constraint(array, pltpu.HBM)


def parity(axis):
    return lax.axis_index(axis) % 2


def first_of(a1, b1, a2, b2):
    return (a1 - b1) - (a2 - b2) * 0.125


def second_of(a1, b1, a2, b2):
    return (a1 + b1) - (a2 + b2) * 0.0625


def z_four(below, columns, above):
    lane = iota(columns[0].shape, 1)
    zero = jnp.zeros_like(columns[0])
    count = len(columns)
    out = [[] for _ in columns]
    for s in (1, -1, 2, -2):
        turned = [pltpu.roll(c, (-s) % LANES, axis=1) for c in columns]
        if s > 0:
            turned.append(zero if above is None else pltpu.roll(above, LANES - s, axis=1))
        else:
            turned.insert(0, zero if below is None else pltpu.roll(below, -s, axis=1))
        for k in range(count):
            if s > 0:
                out[k].append(jnp.where(lane < LANES - s, turned[k], turned[k + 1]))
            else:
                out[k].append(jnp.where(lane >= -s, turned[k + 1], turned[k]))
    return out


def z_first(below, columns, above):
    return [first_of(*four) for four in z_four(below, columns, above)]


def north_four(lower, upper):
    sub = iota(lower.shape, 0)
    zero = jnp.zeros_like(lower)
    out = ([], [])
    for s in (1, -1, 2, -2):
        first, second = [pltpu.roll(tile, (-s) % 8, axis=0) for tile in (lower, upper)]
        if s > 0:
            out[0].append(jnp.where(sub < 8 - s, first, second))
            out[1].append(jnp.where(sub < 8 - s, second, zero))
        else:
            out[0].append(jnp.where(sub >= -s, first, zero))
            out[1].append(jnp.where(sub >= -s, second, first))
    return out


def run_step(vp, prev, buoy, mu, lam, out, pack, work, ready, arrived=None, late=0):
    byx, syz, dyy, dyz, qyx, qyy, qyz, qzz = work
    rows = vp.shape[1] - 4
    span = range(vp.shape[3] // LANES)
    lanes = lambda k: pl.ds(k * LANES, LANES)
    tile = lambda h: pl.ds(8 * h, 8)

    def inner(r, full):
        i = r - 2
        for h in range(2):
            four = z_four(None, [vp[2, r, tile(h), lanes(k)] for k in span], None)
            for k in span:
                syz[r, tile(h), lanes(k)] = first_of(*four[k])
                if full:
                    qzz[i, tile(h), lanes(k)] = second_of(*four[k])
        for k in span:
            for c in range(3 if full else 2):
                four = north_four(*[vp[c, r, tile(h), lanes(k)] for h in range(2)])
                for h in range(2):
                    slope = first_of(*four[h])
                    if c == 0:
                        byx[r, tile(h), lanes(k)] = slope
                    elif c == 1:
                        syz[r, tile(h), lanes(k)] = syz[r, tile(h), lanes(k)] + slope
                    if full:
                        if c > 0:
                            (dyy, dyz)[c - 1][i, tile(h), lanes(k)] = slope
                        (qyx, qyy, qyz)[c][i, tile(h), lanes(k)] = second_of(*four[h])

    def each(start, stop, full):
        def trip(pair, carry):
            inner(start + 2 * pair, full)
            inner(start + 2 * pair + 1, full)
            return carry

        lax.fori_loop(0, (stop - start) // 2, trip, 0)

    each(0, 2, False)
    each(rows + 2, rows + 4, False)
    if arrived is not None:
        each(2, late, True)
        each(rows + 4 - late, rows + 2, True)
        arrived()
    start = max(2, late)
    each(start, rows + 4 - start, True)
    ready()

    def outer(i):
        r = i + 2
        low = iota((8, LANES), 0) < 4
        lower = {}
        for h in range(2):
            here = tile(h)

            def x_four(c, k):
                return [vp[c, r + d, here, lanes(k)] for d in (1, -1, 2, -2)]

            def derived(ref, k):
                return first_of(*[ref[r + d, here, lanes(k)] for d in (1, -1, 2, -2)])

            yz = z_first(None, [dyz[i, here, lanes(k)] for k in span], None)
            xy = z_first(None, [first_of(*x_four(0, k)) + dyy[i, here, lanes(k)] for k in span], None)
            along_z = [z_four(None, [vp[c, r, here, lanes(k)] for k in span], None) for c in range(2)]
            for k in span:
                shear = mu[i, here, lanes(k)]
                both = lam[i, here, lanes(k)] + shear
                scale = buoy[i, here, lanes(k)] * 0.12
                for which, factor in enumerate((shear, both, scale)):
                    if h == 0:
                        lower[which, k] = factor
                    else:
                        pack[which, i, :, lanes(k)] = jnp.where(low, lower[which, k], factor)
                mixed = [derived(syz, k), derived(byx, k) + yz[k], xy[k]]
                for c in range(3):
                    centre = vp[c, r, here, lanes(k)]
                    q = [
                        second_of(*x_four(c, k)),
                        (qyx, qyy, qyz)[c][i, here, lanes(k)],
                        second_of(*along_z[c][k]) if c < 2 else qzz[i, here, lanes(k)],
                    ]
                    laplace = (q[0] + q[1]) + (q[2] - centre * 5.625)
                    along = (q[c] - centre * 1.875) + mixed[c] * (1.0 / 3.0)
                    update = shear * laplace + both * along
                    out[c, i, here, lanes(k)] = (2.0 * centre - prev[c, i, here, lanes(k)]) + scale * update

    def outer_two(pair, carry):
        outer(2 * pair)
        outer(2 * pair + 1)
        return carry

    lax.fori_loop(0, rows // 2, outer_two, 0)


def step_work(rows, cols, depth):
    return [pltpu.VMEM((rows + 4, cols, depth), F32)] * 2 + [pltpu.VMEM((rows, cols, depth), F32)] * 6


def halves(x):
    high = x.astype(jnp.bfloat16)
    return high, (x - high.astype(F32)).astype(jnp.bfloat16)


def product(a, b, dims=((1,), (0,))):
    dot = lambda p, q: lax.dot_general(p, q, (dims, ((), ())), preferred_element_type=F32)
    if a.dtype == jnp.bfloat16:
        high, low = halves(b)
        return dot(a, high) + dot(a, low)
    ah, al = halves(a)
    if b.dtype == jnp.bfloat16:
        return dot(ah, b) + dot(al, b)
    bh, bl = halves(b)
    return dot(ah, bh) + (dot(ah, bl) + dot(al, bh))


def one_hot(mask):
    return jnp.where(mask, 1.0, 0.0).astype(jnp.bfloat16)


def surface_rows(field, first):
    cells = SIDE * SIDE
    flat = jnp.zeros((8, cells), F32)
    for c in range(3):
        pick = one_hot((iota((8, LANES), 0) == first + c) & (iota((8, LANES), 1) == 0))
        flat = flat + product(pick, field[c, :, :, 0:LANES].reshape(cells, LANES), ((1,), (1,)))
    return flat


def started(pairs, sems):
    copies = [pltpu.make_async_copy(src, dst, sems.at[n]) for n, (src, dst) in enumerate(pairs)]
    for copy in copies:
        copy.start()
    return copies


def wait_all(copies):
    for copy in copies:
        copy.wait()


def east_pack_kernel(now, prev, buoy, mu, lam, source, pa, pb, low, high, req, pos, held, sems):
    rows = now.shape[1]
    odd = parity("gx")
    pairs = []
    for out, side in ((pa, 1 - odd), (pb, odd)):
        four = pl.ds((rows - 4) * side, 4)
        two = pl.ds((rows - 2) * side, 2)
        for c in range(3):
            pairs.append((now.at[c, four], out.at[pl.ds(4 * c, 4)]))
            pairs.append((prev.at[c, two], out.at[pl.ds(12 + 2 * c, 2)]))
        for n, field in enumerate((buoy, mu, lam)):
            pairs.append((field.at[two], out.at[pl.ds(18 + 2 * n, 2)]))
    cols = now.shape[2]
    pairs.append((now.at[:, :, pl.ds(0, 2)], low))
    pairs.append((now.at[:, :, pl.ds(cols - 2, 2)], high))
    copies = started([(source, held)] + pairs, sems)
    copies[0].wait()
    build_requests(held, req, pos)
    wait_all(copies[1:])


def east_pack(now, prev, buoy, mu, lam, source):
    _, rows, cols, depth = now.shape
    out = pltpu.VMEM((24, cols, depth), F32)
    side = pltpu.VMEM((3, rows, 2, depth), F32)
    return pl.pallas_call(
        east_pack_kernel,
        out_shape=(
            out,
            out,
            side,
            side,
            jax.ShapeDtypeStruct((LANES, LANES), jnp.int32),
            pltpu.VMEM((1, LANES), jnp.int32),
        ),
        in_specs=[HBM_SPEC] * 6,
        out_specs=(VMEM_SPEC,) * 6,
        scratch_shapes=[pltpu.VMEM((1, LANES), jnp.int32), pltpu.SemaphoreType.DMA((21,))],
        compiler_params=pltpu.CompilerParams(vmem_limit_bytes=VMEM_BYTES),
        name="east_pack",
    )(now, prev, buoy, mu, lam, source)


def first_main_kernel(prev, buoy, mu, lam, now, xa, xb, out, pack, vp, pv, bv, mv, lv, *work):
    rows = now.shape[1]
    own = pl.ds(2, rows)
    copies = started(
        [(now, vp.at[:, pl.ds(4, rows)]), (prev, pv.at[:, own])] + [(src, dst.at[own]) for src, dst in ((buoy, bv), (mu, mv), (lam, lv))],
        work[-1],
    )
    odd = parity("gx")
    for edge, side in ((xa, 1 - odd), (xb, odd)):
        four = pl.ds((rows + 4) * side, 4)
        two = pl.ds((rows + 2) * side, 2)
        for c in range(3):
            vp[c, four] = edge[4 * c : 4 * c + 4]
            pv[c, two] = edge[12 + 2 * c : 14 + 2 * c]
        for n, field in enumerate((bv, mv, lv)):
            field[two] = edge[18 + 2 * n : 20 + 2 * n]
    run_step(
        vp, pv, bv, mv, lv, out, pack, work[:-1], lambda: wait_all(copies[1:]), arrived=copies[0].wait, late=4
    )


def first_main(now, xa, xb, prev, buoy, mu, lam):
    _, rows, cols, depth = now.shape
    wide = rows + 4
    one = pltpu.VMEM((wide, cols, depth), F32)
    return pl.pallas_call(
        first_main_kernel,
        out_shape=(pltpu.VMEM((3, wide, cols, depth), F32), pltpu.VMEM((3, wide, 8, depth), F32)),
        in_specs=[HBM_SPEC] * 5 + [VMEM_SPEC] * 2,
        out_specs=(VMEM_SPEC,) * 2,
        scratch_shapes=[
            pltpu.VMEM((3, wide + 4, cols, depth), F32),
            pltpu.VMEM((3, wide, cols, depth), F32),
            one,
            one,
            one,
            *step_work(wide, cols, depth),
            pltpu.SemaphoreType.DMA((5,)),
        ],
        compiler_params=pltpu.CompilerParams(vmem_limit_bytes=VMEM_BYTES),
        name="first_main",
    )(prev, buoy, mu, lam, now, xa, xb)


def first_north_kernel(main, pack, ya, yb, mid, ma, mb, top, rim, ex, ey):
    rows = main.shape[1] - 4
    fill_north(rim, ya, yb)
    add_north(rim, pack, main, mid, ex, ey, 0, main.shape[3] // LANES)
    odd = parity("gy")

    wide = rows + 4

    def gather(edge, first):
        cells = slice(first, first + 2)
        edge[0:wide] = mid[0, :, cells, :]
        edge[wide : 2 * wide] = mid[1, :, cells, :]
        edge[2 * wide :] = mid[2, 2 : wide - 2, cells, :]

    @pl.when(odd == 0)
    def _():
        gather(ma, 14)
        gather(mb, 0)

    @pl.when(odd == 1)
    def _():
        gather(ma, 0)
        gather(mb, 14)

    top[...] = surface_rows(mid.at[:, pl.ds(2, rows)], 0)


def first_north(main, pack, ya, yb):
    _, wide, _, depth = main.shape
    edge = pltpu.VMEM((3 * wide - 4, 2, depth), F32)
    return pl.pallas_call(
        first_north_kernel,
        out_shape=(pltpu.VMEM(main.shape, F32), edge, edge, pltpu.VMEM((8, SIDE * SIDE), F32)),
        in_specs=[VMEM_SPEC] * 4,
        out_specs=(VMEM_SPEC,) * 4,
        scratch_shapes=[
            pltpu.VMEM((3, wide + 4, 8, depth), F32),
            pltpu.VMEM((wide + 4, 8, depth), F32),
            pltpu.VMEM((wide + 4, 8, depth), F32),
        ],
        compiler_params=pltpu.CompilerParams(vmem_limit_bytes=VMEM_BYTES),
        name="first_north",
    )(main, pack, ya, yb)


def second_main_kernel(prev, buoy, mu, lam, vp, mid, out, pack, pv, bv, mv, lv, *work):
    sems = work[-1]
    rows = prev.shape[1]
    copies = started([(prev, pv), (buoy, bv), (mu, mv), (lam, lv)], sems)
    stores = started([(vp.at[:, pl.ds(2, rows)], mid)], sems.at[pl.ds(4, 1)])
    run_step(vp, pv, bv, mv, lv, out, pack, work[:-1], lambda: wait_all(copies))
    wait_all(stores)


def second_main(v, prev, buoy, mu, lam):
    _, rows, cols, depth = prev.shape
    whole = pltpu.VMEM(prev.shape, F32)
    one = pltpu.VMEM((rows, cols, depth), F32)
    return pl.pallas_call(
        second_main_kernel,
        out_shape=(pltpu.HBM(prev.shape, F32), whole, pltpu.VMEM((3, rows, 8, depth), F32)),
        in_specs=[HBM_SPEC] * 4 + [VMEM_SPEC],
        out_specs=(HBM_SPEC,) + (VMEM_SPEC,) * 2,
        scratch_shapes=[
            whole,
            one,
            one,
            one,
            *step_work(rows, cols, depth),
            pltpu.SemaphoreType.DMA((5,)),
        ],
        compiler_params=pltpu.CompilerParams(vmem_limit_bytes=VMEM_BYTES),
        name="second_main",
    )(prev, buoy, mu, lam, v)


def fill_north(rim, ya, yb):
    odd_y = parity("gy")
    rows, wide = rim.shape[1], rim.shape[3]
    rim[:, :, 2:6, :] = jnp.zeros((rim.shape[0], rows, 4, wide), F32)

    def place(edge, first):
        cells = slice(first, first + 2)
        rim[0, :, cells, :] = edge[0:rows, :, :wide]
        rim[1, :, cells, :] = edge[rows : 2 * rows, :, :wide]
        rim[2, 2 : rows - 2, cells, :] = edge[2 * rows :, :, :wide]

    @pl.when(odd_y == 0)
    def _():
        place(yb, 0)
        place(ya, 6)

    @pl.when(odd_y == 1)
    def _():
        place(ya, 0)
        place(yb, 6)


def add_north(rim, pack, main, out, ex, ey, first, last, base=0, done=None, parts=1):
    rows = rim.shape[1] - 4
    total = 3
    span = range(first, last)
    lanes = lambda k: pl.ds(k * LANES, LANES)
    local = lambda k: pl.ds((k - base) * LANES, LANES)
    below, above = max(first - 1, 0), min(last + 1, total)

    sub = iota((8, LANES), 0)
    low = sub < 4

    def rim_parts(c, r, k):
        two = rim[c, r, :, lanes(k)]
        one = jnp.where(sub == 7, pltpu.roll(two, 1, axis=0), 0.0)
        return jnp.where(sub == 0, pltpu.roll(two, 7, axis=0), one), two

    def slope(c, r, k):
        one, two = rim_parts(c, r, k)
        change = one - two * 0.125
        return jnp.where(low, -change, change)

    def bend(c, r, k):
        one, two = rim_parts(c, r, k)
        return one - two * 0.0625

    def ends(get):
        return (
            get(first - 1) if first > 0 else None,
            [get(k) for k in span],
            get(last) if last < total else None,
        )

    def inner(r):
        for k in range(below, above):
            ey[r, :, lanes(k)] = slope(1, r, k)
        for k in span:
            ex[r, :, lanes(k)] = slope(0, r, k)

    def inner_two(pair, carry):
        inner(2 * pair)
        inner(2 * pair + 1)
        return carry

    lax.fori_loop(0, (rows + 4) // 2, inner_two, 0)

    def outer(i):
        r = i + 2
        yz = z_first(*ends(lambda k: slope(2, r, k)))
        xy = z_first(*ends(lambda k: ey[r, :, lanes(k)]))
        for n, k in enumerate(span):

            def derived(ref):
                return first_of(*[ref[r + d, :, lanes(k)] for d in (1, -1, 2, -2)])

            shear, both, scale = [pack[which, i, :, local(k)] for which in range(3)]
            mixed = [derived(ey), derived(ex) + yz[n], xy[n]]
            for c in range(3):
                q = bend(c, r, k)
                along = mixed[c] * (1.0 / 3.0)
                if c == 1:
                    along = along + q
                update = scale * (shear * q + both * along)
                out[c, i, 0:8, local(k)] = main[c, i, 0:8, local(k)] + jnp.where(low, update, 0.0)
                out[c, i, 8:16, local(k)] = main[c, i, 8:16, local(k)] + jnp.where(low, 0.0, update)

    def outer_two(pair, carry):
        outer(2 * pair)
        outer(2 * pair + 1)
        return carry

    count = rows // 2 // parts
    for part in range(parts):
        lax.fori_loop(part * count, (part + 1) * count, outer_two, 0)
        if done is not None:
            done(2 * part * count, 2 * count)


def window_tables(flat, windows):
    span = SIDE - PX + 1
    halves = [flat[:, :LANES], flat[:, LANES:]]
    lane = iota((8, LANES), 1)
    windows[span * span * 8 :, :] = jnp.zeros((windows.shape[0] - span * span * 8, LANES), F32)
    for ox in range(span):
        for oy in range(span):
            half, shift = divmod(ox * SIDE + oy, LANES)
            moved = halves[half]
            if shift:
                other = pltpu.roll(halves[1], LANES - shift, axis=1) if half == 0 else jnp.zeros_like(moved)
                moved = jnp.where(lane < LANES - shift, pltpu.roll(moved, LANES - shift, axis=1), other)
            windows[pl.ds((ox * span + oy) * 8, 8), :] = moved


def corner_forces(flat, weights, windows):
    window_tables(flat, windows)
    both = []
    for n in range(2):
        total = jnp.zeros((LANES, weights.shape[2]), F32)
        for c in range(3):
            total = total + product(windows[pl.ds(3 * n + c, LANES, stride=8), :], weights[c])
        both.append(total)
    return jnp.concatenate(both, axis=1)


def spread(part, c):
    shape = (LANES, part.shape[1])
    cell = iota(shape, 0)
    row = c * PX * PX + (cell // SIDE) * PX + cell % SIDE
    place = jnp.where((iota(shape, 1) == row) & (cell % SIDE < PX), 1.0, 0.0)
    return lax.dot_general(
        place, part[...], (((1,), (1,)), ((), ())), precision=HIGHEST, preferred_element_type=F32
    )


def prepare_kernel(asked, offset, part, chosen, weights):
    span = SIDE - PX + 1
    shape = (LANES, LANES)
    where = offset[0:1, :] * span + offset[1:2, :]
    corner = jnp.where(iota(shape, 0) == where, 1.0, 0.0)
    lane = iota(shape, 1)
    for r in range(2):
        slot = jnp.where(lane == asked[:, r : r + 1], 1.0, 0.0)
        chosen[pl.ds(r, LANES, stride=2), :] = lax.dot_general(
            slot, corner, (((1,), (1,)), ((), ())), preferred_element_type=F32
        )
    for c in range(3):
        weights[c] = spread(part, c)


def prepare(asked, offset, part):
    modes = part.shape[0]
    return pl.pallas_call(
        prepare_kernel,
        out_shape=(pltpu.VMEM((2 * LANES, LANES), F32), pltpu.VMEM((3, LANES, modes), F32)),
        in_specs=[VMEM_SPEC] * 3,
        out_specs=(VMEM_SPEC,) * 2,
        compiler_params=pltpu.CompilerParams(vmem_limit_bytes=VMEM_BYTES),
        name="prepare",
    )(asked, offset, part)


def near_north_kernel(main, pack, ya, yb, top, chosen, weights, near, ans, rim, ex, ey, windows):
    fill_north(rim, ya, yb)
    add_north(rim, pack, main, near, ex, ey, 0, 1)
    forces = corner_forces(top[...] + surface_rows(near, 3), weights, windows)
    ans[...] = product(chosen[...].astype(jnp.bfloat16), forces)


def near_north(main, pack, ya, yb, top, chosen, weights):
    _, rows, cols, _ = main.shape
    return pl.pallas_call(
        near_north_kernel,
        out_shape=(pltpu.VMEM((3, rows, cols, LANES), F32), pltpu.VMEM((2 * LANES, LANES), F32)),
        in_specs=[VMEM_SPEC] * 7,
        out_specs=(VMEM_SPEC,) * 2,
        scratch_shapes=[
            pltpu.VMEM((3, rows + 4, 8, 2 * LANES), F32),
            pltpu.VMEM((rows + 4, 8, 2 * LANES), F32),
            pltpu.VMEM((rows + 4, 8, 2 * LANES), F32),
            pltpu.VMEM((8 * LANES, LANES), F32),
        ],
        compiler_params=pltpu.CompilerParams(vmem_limit_bytes=VMEM_BYTES),
        name="near_north",
    )(main, pack, ya, yb, top, chosen, weights)


def far_north_kernel(main, pack, near, ya, yb, nxt, rim, out, ex, ey, sems):
    stores = started([(near, nxt.at[:, :, :, pl.ds(0, LANES)])], sems.at[pl.ds(0, 1)])
    columns = pl.ds(LANES, out.shape[3] - LANES)

    def done(row, count):
        part = (slice(None), pl.ds(row, count), slice(None), columns)
        stores.extend(started([(out.at[part], nxt.at[part])], sems.at[pl.ds(len(stores), 1)]))

    fill_north(rim, ya, yb)
    add_north(rim, pack, main, out, ex, ey, 1, out.shape[3] // LANES, done=done, parts=4)
    wait_all(stores)


def far_north(main, pack, near, ya, yb):
    _, rows, _, depth = main.shape
    return pl.pallas_call(
        far_north_kernel,
        out_shape=pltpu.HBM(main.shape, F32),
        in_specs=[VMEM_SPEC] * 5,
        out_specs=HBM_SPEC,
        scratch_shapes=[
            pltpu.VMEM((3, rows + 4, 8, depth), F32),
            pltpu.VMEM(main.shape, F32),
            pltpu.VMEM((rows + 4, 8, depth), F32),
            pltpu.VMEM((rows + 4, 8, depth), F32),
            pltpu.SemaphoreType.DMA((5,)),
        ],
        compiler_params=pltpu.CompilerParams(vmem_limit_bytes=VMEM_BYTES),
        name="far_north",
    )(main, pack, near, ya, yb)


def north_kernel(low, high, xa, xb, ya, yb):
    rows = low.shape[1]
    odd_x, odd_y = parity("gx"), parity("gy")

    wide = rows + 8

    def gather(out, own, edge):
        cells = slice(edge, edge + 2)
        for c in range(3):
            start = c * wide + (2 if c == 2 else 4)
            out[start : start + rows] = own[c]
        for rim, side in ((xa, 1 - odd_x), (xb, odd_x)):
            for c in range(2):
                out[pl.ds(c * wide + (rows + 4) * side, 4)] = rim[4 * c : 4 * c + 4, cells, :]
            out[pl.ds(2 * wide + (rows + 2) * side, 2)] = rim[pl.ds(10 - 2 * side, 2), cells, :]

    last = SIDE - 2

    @pl.when(odd_y == 0)
    def _():
        gather(ya, high, last)
        gather(yb, low, 0)

    @pl.when(odd_y == 1)
    def _():
        gather(ya, low, 0)
        gather(yb, high, last)


def north_edges(low, high, xa, xb):
    _, rows, two, depth = low.shape
    out = pltpu.VMEM((3 * (rows + 8) - 4, two, depth), F32)
    return pl.pallas_call(
        north_kernel,
        out_shape=(out, out),
        in_specs=[VMEM_SPEC] * 4,
        out_specs=(VMEM_SPEC, VMEM_SPEC),
        compiler_params=pltpu.CompilerParams(vmem_limit_bytes=VMEM_BYTES),
        name="north_edges",
    )(low, high, xa, xb)


def build_requests(source, req, pos):
    shape = (LANES, LANES)
    src = source[...]
    tile = src // LANES
    local = (src % LANES).astype(F32)
    mine = jnp.where(iota(shape, 0) == tile, 1.0, 0.0)
    earlier = jnp.where(iota(shape, 0) < iota(shape, 1), 1.0, 0.0)
    before = jnp.dot(mine, earlier, preferred_element_type=F32)
    rank = jnp.sum(before * mine, axis=0, keepdims=True)
    wanted = mine * local
    lane = iota(shape, 1)
    first = jnp.sum(jnp.where(rank == 0.0, wanted, 0.0), axis=1, keepdims=True)
    second = jnp.sum(jnp.where(rank == 1.0, wanted, 0.0), axis=1, keepdims=True)
    req[...] = jnp.where(lane == 0, first, jnp.where(lane == 1, second, 0.0)).astype(jnp.int32)
    pos[...] = tile * 2 + jnp.minimum(rank, 1.0).astype(jnp.int32)


def columns_of(ker):
    taps = ker.shape[0]
    same = jnp.where(iota((taps, taps), 0) == iota((taps, taps), 1), 1.0, 0.0)
    return lax.dot_general(
        ker[...], same, (((0,), (0,)), ((), ())), precision=HIGHEST, preferred_element_type=F32
    )


def history_kernel(hist, ker, out):
    k = columns_of(ker)
    steps = hist.shape[0]
    half = hist.shape[1] // 2
    for part in range(2):
        rows = pl.ds(part * half, half)
        kp = k[part * half : (part + 1) * half]
        first = jnp.zeros((half, LANES), F32)
        second = jnp.zeros((half, LANES), F32)
        for h in range(steps):
            past = hist[h, rows, :]
            first = first + kp[:, steps - h : steps - h + 1] * past
            if h > 0:
                second = second + kp[:, steps + 1 - h : steps + 2 - h] * past
        out[0, rows, :] = first
        out[1, rows, :] = second


def history_part(hist, ker):
    return pl.pallas_call(
        history_kernel,
        out_shape=pltpu.VMEM((2,) + hist.shape[1:], F32),
        in_specs=[VMEM_SPEC, VMEM_SPEC],
        out_specs=VMEM_SPEC,
        compiler_params=pltpu.CompilerParams(vmem_limit_bytes=VMEM_BYTES),
        name="history",
    )(hist, ker)


def response_kernel(ans, pos, count, base, ker, out):
    at = pos[...]
    forces = product(ans[...], one_hot(iota((2 * LANES, LANES), 0) == at), ((0,), (0,)))
    k = columns_of(ker)
    modes = k.shape[0]
    early, late = forces[:modes], forces[modes:]
    live = iota((1, LANES), 1) < count[...]
    out[0] = jnp.where(live, base[0] + k[:, 0:1] * early, 0.0)
    out[1] = jnp.where(live, base[1] + k[:, 0:1] * late + k[:, 1:2] * early, 0.0)


def make_responses(ans, pos, count, base, ker):
    return pl.pallas_call(
        response_kernel,
        out_shape=jax.ShapeDtypeStruct(base.shape, F32),
        in_specs=[VMEM_SPEC] * 5,
        out_specs=VMEM_SPEC,
        compiler_params=pltpu.CompilerParams(vmem_limit_bytes=VMEM_BYTES),
        name="responses",
    )(ans, pos, count.reshape(1, 1), base, ker)


def swap(array, axis, first):
    pairs = []
    for low in range(first, lax.axis_size(axis) - 1, 2):
        pairs += [(low, low + 1), (low + 1, low)]
    return in_vmem(lax.ppermute(array, axis, pairs))


def east_swaps(xa, xb):
    return swap(xa, "gx", 0), swap(xb, "gx", 1)


def north_swaps(ya, yb):
    yb = swap(yb, "gy", 1)
    ya = swap(ya, "gy", 0)
    return ya, yb


def per_device(
    disp_prev,
    disp_now,
    buoyancy,
    shear_mod,
    lame_first,
    foot_offset,
    owner_source,
    owner_count,
    force_history,
    participation,
    kernels,
):
    return steps(
        disp_prev,
        disp_now,
        tuple(in_hbm(a) for a in (buoyancy, shear_mod, lame_first)),
        foot_offset.T,
        owner_source,
        owner_count,
        force_history,
        participation.T,
        kernels.T,
    )


def exchange(array, place=lambda rows: rows):
    rows = place(array.reshape(LANES, -1, LANES))
    out = lax.all_to_all(rows, ("gx", "gy"), split_axis=0, concat_axis=0)
    return out.reshape(array.shape)


def steps(prev, now, medium, offset, source, count, history, part, kernels):
    pa, pb, low, high, req, pos = east_pack(
        in_hbm(now), in_hbm(prev), *medium, in_hbm(source.reshape(1, LANES))
    )
    east = east_swaps(in_vmem(pa), in_vmem(pb))
    asked = exchange(req)
    north = north_edges(in_vmem(low), in_vmem(high), *east)
    north = north_swaps(*north)
    main = first_main(in_hbm(now), *east, in_hbm(prev), *medium)
    north, main = lax.optimization_barrier((north, main))
    mid, ya, yb, top = first_north(*main, *north)
    north = north_swaps(ya, yb)
    prepared = prepare(in_vmem(asked), offset, part)
    disp_mid, main, pack = second_main(mid, in_hbm(now), *medium)
    north, main, pack, prepared = lax.optimization_barrier((north, main, pack, prepared))
    near, ans = near_north(main, pack, *north, in_vmem(top), *prepared)
    back = exchange(ans)
    base = in_vmem(history_part(history, kernels))
    disp_next = far_north(in_vmem(main), in_vmem(pack), in_vmem(near), *(in_vmem(a) for a in north))
    responses = make_responses(back, in_vmem(pos), count, base, kernels)
    return disp_mid, disp_next, responses


def solution(mesh):
    return jax.shard_map(
        per_device,
        mesh=mesh,
        in_specs=(
            P(None, "gx", "gy", None),
            P(None, "gx", "gy", None),
            P("gx", "gy", None),
            P("gx", "gy", None),
            P("gx", "gy", None),
            P(("gx", "gy"), None),
            P(("gx", "gy")),
            P(("gx", "gy")),
            P(None, None, ("gx", "gy")),
            P(),
            P(),
        ),
        out_specs=(
            P(None, "gx", "gy", None),
            P(None, "gx", "gy", None),
            P(None, None, ("gx", "gy")),
        ),
        check_vma=False,
    )
```
